32 devices in a mesh: dp: 8 (over z, core), tensor: 4 (over y, x).
Axes of the slice: x: 2, y: 2, z: 4, core: 2. Of those that a mesh axis runs over, the one named last changes fastest.
Arguments:
- hidden_in: bfloat16 [2048, 2048], P('dp'), may hold values from -6 to 6
- seq_lengths: int32 [8, 16], P('dp'), may hold values from 0 to 256, as said below
- norm_gain: float32 [2048], replicated, may hold values from 0.25 to 1.75
- norm_bias: float32 [2048], replicated, may hold values from -3 to 3
- qkv_master: float32 [3, 2048, 2048], P(None, 'dp', 'tensor'), may hold values from -0.125 to 0.125
- qkv_bias: float32 [3, 2048], P(None, 'tensor'), may hold values from -3 to 3
- out_master: float32 [2048, 2048], P('tensor', 'dp'), may hold values from -1 to 1
- out_bias: float32 [2048], replicated, may hold values from -3 to 3
- up_master: float32 [2048, 8192], P('dp', 'tensor'), may hold values from -0.125 to 0.125
- up_bias: float32 [8192], P('tensor'), may hold values from -3 to 3
- down_master: float32 [8192, 2048], P('tensor', 'dp'), may hold values from -0.0625 to 0.0625
- down_bias: float32 [2048], replicated, may hold values from -3 to 3
- out_grad: bfloat16 [2048, 2048], P('dp'), may hold values from -6 to 6
Outputs:
- hidden_out: bfloat16 [2048, 2048], P('dp')
- input_grad: bfloat16 [2048, 2048], P('dp')
- norm_gain_grad: float32 [2048], replicated
- norm_bias_grad: float32 [2048], replicated
- qkv_master_grad: float32 [3, 2048, 2048], P(None, 'dp', 'tensor')
- qkv_bias_grad: float32 [3, 2048], P(None, 'tensor')
- out_master_grad: float32 [2048, 2048], P('tensor', 'dp')
- out_bias_grad: float32 [2048], replicated
- up_master_grad: float32 [2048, 8192], P('dp', 'tensor')
- up_bias_grad: float32 [8192], P('tensor')
- down_master_grad: float32 [8192, 2048], P('tensor', 'dp')
- down_bias_grad: float32 [2048], replicated
The draws below stay inside these ranges and needn't reach their ends.
Inputs may be any that keep to these rules, and one draw needn't show every extreme that they name: `seq_lengths`: row i lists, in order, the lengths of the sequences packed from the first token slot of index i of dp; a zero length means no sequence and all later ones in the row are zero; nonzero lengths are 64 or more; a row's first length is nonzero and its lengths sum to at most 256; in some row the first length is 256.
All inputs are finite; a program needn't handle non-finite values.
Results may differ from the reference program's by a relative error of at most 0.014.
Values may be sent and summed in bfloat16 or wider, within the bound.
No kernel may reach another device: no remote copies, remote signals or barrier semaphores. Data moves between devices by JAX's collectives and lax.ppermute only.
A program may use at most 128 MiB of HBM per device.

```python
import math
import jax
import jax.numpy as jnp
from jax import lax

D = 2048
HEADS = 32
HEAD_DIM = 64
ROT_DIM = 32
FF = 8192
ROWS_DEV = 256
SLOTS = 16
MIN_LEN = 64
MAX_LEN = 256
TOKENS = 2048
N_DP = 8
N_TENSOR = 4


def draw_seq_lengths(key, part):
    length_key, device_key = jax.random.split(jax.random.fold_in(key, 17))
    uniform_ints = jax.random.randint(length_key, (N_DP, SLOTS), 0, 1001)
    cubed = uniform_ints * uniform_ints // 1000 * uniform_ints // 1000
    lengths = MIN_LEN + (MAX_LEN - MIN_LEN) * cubed // 1000
    chosen = jax.random.randint(device_key, (), 0, N_DP)
    forced = (lax.iota(jnp.int32, N_DP)[:, None] == chosen) & (lax.iota(jnp.int32, SLOTS)[None, :] == 0)
    lengths = jnp.where(forced, MAX_LEN, lengths)
    seq_ends = jnp.cumsum(lengths, axis=1)
    return jnp.where(seq_ends <= ROWS_DEV, lengths, 0).astype(jnp.int32)


def shard_levels(key, extent, cuts, low, high):
    def one(dim, blocks):
        steps = jax.random.uniform(jax.random.fold_in(jax.random.fold_in(key, 6), dim), (blocks,), jnp.float32, low / len(cuts), high / len(cuts))
        return jnp.repeat(jnp.exp(steps), extent[dim] // blocks).reshape((-1,) + (1,) * (len(extent) - dim - 1))

    factor_of = one(*cuts[0])
    for cut in cuts[1:]:
        factor_of = factor_of * one(*cut)
    return factor_of


def scatter_about(own_key, extent, deviation, most, shards=(), dtype=jnp.bfloat16):
    level = shard_levels(own_key, extent, shards, -0.22, 0.18) if shards else 1.0
    array = jax.random.normal(own_key, extent, jnp.float32) * deviation * level
    return jnp.minimum(jnp.maximum(array, -most), most).astype(dtype)


def setup_inputs(seed: int = 0) -> dict:
    seeds = jax.random.split(jax.random.key(seed), 14)
    return {
        "hidden_in": scatter_about(seeds[0], (TOKENS, D), 1.0, 6.0, ((0, 8),)),
        "seq_lengths": draw_seq_lengths(jax.random.fold_in(seeds[13], 71), 0),
        "norm_gain": jnp.clip(1.0 + 0.15 * jax.random.normal(seeds[2], (D,), jnp.float32), 0.25, 1.75),
        "norm_bias": scatter_about(seeds[3], (D,), 0.5, 3.0, (), jnp.float32),
        "qkv_master": scatter_about(seeds[4], (3, D, D), D ** -0.5, 0.125, ((1, 8), (2, 4)), jnp.float32),
        "qkv_bias": scatter_about(seeds[5], (3, D), 0.5, 3.0, ((1, 4),), jnp.float32),
        "out_master": scatter_about(seeds[6], (D, D), (D // 64) ** -0.5, 1.0, ((0, 4), (1, 8)), jnp.float32),
        "out_bias": scatter_about(seeds[7], (D,), 0.5, 3.0, (), jnp.float32),
        "up_master": scatter_about(seeds[8], (D, FF), D ** -0.5, 0.125, ((0, 8), (1, 4)), jnp.float32),
        "up_bias": scatter_about(seeds[9], (FF,), 0.5, 3.0, ((0, 4),), jnp.float32),
        "down_master": scatter_about(seeds[10], (FF, D), FF ** -0.5, 0.0625, ((0, 4), (1, 8)), jnp.float32),
        "down_bias": scatter_about(seeds[11], (D,), 0.5, 3.0, (), jnp.float32),
        "out_grad": scatter_about(seeds[12], (TOKENS, D), 1.0, 6.0, ((0, 8),)),
    }


@jax.custom_vjp
def low(v):
    return lax.optimization_barrier(v.astype(jnp.bfloat16)).astype(jnp.float32)

@jax.custom_vjp
def low_back(v):
    return v

def low_keep(v):
    return (low(v), None)

def low_pass(kept, grad):
    return (grad,)

def back_keep(v):
    return (v, None)

def back_low(kept, grad):
    return (low(grad),)
low.defvjp(low_keep, low_pass)
low_back.defvjp(back_keep, back_low)
highest = lax.Precision.HIGHEST

def layer_norm(inputs, norm_gain, norm_bias):
    middle = lax.optimization_barrier(jnp.mean(inputs, axis=-1, keepdims=True))
    centred = inputs - middle
    spread = lax.optimization_barrier(jnp.mean(centred * centred, axis=-1, keepdims=True))
    return centred * lax.rsqrt(spread + 1e-05) * norm_gain + norm_bias

def layout(lengths, rows_count):
    seq_ends = jnp.cumsum(lengths).astype(jnp.int32)
    row_ids = lax.iota(jnp.int32, rows_count)
    passed = row_ids[:, None] >= seq_ends[None, :]
    segment = lax.optimization_barrier(jnp.sum(passed.astype(jnp.int32), axis=1)).astype(jnp.int32)
    begins = lax.optimization_barrier(jnp.max(jnp.where(passed, seq_ends[None, :], 0), axis=1)).astype(jnp.int32)
    position = row_ids - begins
    validity = (row_ids < seq_ends[-1]).astype(jnp.float32)
    return (segment, position, validity)

def rotary_tables(position):
    halves = ROT_DIM // 2
    frequency = 10000.0 ** (-(2.0 * lax.iota(jnp.float32, halves)) / ROT_DIM)
    angles = position.astype(jnp.float32)[:, None] * frequency[None, :]
    return (jnp.cos(angles), jnp.sin(angles))

def rotate(head_data, cosine_table, sine_table):
    halves = ROT_DIM // 2
    front_half = head_data[..., :halves]
    back_half = head_data[..., halves:ROT_DIM]
    cosine_part = cosine_table[:, None, :]
    sine_part = sine_table[:, None, :]
    return jnp.concatenate([front_half * cosine_part - back_half * sine_part, back_half * cosine_part + front_half * sine_part, head_data[..., ROT_DIM:]], axis=-1)

def attention(queries, key_heads, values, segment):
    rows_count = queries.shape[0]
    block_rows = min(512, rows_count)
    row_ids = lax.iota(jnp.int32, rows_count)
    score_scale = 1.0 / math.sqrt(HEAD_DIM)

    @jax.checkpoint
    def one_block(first_row):
        query_block = lax.dynamic_slice_in_dim(queries, first_row, block_rows, 0)
        seg_query = lax.dynamic_slice_in_dim(segment, first_row, block_rows, 0)
        row_query = first_row + lax.iota(jnp.int32, block_rows)
        allowed = (seg_query[:, None] == segment[None, :]) & (row_ids[None, :] <= row_query[:, None])
        scores = low_back(jnp.einsum('qhc,khc->hqk', query_block, key_heads, precision=highest) * score_scale)
        scores = jnp.where(allowed[None], scores, -1e+30)
        largest = lax.optimization_barrier(jnp.max(scores, axis=-1, keepdims=True))
        raised = jnp.exp(scores - largest)
        weights = raised / lax.optimization_barrier(jnp.sum(raised, axis=-1, keepdims=True))
        return jnp.einsum('hqk,khc->qhc', low(weights), values, precision=highest)
    starts = lax.iota(jnp.int32, rows_count // block_rows) * block_rows
    blocks_out = lax.map(one_block, starts)
    return blocks_out.reshape(rows_count, HEADS, HEAD_DIM)

def forward(inputs, norm_gain, norm_bias, qkv_master, qkv_bias, out_master, out_bias, up_master, up_bias, down_master, down_bias, segment, position, validity):
    rows_count = inputs.shape[0]
    normed = low(layer_norm(inputs, norm_gain, norm_bias))
    joined_proj = jnp.einsum('rd,jde->jre', normed, low(qkv_master), precision=highest) + qkv_bias[:, None, :]
    joined_proj = low_back(joined_proj).reshape(3, rows_count, HEADS, HEAD_DIM)
    cosine_table, sine_table = rotary_tables(position)
    queries = low(rotate(joined_proj[0], cosine_table, sine_table))
    key_heads = low(rotate(joined_proj[1], cosine_table, sine_table))
    values = low(joined_proj[2])
    context = attention(queries, key_heads, values, segment).reshape(rows_count, D)
    context = low(low_back(context))
    pre_act = low_back(jnp.dot(normed, low(up_master), precision=highest) + up_bias)
    active = low(jax.nn.gelu(pre_act, approximate=True))
    groups = N_TENSOR
    attn_part = jnp.einsum('rtk,tkd->rtd', context.reshape(rows_count, groups, D // groups), low(out_master).reshape(groups, D // groups, D), precision=highest)
    ffn_part = jnp.einsum('rtk,tkd->rtd', active.reshape(rows_count, groups, FF // groups), low(down_master).reshape(groups, FF // groups, D), precision=highest)
    partial_sum = low(attn_part + ffn_part)
    branch = lax.optimization_barrier(jnp.sum(partial_sum, axis=1)) + out_bias + down_bias
    return inputs + validity[:, None] * branch

def reference(hidden_in, seq_lengths, norm_gain, norm_bias, qkv_master, qkv_bias, out_master, out_bias, up_master, up_bias, down_master, down_bias, out_grad):
    params = (norm_gain, norm_bias, qkv_master, qkv_bias, out_master, out_bias, up_master, up_bias, down_master, down_bias)
    inputs_all = hidden_in.astype(jnp.float32).reshape(N_DP, ROWS_DEV, D)
    cotangent_all = out_grad.astype(jnp.float32).reshape(N_DP, ROWS_DEV, D)

    def one_device(running, pieces):
        inputs, cotangent, lengths = pieces
        segment, position, validity = layout(lengths, ROWS_DEV)

        def apply_layer(layer_in, *weight_list):
            return forward(layer_in, *weight_list, segment, position, validity)
        result, pullback = jax.vjp(apply_layer, inputs, *params)
        gradients = pullback(cotangent)
        running = tuple((summed + fresh for summed, fresh in zip(running, gradients[1:])))
        return (running, (result.astype(jnp.bfloat16), gradients[0].astype(jnp.bfloat16)))
    zero_grads = tuple((jnp.zeros(weight_item.shape, jnp.float32) for weight_item in params))
    totals, (outputs, input_grads) = lax.scan(one_device, zero_grads, (inputs_all, cotangent_all, seq_lengths))
    return (outputs.reshape(TOKENS, D), input_grads.reshape(TOKENS, D), totals[0], totals[1], totals[2], totals[3], totals[4], totals[5], totals[6], totals[7], totals[8], totals[9])
```

```python
import functools
import math

import jax
import jax.numpy as jnp
from jax import lax
from jax.experimental import pallas as pl
from jax.experimental.pallas import tpu as pltpu
from jax.sharding import PartitionSpec as P

HEAD_DIM = 64
ROT_DIM = 32
GROUP = 4
CORES = 2
BF16 = jnp.bfloat16
F32 = jnp.float32
GELU_A = math.sqrt(2.0 / math.pi)
GELU_B = 0.044715
SCORE_SCALE = 1.0 / math.sqrt(HEAD_DIM)
VMEM_LIMIT = 50 * 2**20


def mm(a, b, ca=1, cb=0):
    return lax.dot_general(a, b, (((ca,), (cb,)), ((), ())), preferred_element_type=F32)


def whole(shape):
    zeros = (0,) * len(shape)
    return pl.BlockSpec(tuple(shape), lambda i, sc: zeros)


def lead(shape, index=lambda i, sc: i):
    tail = (0,) * (len(shape) - 1)
    return pl.BlockSpec(tuple(shape), lambda i, sc: (index(i, sc),) + tail)


def run(name, body, steps, scalars, ins, outs, scratch=(), flops=0):
    size = lambda shape, dtype: math.prod(shape) * jnp.dtype(dtype).itemsize
    moved = sum(size(a.shape, a.dtype) for a, _ in ins) + sum(size(s, d) for s, d, _ in outs)
    return pl.pallas_call(
        body,
        name=name,
        out_shape=[jax.ShapeDtypeStruct(s, d) for s, d, _ in outs],
        grid_spec=pltpu.PrefetchScalarGridSpec(
            num_scalar_prefetch=1,
            grid=(steps,),
            in_specs=[spec for _, spec in ins],
            out_specs=[spec for _, _, spec in outs],
            scratch_shapes=list(scratch),
        ),
        compiler_params=pltpu.CompilerParams(vmem_limit_bytes=VMEM_LIMIT),
        cost_estimate=pl.CostEstimate(flops=flops, bytes_accessed=moved, transcendentals=0),
    )(scalars, *[a for a, _ in ins])


def rotated(x, left, right):
    h = ROT_DIM // 2
    to_left = jnp.concatenate([x[:, h:], x[:, :h]], axis=1)
    to_right = jnp.concatenate([x[:, -h:], x[:, :-h]], axis=1)
    return to_left * left + to_right * right


def gelu_parts(u):
    t = jnp.tanh(GELU_A * (u + GELU_B * u * u * u))
    return 0.5 * u * (1.0 + t), t


def layout(lengths, rows):
    slots = lengths.shape[0]
    upper = lax.iota(jnp.int32, slots)[:, None] <= lax.iota(jnp.int32, slots)[None, :]
    ends = jnp.sum(jnp.where(upper, lengths[:, None], 0), axis=0)
    ids = lax.iota(jnp.int32, rows)
    passed = ids[:, None] >= ends[None, :]
    begins = jnp.max(jnp.where(passed, ends[None, :], 0), axis=1)
    return begins, ids - begins, (ids < jnp.max(ends)).astype(F32)


def make(n_dp, n_t):
    reps = n_dp // GROUP
    block = GROUP * CORES

    def join(rep, member):
        return (rep // CORES * GROUP + member) * CORES + rep % CORES

    def parts_of(index):
        return index // block * CORES + index % CORES, (index // CORES) % GROUP

    def to_member(value, k):
        pairs = [(i, join(parts_of(i)[0], parts_of(i)[1] ^ k)) for i in range(n_dp)]
        return lax.ppermute(value, "dp", pairs)

    def to_rep(value, s):
        pairs = [(i, join(parts_of(i)[0] ^ s, parts_of(i)[1])) for i in range(n_dp)]
        return lax.ppermute(value, "dp", pairs)

    def to_tensor(value, m):
        return lax.ppermute(value, "tensor", [(i, i ^ m) for i in range(n_t)])

    def per_device(
        hidden_in, seq_lengths, norm_gain, norm_bias, qkv_master, qkv_bias, out_master, out_bias,
        up_master, up_bias, down_master, down_bias, out_grad,
    ):
        rows, width = hidden_in.shape
        db = up_master.shape[0]
        fz = up_master.shape[1] // GROUP
        ez = qkv_master.shape[2] // GROUP
        heads = ez // HEAD_DIM
        fw = fz + 3 * ez
        fo = fz + ez
        part = rows // n_t
        me_dp, me_t = lax.axis_index("dp"), lax.axis_index("tensor")
        me_r, me_z = parts_of(me_dp)
        sc = jnp.stack([me_r, me_z, me_t]).astype(jnp.int32)
        all_rows = GROUP * rows
        gain, shift = norm_gain.reshape(1, width), norm_bias.reshape(1, width)

        def blk(sref, s, k):
            return join(sref[0] ^ s, sref[1] ^ k)

        def at(index, size):
            return pl.ds(pl.multiple_of(index * size, size), size)

        def from_members(mine):
            return jnp.stack([to_member(mine, k) for k in range(1, GROUP)])

        def share(b):
            if n_t != 4:
                return [(m, 0, to_tensor(b, m)) for m in range(1, n_t)]
            one, two = to_tensor(b, 1), to_tensor(b, 2)
            half = b.shape[1] // 2
            return [
                (1, 0, one),
                (2, 0, two),
                (3, 0, to_tensor(one[:, :half], 2)),
                (3, half, to_tensor(two[:, half:], 1)),
            ]

        def place(sref, step, own, first, others, metas, out):
            @pl.when(step == 0)
            def _():
                out[0] = own[...]

            @pl.when(step > 0)
            def _():
                out[0, at(sref[2], part), :] = first[0]
                for (m, off, _), ref in zip(metas, others):
                    n = ref.shape[1]
                    start = pl.multiple_of((sref[2] ^ m) * part + off, n)
                    out[0, pl.ds(start, n), :] = ref[0]

        def piece_specs(first, metas):
            prev = lambda i, s: jnp.maximum(i - 1, 0)
            return [(first, lead((1,) + first.shape[1:], prev))] + [
                (a, lead((1,) + a.shape[1:], prev)) for _, _, a in metas
            ]

        member_block = lambda i, s: s[1] ^ i

        def cast_in(s, up, qkv, *rest):
            outs, scr = rest[:GROUP], rest[GROUP]
            for z in range(GROUP):
                scr[z, :, :fz] = up[:, z * fz : (z + 1) * fz].astype(BF16)
                for j in range(3):
                    scr[z, :, fz + j * ez : fz + (j + 1) * ez] = qkv[
                        j, :, z * ez : (z + 1) * ez
                    ].astype(BF16)
            for k in range(GROUP):
                outs[k][...] = scr[s[1] ^ k]

        def cast_out(s, down, out, *outs):
            for k in range(GROUP):
                outs[k][:fz] = down[at(s[1] ^ k, fz), :].astype(BF16)
                outs[k][fz:] = out[at(s[1] ^ k, ez), :].astype(BF16)

        def spread(pieces):
            out = []
            for k in range(GROUP):
                got = to_member(pieces[k], k) if k else pieces[k]
                for s in range(reps):
                    out.append((s, k, to_rep(got, s) if s else got))
            return out

        steps_in = 2
        sent_in = run(
            "cast_in", cast_in, steps_in, sc,
            [
                (up_master, lead((db // steps_in, GROUP * fz))),
                (qkv_master, pl.BlockSpec((3, db // steps_in, GROUP * ez), lambda i, s: (0, i, 0))),
            ],
            [((db, fw), BF16, lead((db // steps_in, fw)))] * GROUP,
            [pltpu.VMEM((GROUP, db // steps_in, fw), BF16)],
        )
        sent_out = run(
            "cast_out", cast_out, 1, sc,
            [(down_master, whole(down_master.shape)), (out_master, whole(out_master.shape))],
            [((fo, db), BF16, whole((fo, db)))] * GROUP,
        )

        own_begins, _, own_valid = layout(seq_lengths[0], rows)
        lengths = [seq_lengths[0]] + [to_member(seq_lengths[0], k) for k in range(1, GROUP)]
        x_mine = lax.dynamic_slice_in_dim(hidden_in, me_t * part, part, 0)
        valid_mine = lax.dynamic_slice_in_dim(own_valid, me_t * part, part, 0)
        x_first = from_members(x_mine)
        x_metas = share(x_first)
        w_in = spread(sent_in)
        g_own = (out_grad.astype(F32) * own_valid[:, None]).astype(BF16)
        g_mine = lax.dynamic_slice_in_dim(g_own, me_t * part, part, 0)
        g_first = from_members(g_mine)
        g_metas = share(g_first)
        w_out = spread(sent_out)

        begins, position, _ = jax.vmap(lambda v: layout(v, rows))(jnp.stack(lengths))
        order = me_z ^ lax.iota(jnp.int32, GROUP)
        begins, position = begins[order], position[order]
        lane = lax.iota(jnp.int32, ez) % HEAD_DIM
        halves = ROT_DIM // 2
        rate = 10000.0 ** (-(2.0 * (lane % halves).astype(F32)) / ROT_DIM)
        rate = jnp.where(lane < ROT_DIM, rate, 0.0)
        angle = position.astype(F32)[:, :, None] * rate
        cosine, sine = jnp.cos(angle), jnp.sin(angle)
        left = jnp.where(lane < halves, -sine, 0.0)
        right = jnp.where(lane >= halves, sine, 0.0)
        begins = begins[:, :, None]

        def norm_body(s, own, first, *rest):
            others = rest[: len(x_metas)]
            gn, bs, x_out, n_out, nt_out, st_out = rest[len(x_metas) :]
            place(s, pl.program_id(0), own, first, others, x_metas, x_out)
            v = x_out[0].astype(F32)
            mean = jnp.mean(v, axis=1, keepdims=True)
            v = v - mean
            scale = lax.rsqrt(jnp.mean(v * v, axis=1, keepdims=True) + 1e-05)
            v = v * scale * gn[...] + bs[...]
            n_out[0] = v.astype(BF16)
            nt_out[...] = v.T.astype(BF16)
            which = lax.broadcasted_iota(jnp.int32, (rows, 128), 1)
            st_out[0] = jnp.where(which == 0, mean, scale)

        x_all, normed, normed_t, stats = run(
            "norm", norm_body, GROUP, sc,
            [(hidden_in, whole(hidden_in.shape))]
            + piece_specs(x_first, x_metas)
            + [(gain, whole(gain.shape)), (shift, whole(shift.shape))],
            [
                ((GROUP, rows, width), BF16, lead((1, rows, width), member_block)),
                ((GROUP, rows, width), BF16, lead((1, rows, width), member_block)),
                ((width, all_rows), BF16, pl.BlockSpec((width, rows), lambda i, s: (0, s[1] ^ i))),
                ((GROUP, rows, 128), F32, lead((1, rows, 128), member_block)),
            ],
        )

        my_bias = jnp.concatenate(
            [
                lax.dynamic_slice_in_dim(up_bias, me_z * fz, fz, 0),
                lax.dynamic_slice_in_dim(qkv_bias, me_z * ez, ez, 1).reshape(-1),
            ]
        ).reshape(1, fw)
        n_w = len(w_in)

        def forward_body(s, x, cs, lf, rt, bg, bias, *rest):
            w, (branch, branch_t, pre, qkv, probs, wide) = rest[:n_w], rest[n_w:]

            @pl.when(pl.program_id(0) == 0)
            def _():
                for (rep, k, _), ref in zip(w_in, w):
                    wide[at(blk(s, rep, k), db), :] = ref[...]

            u = mm(x[0], wide[:, :fz]) + bias[:, :fz]
            pre[0] = u
            act = gelu_parts(u)[0]
            branch[0, :, :fz] = act.astype(BF16)
            branch_t[:fz] = act.T.astype(BF16)
            j = mm(x[0], wide[:, fz:]) + bias[:, fz:]
            c, l, r = cs[0], lf[0], rt[0]
            q, k, v = j[:, :ez], j[:, ez : 2 * ez], j[:, 2 * ez :]
            q = (q * c + rotated(q, l, r)).astype(BF16)
            k = (k * c + rotated(k, l, r)).astype(BF16)
            v = v.astype(BF16)
            qkv[0, :, :ez] = q
            qkv[0, :, ez : 2 * ez] = k
            qkv[0, :, 2 * ez :] = v
            col = lax.broadcasted_iota(jnp.int32, (rows, rows), 1)
            row = lax.broadcasted_iota(jnp.int32, (rows, rows), 0)
            allowed = (col >= bg[0]) & (col <= row)
            for h in range(heads):
                lo, hi = h * HEAD_DIM, (h + 1) * HEAD_DIM
                sco = mm(q[:, lo:hi], k[:, lo:hi], 1, 1) * SCORE_SCALE
                sco = jnp.where(allowed, sco, -1e30)
                e = jnp.exp(sco - jnp.max(sco, axis=1, keepdims=True))
                p = e / jnp.sum(e, axis=1, keepdims=True)
                probs[0, h] = p
                ctx = mm(p.astype(BF16), v[:, lo:hi])
                branch[0, :, fz + lo : fz + hi] = ctx.astype(BF16)
                branch_t[fz + lo : fz + hi] = ctx.T.astype(BF16)

        row_block = lambda n: lead((1, rows, n))
        branch, branch_t, pre, qkv, probs = run(
            "forward", forward_body, GROUP, sc,
            [
                (normed, row_block(width)), (cosine, row_block(ez)), (left, row_block(ez)),
                (right, row_block(ez)), (begins, row_block(1)), (my_bias, whole(my_bias.shape)),
            ]
            + [(a, whole(a.shape)) for _, _, a in w_in],
            [
                ((GROUP, rows, fo), BF16, row_block(fo)),
                ((fo, all_rows), BF16, pl.BlockSpec((fo, rows), lambda i, s: (0, i))),
                ((GROUP, rows, fz), F32, row_block(fz)),
                ((GROUP, rows, 3 * ez), BF16, row_block(3 * ez)),
                ((GROUP, heads, rows, rows), F32, lead((1, heads, rows, rows))),
            ],
            [pltpu.VMEM((width, fw), BF16)],
            flops=2 * all_rows * width * fw,
        )

        def grad_rows_body(s, own, first, *rest):
            others, (g_out, sum_out) = rest[: len(g_metas)], rest[len(g_metas) :]
            place(s, pl.program_id(0), own, first, others, g_metas, g_out)
            sum_out[0] = jnp.sum(g_out[0].astype(F32), axis=0, keepdims=True)

        grads, row_sums = run(
            "grad_rows", grad_rows_body, GROUP, sc,
            [(g_own, whole(g_own.shape))] + piece_specs(g_first, g_metas),
            [
                ((GROUP, rows, width), BF16, lead((1, rows, width), member_block)),
                ((GROUP, 1, width), F32, lead((1, 1, width), member_block)),
            ],
        )

        def rep_of(i):
            return reps - 1 - i // GROUP

        def weight_grad(name, left_arr, left_spec, right_arr, right_spec, shape, product):
            def body(s, a, b, *outs):
                i = pl.program_id(0)
                got = product(a, b)
                for n in range(1, reps):
                    @pl.when(rep_of(i) == n)
                    def _(n=n):
                        outs[n][0] = got.astype(BF16)

                @pl.when(rep_of(i) == 0)
                def _():
                    outs[0][0] = got

            def out_index(n):
                first = (reps - 1 - n) * GROUP
                return lambda i, s: jnp.clip(i - first, 0, GROUP - 1)

            return run(
                name, body, GROUP * reps, sc,
                [(left_arr, left_spec), (right_arr, right_spec)],
                [
                    ((GROUP,) + shape, BF16 if n else F32, lead((1,) + shape, out_index(n)))
                    for n in range(reps)
                ],
                flops=2 * all_rows * width * shape[0] * shape[1] // db,
            )

        def block_of(i, s):
            return blk(s, rep_of(i), i % GROUP)

        def collect(grads_by_rep):
            total = grads_by_rep[0]
            for s in range(1, reps):
                total = total + to_rep(grads_by_rep[s], s).astype(F32)
            total = total.astype(BF16)
            return [total[0]] + [to_member(total[k], k) for k in range(1, GROUP)]

        out_parts = weight_grad(
            "out_weight_grad",
            branch_t, whole(branch_t.shape),
            grads, pl.BlockSpec((GROUP, rows, db), lambda i, s: (0, 0, block_of(i, s))),
            (fo, db),
            lambda a, b: mm(a[...], b[...].reshape(all_rows, db)),
        )
        out_pieces = collect(out_parts)

        def finish_out(s, *refs):
            pieces, (down, out) = refs[:GROUP], refs[GROUP:]
            for k in range(GROUP):
                down[at(s[1] ^ k, fz), :] = pieces[k][:fz].astype(F32)
                out[at(s[1] ^ k, ez), :] = pieces[k][fz:].astype(F32)

        down_master_grad, out_master_grad = run(
            "finish_out", finish_out, 1, sc,
            [(a, whole(a.shape)) for a in out_pieces],
            [(down_master.shape, F32, whole(down_master.shape)), (out_master.shape, F32, whole(out_master.shape))],
        )

        def backward_body(s, g, pre, qkv, probs, cs, lf, rt, *rest):
            w, (wide_out, sum_out, w_all) = rest[:n_w], rest[n_w:]

            @pl.when(pl.program_id(0) == 0)
            def _():
                for (rep, k, _), ref in zip(w_out, w):
                    w_all[:, at(blk(s, rep, k), db)] = ref[...]

            ga = mm(g[0], w_all[:fz], 1, 1)
            u = pre[0]
            t = gelu_parts(u)[1]
            slope = 0.5 * (1.0 + t) + 0.5 * u * (1.0 - t * t) * (
                GELU_A * (1.0 + 3.0 * GELU_B * u * u)
            )
            gp = (ga * slope).astype(BF16)
            wide_out[0, :, :fz] = gp
            sum_out[0, :, :fz] = jnp.sum(gp.astype(F32), axis=0, keepdims=True)
            gc = mm(g[0], w_all[fz:], 1, 1).astype(BF16)
            q, k, v = qkv[0, :, :ez], qkv[0, :, ez : 2 * ez], qkv[0, :, 2 * ez :]
            dq, dk, dv = [], [], []
            for h in range(heads):
                lo, hi = h * HEAD_DIM, (h + 1) * HEAD_DIM
                p, gch = probs[0, h], gc[:, lo:hi]
                dv.append(mm(p.astype(BF16), gch, 0, 0))
                dp = mm(gch, v[:, lo:hi], 1, 1)
                ds = (p * (dp - jnp.sum(p * dp, axis=1, keepdims=True))).astype(BF16)
                dq.append(mm(ds, k[:, lo:hi]) * SCORE_SCALE)
                dk.append(mm(ds, q[:, lo:hi], 0, 0) * SCORE_SCALE)
            c, l, r = cs[0], lf[0], rt[0]
            join_heads = lambda parts: parts[0] if heads == 1 else jnp.concatenate(parts, axis=1)
            dq, dk, dv = join_heads(dq), join_heads(dk), join_heads(dv)
            dq = dq * c - rotated(dq, l, r)
            dk = dk * c - rotated(dk, l, r)
            for j, d in enumerate((dq, dk, dv)):
                low = d.astype(BF16)
                lo = fz + j * ez
                wide_out[0, :, lo : lo + ez] = low
                sum_out[0, :, lo : lo + ez] = jnp.sum(low.astype(F32), axis=0, keepdims=True)

        wide, wide_sums = run(
            "backward", backward_body, GROUP, sc,
            [
                (grads, row_block(width)), (pre, row_block(fz)), (qkv, row_block(3 * ez)),
                (probs, lead((1, heads, rows, rows))), (cosine, row_block(ez)),
                (left, row_block(ez)), (right, row_block(ez)),
            ]
            + [(a, whole(a.shape)) for _, _, a in w_out],
            [((GROUP, rows, fw), BF16, row_block(fw)), ((GROUP, 1, fw), F32, lead((1, 1, fw)))],
            [pltpu.VMEM((fo, width), BF16)],
            flops=2 * all_rows * width * fo,
        )

        def parted(sref, y, outs):
            for m in range(n_t):
                outs[m][0] = y[at(sref[2] ^ m, part), :].astype(BF16)

        part_outs = [((GROUP, part, width), BF16, lead((1, part, width)))] * n_t

        def normed_grad_body(s, gw, x, st, *rest):
            w, outs, (sums, y) = rest[:n_w], rest[n_w : n_w + n_t], rest[n_w + n_t :]
            for (rep, k, _), ref in zip(w_in, w):
                y[:, at(blk(s, rep, k), db)] = mm(gw[0], ref[...], 1, 1)
            parted(s, y, outs)
            v = y[...]
            hat = (x[0].astype(F32) - st[0, :, 0:1]) * st[0, :, 1:2]

            @pl.when(pl.program_id(0) == 0)
            def _():
                sums[...] = jnp.zeros(sums.shape, F32)

            sums[0:1] += jnp.sum(v * hat, axis=0, keepdims=True)
            sums[1:2] += jnp.sum(v, axis=0, keepdims=True)

        *gn_parts, pair = run(
            "normed_grad", normed_grad_body, GROUP, sc,
            [(wide, row_block(fw)), (x_all, row_block(width)), (stats, row_block(128))]
            + [(a, whole(a.shape)) for _, _, a in w_in],
            part_outs + [((8, width), F32, whole((8, width)))],
            [pltpu.VMEM((rows, width), F32)],
            flops=2 * all_rows * width * fw,
        )
        pair = pair[:2]

        def out_body(s, br, *rest):
            w, outs, (y,) = rest[:n_w], rest[n_w : n_w + n_t], rest[n_w + n_t :]
            for (rep, k, _), ref in zip(w_out, w):
                y[:, at(blk(s, rep, k), db)] = mm(br[0], ref[...])
            parted(s, y, outs)

        out_sums = run(
            "out_rows", out_body, GROUP, sc,
            [(branch, row_block(fo))] + [(a, whole(a.shape)) for _, _, a in w_out],
            part_outs,
            [pltpu.VMEM((rows, width), F32)],
            flops=2 * all_rows * width * fo,
        )

        def add_tensor(name, parts):
            got = [parts[0]] + [to_tensor(parts[m], m) for m in range(1, n_t)]

            def body(s, *refs):
                ins, outs = refs[:n_t], refs[n_t:]
                total = ins[0][0].astype(F32)
                for ref in ins[1:]:
                    total = total + ref[0].astype(F32)
                i = pl.program_id(0)

                @pl.when(i == 0)
                def _():
                    outs[0][...] = total

                for k in range(1, GROUP):
                    @pl.when(i == k)
                    def _(k=k):
                        outs[k][...] = total.astype(BF16)

            sums = run(
                name, body, GROUP, sc,
                [(a, lead((1, part, width), member_block)) for a in got],
                [((part, width), BF16 if k else F32, whole((part, width))) for k in range(GROUP)],
            )
            return [sums[0]] + [to_member(sums[k], k) for k in range(1, GROUP)]

        mine_rows = lead((part, width), lambda i, s: s[2])

        def join_rows(name, mine):
            metas = share(mine[None])

            def body(s, first, *rest):
                others, out = rest[:-1], rest[-1]
                out[at(s[2], part), :] = first[...]
                for (m, off, _), ref in zip(metas, others):
                    n = ref.shape[1]
                    out[pl.ds(pl.multiple_of((s[2] ^ m) * part + off, n), n), :] = ref[0]

            return run(
                name, body, 1, sc,
                [(mine, whole(mine.shape))] + [(a, whole(a.shape)) for _, _, a in metas],
                [((rows, width), BF16, whole((rows, width)))],
            )[0]

        gn_sums = add_tensor("gn_add", gn_parts)

        def input_grad_body(s, *refs):
            sums, (x, g, gn, out) = refs[:GROUP], refs[GROUP:]
            total = sums[0][...]
            for ref in sums[1:]:
                total = total + ref[...].astype(F32)
            v = x[...].astype(F32)
            v = v - jnp.mean(v, axis=1, keepdims=True)
            scale = lax.rsqrt(jnp.mean(v * v, axis=1, keepdims=True) + 1e-05)
            hat = v * scale
            gy = total * gn[...]
            d = gy - jnp.mean(gy, axis=1, keepdims=True) - hat * jnp.mean(gy * hat, axis=1, keepdims=True)
            out[...] = (g[...].astype(F32) + d * scale).astype(BF16)

        input_grad_mine = run(
            "input_grad", input_grad_body, 1, sc,
            [(a, whole(a.shape)) for a in gn_sums]
            + [(hidden_in, mine_rows), (out_grad, mine_rows), (gain, whole(gain.shape))],
            [((part, width), BF16, whole((part, width)))],
        )[0]
        input_grad = join_rows("input_grad_rows", input_grad_mine)

        o_sums = add_tensor("out_add", out_sums)
        both_bias = (out_bias + down_bias).reshape(1, width)

        def hidden_out_body(s, *refs):
            sums, (x, ok, bias, out) = refs[:GROUP], refs[GROUP:]
            total = sums[0][...]
            for ref in sums[1:]:
                total = total + ref[...].astype(F32)
            out[...] = (x[...].astype(F32) + ok[...] * (total + bias[...])).astype(BF16)

        hidden_out_mine = run(
            "hidden_out", hidden_out_body, 1, sc,
            [(a, whole(a.shape)) for a in o_sums]
            + [(hidden_in, mine_rows), (valid_mine[:, None], whole((part, 1))), (both_bias, whole(both_bias.shape))],
            [((part, width), BF16, whole((part, width)))],
        )[0]
        hidden_out = join_rows("hidden_out_rows", hidden_out_mine)

        in_parts = weight_grad(
            "in_weight_grad",
            normed_t, lead((db, all_rows), block_of),
            wide, whole(wide.shape),
            (db, fw),
            lambda a, b: mm(a[...], b[...].reshape(all_rows, fw)),
        )
        in_pieces = collect(in_parts)

        def finish_in(s, *refs):
            pieces, (up, qkv, scr) = refs[:GROUP], refs[GROUP:]
            for k in range(GROUP):
                scr[s[1] ^ k] = pieces[k][...]
            for z in range(GROUP):
                up[:, z * fz : (z + 1) * fz] = scr[z, :, :fz].astype(F32)
                for j in range(3):
                    lo = fz + j * ez
                    qkv[j, :, z * ez : (z + 1) * ez] = scr[z, :, lo : lo + ez].astype(F32)

        up_master_grad, qkv_master_grad = run(
            "finish_in", finish_in, 2, sc,
            [(a, lead((db // 2, fw))) for a in in_pieces],
            [
                (up_master.shape, F32, lead((db // 2, GROUP * fz))),
                (qkv_master.shape, F32, pl.BlockSpec((3, db // 2, GROUP * ez), lambda i, s: (0, i, 0))),
            ],
            [pltpu.VMEM((GROUP, db // 2, fw), BF16)],
        )

        def doubling(value, count, move):
            hop = 1
            while hop < count:
                value = value + move(value, hop)
                hop *= 2
            return value

        pair = doubling(doubling(doubling(pair, reps, to_rep), n_t, to_tensor), GROUP, to_member)
        flat = row_sums.reshape(GROUP, width)
        bias_total = doubling((flat[0] + flat[1]) + (flat[2] + flat[3]), reps, to_rep)
        flat = wide_sums.reshape(GROUP, fw)
        wide_sum = doubling((flat[0] + flat[1]) + (flat[2] + flat[3]), reps, to_rep)
        up_bias_grad = jnp.zeros(up_bias.shape, F32)
        qkv_bias_grad = jnp.zeros(qkv_bias.shape, F32)
        for k in range(GROUP):
            z = me_z ^ k
            piece = to_member(wide_sum, k) if k else wide_sum
            up_bias_grad = lax.dynamic_update_slice(up_bias_grad, piece[:fz], (z * fz,))
            qkv_bias_grad = lax.dynamic_update_slice(
                qkv_bias_grad, piece[fz:].reshape(3, ez), (0, z * ez)
            )
        return (
            hidden_out, input_grad, pair[0], pair[1], qkv_master_grad, qkv_bias_grad,
            out_master_grad, bias_total, up_master_grad, up_bias_grad, down_master_grad, bias_total,
        )

    return per_device


def solution(mesh):
    placed = (
        P("dp", None), P("dp", None), P(), P(), P(None, "dp", "tensor"), P(None, "tensor"),
        P("tensor", "dp"), P(), P("dp", "tensor"), P("tensor"), P("tensor", "dp"), P(), P("dp", None),
    )
    return jax.shard_map(
        make(mesh.shape["dp"], mesh.shape["tensor"]),
        mesh=mesh,
        in_specs=placed,
        out_specs=(
            P("dp", None), P("dp", None), P(), P(), P(None, "dp", "tensor"), P(None, "tensor"),
            P("tensor", "dp"), P(), P("dp", "tensor"), P("tensor"), P("tensor", "dp"), P(),
        ),
        check_vma=False,
    )
```

```python
import functools
import math

import jax
import jax.numpy as jnp
from jax import lax
from jax.experimental import pallas as pl
from jax.experimental.pallas import tpu as pltpu
from jax.sharding import PartitionSpec as P

HEAD_DIM = 64
ROT_DIM = 32
GROUP = 4
CORES = 2
BF16 = jnp.bfloat16
F32 = jnp.float32
GELU_A = math.sqrt(2.0 / math.pi)
GELU_B = 0.044715
SCORE_SCALE = 1.0 / math.sqrt(HEAD_DIM)
VMEM_LIMIT = 50 * 2**20
GATES = {'g_far': ('x_far',), 'in_stack': ('x_first', 'l_near', 'g_far'), 'x_near': ('l_near', 'g_far'), 'g_first': ('x_first',), 'x_rest': ('tables',), 'out_stack': ('g_first', 'in_stack', 'x_near', 'x_rest'), 'w_in': ('norm', 'x_near', 'x_rest'), 'g_near': ('x_rest', 'in_stack'), 'forward': ('g_near',), 'w_out': ('forward',), 'out_weight_grad_other': ('out_rows',), 'backward': ('out_rows', 'out_weight_grad'), 'gn_got': ('o_got', 'out_pieces'), 'in_weight_grad_other': ('normed_grad',), 'out_add': ('normed_grad',), 'small': ('gn_add',), 'normed_grad': ('o_got',), 'out_add_sent': ('in_weight_grad',), 'o_got': ('out_weight_grad',), 'small_member': ('gn_sums',), 'out_weight_grad': ('out_rows',)}
COSTS = {'cast_in': 352, 'cast_out': 1518, 'tables': 858, 'norm': 715, 'forward': 8250, 'grad_rows': 2904, 'out_rows': 5082, 'out_weight_grad': 3498, 'backward': 9900, 'normed_grad': 7788, 'in_weight_grad': 682, 'out_add': 2706, 'gn_add': 7920, 'hidden_out': 594, 'input_grad': 726, 'hidden_out_rows': 176, 'input_grad_rows': 1056, 'finish_out': 1650, 'finish_in': 1716}
UNIT = 524288
OUT_FIRST = True


def mm(a, b, ca=1, cb=0):
    return lax.dot_general(a, b, (((ca,), (cb,)), ((), ())), preferred_element_type=F32)


def whole(shape):
    zeros = (0,) * len(shape)
    return pl.BlockSpec(tuple(shape), lambda i, sc: zeros)


def lead(shape, index=lambda i, sc: i):
    tail = (0,) * (len(shape) - 1)
    return pl.BlockSpec(tuple(shape), lambda i, sc: (index(i, sc),) + tail)


def run(name, body, steps, scalars, ins, outs, scratch=(), flops=0):
    size = lambda shape, dtype: math.prod(shape) * jnp.dtype(dtype).itemsize
    moved = sum(size(a.shape, a.dtype) for a, _ in ins) + sum(size(s, d) for s, d, _ in outs)
    return pl.pallas_call(
        body,
        name=name,
        out_shape=[jax.ShapeDtypeStruct(s, d) for s, d, _ in outs],
        grid_spec=pltpu.PrefetchScalarGridSpec(
            num_scalar_prefetch=1,
            grid=(steps,),
            in_specs=[spec for _, spec in ins],
            out_specs=[spec for _, _, spec in outs],
            scratch_shapes=list(scratch),
        ),
        compiler_params=pltpu.CompilerParams(vmem_limit_bytes=VMEM_LIMIT),
        cost_estimate=pl.CostEstimate(
            flops=COSTS.get(name, 1000) * UNIT, bytes_accessed=moved, transcendentals=0
        ),
    )(scalars, *[a for a, _ in ins])


def after(value, *done):
    return lax.optimization_barrier((value,) + done)[0]


def rotated(x, left, right):
    h = ROT_DIM // 2
    to_left = jnp.concatenate([x[:, h:], x[:, :h]], axis=1)
    to_right = jnp.concatenate([x[:, -h:], x[:, :-h]], axis=1)
    return to_left * left + to_right * right


def gelu_parts(u):
    t = jnp.tanh(GELU_A * (u + GELU_B * u * u * u))
    return 0.5 * u * (1.0 + t), t


def layout(lengths, rows):
    slots = lengths.shape[0]
    upper = lax.iota(jnp.int32, slots)[:, None] <= lax.iota(jnp.int32, slots)[None, :]
    ends = jnp.sum(jnp.where(upper, lengths[:, None], 0), axis=0)
    ids = lax.iota(jnp.int32, rows)
    passed = ids[:, None] >= ends[None, :]
    begins = jnp.max(jnp.where(passed, ends[None, :], 0), axis=1)
    return begins, ids - begins, (ids < jnp.max(ends)).astype(F32)


def make(n_dp, n_t):
    reps = n_dp // GROUP
    block = GROUP * CORES

    def join(rep, member):
        return (rep // CORES * GROUP + member) * CORES + rep % CORES

    def parts_of(index):
        return index // block * CORES + index % CORES, (index // CORES) % GROUP

    def to_member(value, k):
        pairs = [(i, join(parts_of(i)[0], parts_of(i)[1] ^ k)) for i in range(n_dp)]
        return lax.ppermute(value, "dp", pairs)

    members = [[join(rep, z) for z in range(GROUP)] for rep in range(reps)]

    def among_members(value):
        return lax.all_to_all(value, "dp", 0, 0, axis_index_groups=members, tiled=True)

    def to_rep(value, s):
        pairs = [(i, join(parts_of(i)[0] ^ s, parts_of(i)[1])) for i in range(n_dp)]
        return lax.ppermute(value, "dp", pairs)

    def to_tensor(value, m):
        return lax.ppermute(value, "tensor", [(i, i ^ m) for i in range(n_t)])

    def per_device(
        hidden_in, seq_lengths, norm_gain, norm_bias, qkv_master, qkv_bias, out_master, out_bias,
        up_master, up_bias, down_master, down_bias, out_grad,
    ):
        rows, width = hidden_in.shape
        db = up_master.shape[0]
        fz = up_master.shape[1] // GROUP
        ez = qkv_master.shape[2] // GROUP
        heads = ez // HEAD_DIM
        fw = fz + 3 * ez
        fo = fz + ez
        part = rows // n_t
        me_dp, me_t = lax.axis_index("dp"), lax.axis_index("tensor")
        me_r, me_z = parts_of(me_dp)
        sc = jnp.stack([me_r, me_z, me_t]).astype(jnp.int32)
        all_rows = GROUP * rows
        gain, shift = norm_gain.reshape(1, width), norm_bias.reshape(1, width)

        def blk(sref, s, z):
            return join(sref[0] ^ s, z)

        done = {}

        def gate(name, value):
            waits = [a for n in GATES.get(name, ()) if n in done for a in done[n]]
            return after(value, *waits) if waits else value

        def at(index, size):
            return pl.ds(pl.multiple_of(index * size, size), size)

        def swapped(i):
            return (i % 2) * 2 + i // 2

        def first_hop(mine):
            return to_member(mine, 2)

        def second_hop(mine, far):
            near = to_member(jnp.stack([mine, far]), 1)
            return jnp.concatenate([far[None], near], axis=0)

        paired = n_t == 4
        half = part // 2

        def exchange(b):
            return [to_tensor(b, m) for m in ((1, 2) if paired else range(1, n_t))]

        def forwarded(got):
            return [got[0][:, :half], got[1][:, half:]] if paired else []

        def pieces(got, rest, start=0):
            if not paired:
                return [(m, 0, part, start, a) for m, a in enumerate(got, 1)]
            (one, one_at), (two, two_at) = got
            (far, far_at), (near, near_at) = rest
            return [
                (1, 0, part, one_at, one),
                (2, 0, part, two_at, two),
                (3, 0, half, far_at, far),
                (3, half, half, near_at, near),
            ]

        def place(sref, step, own, first, others, metas, out):
            @pl.when(step == 0)
            def _():
                out[0] = own[...]

            @pl.when(step > 0)
            def _():
                out[0, at(sref[2], part), :] = first[0]
                for (m, off, n, lo, _), ref in zip(metas, others):
                    start = pl.multiple_of((sref[2] ^ m) * part + off, n)
                    out[0, pl.ds(start, n), :] = ref[0, lo : lo + n]

        def piece_specs(first, metas):
            prev = lambda i, s: jnp.maximum(i - 1, 0)
            return [(first, lead((1,) + first.shape[1:], prev))] + [
                (a, lead((1,) + a.shape[1:], prev)) for *_, a in metas
            ]

        member_block = lambda i, s: s[1] ^ swapped(i)

        def cast_in(s, up, qkv, out):
            for z in range(GROUP):
                out[z, :, :fz] = up[:, z * fz : (z + 1) * fz].astype(BF16)
                for j in range(3):
                    lo = fz + j * ez
                    out[z, :, lo : lo + ez] = qkv[j, :, z * ez : (z + 1) * ez].astype(BF16)

        def cast_out(s, down, wo, out):
            out[0, :fz] = down[...].astype(BF16)
            out[0, fz:] = wo[...].astype(BF16)

        def to_reps(stack):
            return [stack] + [to_rep(stack, s) for s in range(1, reps)]

        steps_in = 2
        in_block = [
            lead((db // steps_in, GROUP * fz)),
            pl.BlockSpec((3, db // steps_in, GROUP * ez), lambda i, s: (0, i, 0)),
            pl.BlockSpec((GROUP, db // steps_in, fw), lambda i, s: (0, i, 0)),
        ]
        out_block = [lead((fz, db)), lead((ez, db)), lead((1, fo, db))]
        sent_in = run(
            "cast_in", cast_in, steps_in, sc,
            [(up_master, in_block[0]), (qkv_master, in_block[1])],
            [((GROUP, db, fw), BF16, in_block[2])],
        )[0]
        sent_out = run(
            "cast_out", cast_out, GROUP, sc,
            [(down_master, out_block[0]), (out_master, out_block[1])],
            [((GROUP, fo, db), BF16, out_block[2])],
        )[0]

        _, _, own_valid = layout(seq_lengths[0], rows)
        x_mine = lax.dynamic_slice_in_dim(hidden_in, me_t * part, part, 0)
        valid_mine = lax.dynamic_slice_in_dim(own_valid, me_t * part, part, 0)
        x_far = first_hop(x_mine)
        done["x_far"] = [x_far]
        l_far = to_member(seq_lengths, 2)
        g_own = (out_grad.astype(F32) * own_valid[:, None]).astype(BF16)
        g_mine = lax.dynamic_slice_in_dim(g_own, me_t * part, part, 0)
        x_first = second_hop(x_mine, gate("x_first", x_far))
        l_near = to_member(jnp.concatenate([seq_lengths, l_far]), 1)
        done["x_first"] = [x_first]
        done["l_near"] = [l_near]
        g_far = first_hop(gate("g_far", g_mine))
        done["g_far"] = [g_far]
        in_stack = among_members(gate("in_stack", sent_in))
        done["in_stack"] = [in_stack]
        x_near = exchange(gate("x_near", x_first))
        done["x_near"] = x_near
        g_first = second_hop(g_mine, gate("g_first", g_far))
        done["g_first"] = [g_first]

        def table_body(s, own, far, near, cs, lf, rt, bg):
            i = pl.program_id(0)
            row = lax.broadcasted_iota(jnp.int32, (rows, ez), 0)
            begin, end = jnp.zeros((rows, ez), jnp.int32), jnp.int32(0)
            for j in range(seq_lengths.shape[1]):
                length = jnp.where(i == 0, own[0, j], jnp.where(i == 1, far[0, j], near[0, j]))
                length = jnp.where(i == 3, near[1, j], length)
                end = end + length
                begin = jnp.where(row >= end, end, begin)
            lane = lax.broadcasted_iota(jnp.int32, (rows, ez), 1) % HEAD_DIM
            halves = ROT_DIM // 2
            step = (lane % halves).astype(F32) * (-2.0 / ROT_DIM)
            rate = jnp.exp(step * math.log(10000.0))
            angle = jnp.where(lane < ROT_DIM, (row - begin).astype(F32) * rate, 0.0)
            sine = jnp.sin(angle)
            cs[0] = jnp.cos(angle)
            lf[0] = jnp.where(lane < halves, -sine, 0.0)
            rt[0] = jnp.where(lane >= halves, sine, 0.0)
            bg[0] = begin[:, 0:1]

        smem = pl.BlockSpec(memory_space=pltpu.SMEM)
        cosine, left, right, begins = run(
            "tables", table_body, GROUP, sc,
            [(seq_lengths, smem), (l_far, smem), (l_near, smem)],
            [((GROUP, rows, ez), F32, lead((1, rows, ez), member_block))] * 3
            + [((GROUP, rows, 1), jnp.int32, lead((1, rows, 1), member_block))],
        )

        done["tables"] = [cosine]
        x_rest = [to_tensor(gate("x_rest", b), m) for b, m in zip(forwarded(x_near), (2, 1))]
        done["x_rest"] = x_rest
        if paired:
            x_metas = pieces([(a, 0) for a in x_near], [(a, 0) for a in x_rest])
        else:
            x_metas = pieces(x_near, None)

        def norm_body(s, own, first, *rest):
            others = rest[: len(x_metas)]
            gn, bs, x_out, n_out, st_out = rest[len(x_metas) :]
            place(s, pl.program_id(0), own, first, others, x_metas, x_out)
            v = x_out[0].astype(F32)
            mean = jnp.mean(v, axis=1, keepdims=True)
            v = v - mean
            scale = lax.rsqrt(jnp.mean(v * v, axis=1, keepdims=True) + 1e-05)
            v = v * scale * gn[...] + bs[...]
            n_out[0] = v.astype(BF16)
            which = lax.broadcasted_iota(jnp.int32, (rows, 128), 1)
            st_out[0] = jnp.where(which == 0, mean, scale)

        x_all, normed, stats = run(
            "norm", norm_body, GROUP, sc,
            [(hidden_in, whole(hidden_in.shape))]
            + piece_specs(x_first, x_metas)
            + [(gain, whole(gain.shape)), (shift, whole(shift.shape))],
            [
                ((GROUP, rows, width), BF16, lead((1, rows, width), member_block)),
                ((GROUP, rows, width), BF16, lead((1, rows, width), member_block)),
                ((GROUP, rows, 128), F32, lead((1, rows, 128), member_block)),
            ],
        )

        done["norm"] = [normed]
        out_stack = among_members(gate("out_stack", sent_out))
        done["out_stack"] = [out_stack]
        w_in = to_reps(gate("w_in", in_stack))
        g_near = exchange(gate("g_near", g_first))
        done["g_near"] = g_near

        my_bias = jnp.concatenate(
            [
                lax.dynamic_slice_in_dim(up_bias, me_z * fz, fz, 0),
                lax.dynamic_slice_in_dim(qkv_bias, me_z * ez, ez, 1).reshape(-1),
            ]
        ).reshape(1, fw)
        n_w = reps

        def forward_body(s, x, cs, lf, rt, bg, bias, *rest):
            w, (branch, pre, qkv, probs, wide) = rest[:n_w], rest[n_w:]

            @pl.when(pl.program_id(0) == 0)
            def _():
                for rep in range(reps):
                    for k in range(GROUP):
                        wide[at(blk(s, rep, k), db), :] = w[rep][k]

            u = mm(x[0], wide[:, :fz]) + bias[:, :fz]
            pre[0] = u
            act = gelu_parts(u)[0]
            branch[0, :, :fz] = act.astype(BF16)
            j = mm(x[0], wide[:, fz:]) + bias[:, fz:]
            c, l, r = cs[0], lf[0], rt[0]
            q, k, v = j[:, :ez], j[:, ez : 2 * ez], j[:, 2 * ez :]
            q = (q * c + rotated(q, l, r)).astype(BF16)
            k = (k * c + rotated(k, l, r)).astype(BF16)
            v = v.astype(BF16)
            qkv[0, :, :ez] = q
            qkv[0, :, ez : 2 * ez] = k
            qkv[0, :, 2 * ez :] = v
            col = lax.broadcasted_iota(jnp.int32, (rows, rows), 1)
            row = lax.broadcasted_iota(jnp.int32, (rows, rows), 0)
            allowed = (col >= bg[0]) & (col <= row)
            for h in range(heads):
                lo, hi = h * HEAD_DIM, (h + 1) * HEAD_DIM
                sco = mm(q[:, lo:hi], k[:, lo:hi], 1, 1) * SCORE_SCALE
                sco = jnp.where(allowed, sco, -1e30)
                e = jnp.exp(sco - jnp.max(sco, axis=1, keepdims=True))
                p = e / jnp.sum(e, axis=1, keepdims=True)
                probs[0, h] = p
                ctx = mm(p.astype(BF16), v[:, lo:hi])
                branch[0, :, fz + lo : fz + hi] = ctx.astype(BF16)

        row_block = lambda n: lead((1, rows, n))
        branch, pre, qkv, probs = run(
            "forward", forward_body, GROUP, sc,
            [
                (gate("forward", normed), row_block(width)), (cosine, row_block(ez)), (left, row_block(ez)),
                (right, row_block(ez)), (begins, row_block(1)), (my_bias, whole(my_bias.shape)),
            ]
            + [(a, whole(a.shape)) for a in w_in],
            [
                ((GROUP, rows, fo), BF16, row_block(fo)),
                ((GROUP, rows, fz), F32, row_block(fz)),
                ((GROUP, rows, 3 * ez), BF16, row_block(3 * ez)),
                ((GROUP, heads, rows, rows), F32, lead((1, heads, rows, rows))),
            ],
            [pltpu.VMEM((width, fw), BF16)],
            flops=2 * all_rows * width * fw,
        )

        done["forward"] = [branch]
        w_out = to_reps(gate("w_out", out_stack))
        g_rest = [to_tensor(gate("g_rest", b), m) for b, m in zip(forwarded(g_near), (2, 1))]
        if paired:
            g_metas = pieces([(a, 0) for a in g_near], [(a, 0) for a in g_rest])
        else:
            g_metas = pieces(g_near, None)

        def grad_rows_body(s, own, first, *rest):
            others, (g_out, sum_out) = rest[: len(g_metas)], rest[len(g_metas) :]
            place(s, pl.program_id(0), own, first, others, g_metas, g_out)
            sum_out[0] = jnp.sum(g_out[0].astype(F32), axis=0, keepdims=True)

        grads, row_sums = run(
            "grad_rows", grad_rows_body, GROUP, sc,
            [(g_own, whole(g_own.shape))] + piece_specs(g_first, g_metas),
            [
                ((GROUP, rows, width), BF16, lead((1, rows, width), member_block)),
                ((GROUP, 1, width), F32, lead((1, 1, width), member_block)),
            ],
        )

        def parted(sref, y, outs):
            for m in range(n_t):
                outs[m][0] = y[at(sref[2] ^ m, part), :].astype(BF16)

        part_outs = [((GROUP, part, width), BF16, lead((1, part, width)))] * n_t

        def out_body(s, br, *rest):
            w, outs, (y,) = rest[:n_w], rest[n_w:-1], rest[-1:]
            for rep in range(reps):
                for k in range(GROUP):
                    y[:, at(blk(s, rep, k), db)] = mm(br[0], w[rep][k])
            parted(s, y, outs)

        def branch_rows():
            out_sums = run(
                "out_rows", out_body, GROUP, sc,
                [(gate("out_rows", branch), row_block(fo))] + [(a, whole(a.shape)) for a in w_out],
                part_outs,
                [pltpu.VMEM((rows, width), F32)],
                flops=2 * all_rows * width * fo,
            )
            done["out_rows"] = [out_sums[0]]
            got = [out_sums[0]] + [
                to_tensor(gate("o_got", out_sums[m]), m) for m in range(1, n_t)
            ]
            done["o_got"] = got[1:]
            return got

        def weight_grad(name, left_arr, left_spec, right_arr, right_spec, shape):
            def product(a, b):
                flat = lambda v: v.reshape(all_rows, v.shape[-1])
                return mm(flat(a[...]), flat(b[...]), 0, 0)

            flops = 2 * all_rows * shape[0] * shape[1] * GROUP
            got = []
            first = gate(name + "_other", right_arr)
            for rep in range(1, reps):
                def other(s, a, b, out):
                    out[0] = product(a, b).astype(BF16)

                sent = run(
                    name + "_other", other, GROUP, sc,
                    [(left_arr, left_spec(rep)), (first, right_spec(rep))],
                    [((GROUP,) + shape, BF16, lead((1,) + shape))],
                    flops=flops,
                )[0]
                done[name + "_other"] = [sent]
                got.append(to_rep(sent, rep))

            def mine(s, a, b, *refs):
                total = product(a, b)
                for ref in refs[:-1]:
                    total = total + ref[0].astype(F32)
                refs[-1][0] = total.astype(BF16)

            right_arr = gate(name, right_arr)
            return run(
                name, mine, GROUP, sc,
                [(left_arr, left_spec(0)), (right_arr, right_spec(0))]
                + [(a, lead((1,) + shape)) for a in got],
                [((GROUP,) + shape, BF16, lead((1,) + shape))],
                flops=flops,
            )[0]

        def columns(rep):
            return pl.BlockSpec((GROUP, rows, db), lambda i, s: (0, 0, blk(s, rep, i)))

        if OUT_FIRST:
            o_got = branch_rows()
        out_parts = weight_grad(
            "out_weight_grad",
            branch, lambda rep: whole(branch.shape),
            grads, columns,
            (fo, db),
        )
        done["out_weight_grad"] = [out_parts]
        out_pieces = among_members(out_parts)
        done["out_pieces"] = [out_pieces]
        if not OUT_FIRST:
            o_got = branch_rows()

        def backward_body(s, g, pre, qkv, probs, cs, lf, rt, *rest):
            w, (wide_out, sum_out, w_all) = rest[:n_w], rest[n_w:]

            @pl.when(pl.program_id(0) == 0)
            def _():
                for rep in range(reps):
                    for k in range(GROUP):
                        w_all[:, at(blk(s, rep, k), db)] = w[rep][k]

            ga = mm(g[0], w_all[:fz], 1, 1)
            u = pre[0]
            t = gelu_parts(u)[1]
            slope = 0.5 * (1.0 + t) + 0.5 * u * (1.0 - t * t) * (
                GELU_A * (1.0 + 3.0 * GELU_B * u * u)
            )
            gp = (ga * slope).astype(BF16)
            wide_out[0, :, :fz] = gp
            sum_out[0, :, :fz] = jnp.sum(gp.astype(F32), axis=0, keepdims=True)
            gc = mm(g[0], w_all[fz:], 1, 1).astype(BF16)
            q, k, v = qkv[0, :, :ez], qkv[0, :, ez : 2 * ez], qkv[0, :, 2 * ez :]
            dq, dk, dv = [], [], []
            for h in range(heads):
                lo, hi = h * HEAD_DIM, (h + 1) * HEAD_DIM
                p, gch = probs[0, h], gc[:, lo:hi]
                dv.append(mm(p.astype(BF16), gch, 0, 0))
                dp = mm(gch, v[:, lo:hi], 1, 1)
                ds = (p * (dp - jnp.sum(p * dp, axis=1, keepdims=True))).astype(BF16)
                dq.append(mm(ds, k[:, lo:hi]) * SCORE_SCALE)
                dk.append(mm(ds, q[:, lo:hi], 0, 0) * SCORE_SCALE)
            c, l, r = cs[0], lf[0], rt[0]
            join_heads = lambda parts: parts[0] if heads == 1 else jnp.concatenate(parts, axis=1)
            dq, dk, dv = join_heads(dq), join_heads(dk), join_heads(dv)
            dq = dq * c - rotated(dq, l, r)
            dk = dk * c - rotated(dk, l, r)
            for j, d in enumerate((dq, dk, dv)):
                low = d.astype(BF16)
                lo = fz + j * ez
                wide_out[0, :, lo : lo + ez] = low
                sum_out[0, :, lo : lo + ez] = jnp.sum(low.astype(F32), axis=0, keepdims=True)

        wide, wide_sums = run(
            "backward", backward_body, GROUP, sc,
            [
                (gate("backward", grads), row_block(width)), (pre, row_block(fz)), (qkv, row_block(3 * ez)),
                (probs, lead((1, heads, rows, rows))), (cosine, row_block(ez)),
                (left, row_block(ez)), (right, row_block(ez)),
            ]
            + [(a, whole(a.shape)) for a in w_out],
            [((GROUP, rows, fw), BF16, row_block(fw)), ((GROUP, 1, fw), F32, lead((1, 1, fw)))],
            [pltpu.VMEM((fo, width), BF16)],
            flops=2 * all_rows * width * fo,
        )

        def normed_grad_body(s, gw, x, st, *rest):
            w, outs, (sums, y) = rest[:n_w], rest[n_w:-2], rest[-2:]
            for rep in range(reps):
                for k in range(GROUP):
                    y[:, at(blk(s, rep, k), db)] = mm(gw[0], w[rep][k], 1, 1)
            parted(s, y, outs)
            v = y[...]
            hat = (x[0].astype(F32) - st[0, :, 0:1]) * st[0, :, 1:2]

            @pl.when(pl.program_id(0) == 0)
            def _():
                sums[...] = jnp.zeros(sums.shape, F32)

            sums[0:1] += jnp.sum(v * hat, axis=0, keepdims=True)
            sums[1:2] += jnp.sum(v, axis=0, keepdims=True)

        *gn_parts, gain_sums = run(
            "normed_grad", normed_grad_body, GROUP, sc,
            [(gate("normed_grad", wide), row_block(fw)), (x_all, row_block(width)), (stats, row_block(128))]
            + [(a, whole(a.shape)) for a in w_in],
            part_outs + [((2, width), F32, whole((2, width)))],
            [pltpu.VMEM((rows, width), F32)],
            flops=2 * all_rows * width * fw,
        )

        def to_members(name, sums):
            return [sums[0]] + [to_member(gate(name, sums[k]), k) for k in range(1, GROUP)]

        k_outs = [((part, width), BF16 if k else F32, whole((part, width))) for k in range(GROUP)]
        own_block = lambda i, s: s[1] ^ i

        def store_members(total, outs):
            i = pl.program_id(0)
            for k in range(GROUP):
                @pl.when(i == k)
                def _(k=k):
                    outs[k][...] = total.astype(outs[k].dtype)

        def among(parts):
            return [parts[0]] + [to_tensor(parts[m], m) for m in range(1, n_t)]

        def add_tensor(name, got):
            def body(s, *refs):
                ins, outs = refs[:n_t], refs[n_t:]
                total = ins[0][0].astype(F32)
                for ref in ins[1:]:
                    total = total + ref[0].astype(F32)
                store_members(total, outs)

            return to_members(
                name + "_sent",
                run(
                    name, body, GROUP, sc,
                    [(a, lead((1, part, width), own_block)) for a in got], k_outs,
                )
            )

        mine_rows = lead((part, width), lambda i, s: s[2])

        def join_rows(name, mine):
            got = [to_tensor(mine, m) for m in range(1, n_t)]

            def body(s, first, *rest):
                for m, ref in enumerate((first,) + rest[:-1]):
                    rest[-1][at(s[2] ^ m, part), :] = ref[...]

            return run(
                name, body, 1, sc,
                [(a, whole(a.shape)) for a in [mine] + got],
                [((rows, width), BF16, whole((rows, width)))],
            )[0]

        done["normed_grad"] = [gn_parts[0]]
        in_parts = weight_grad(
            "in_weight_grad",
            normed, columns,
            wide, lambda rep: whole(wide.shape),
            (db, fw),
        )
        done["in_weight_grad"] = [in_parts]
        gn_got = [gn_parts[0]] + [to_tensor(gate("gn_got", gn_parts[m]), m) for m in range(1, n_t)]
        done["gn_got"] = gn_got[1:]
        o_got[0] = gate("out_add", o_got[0])
        o_sums = add_tensor("out_add", o_got)
        done["out_add"] = [o_sums[0]]
        done["o_sums"] = o_sums[1:]
        gn_got[0] = gate("gn_add", gn_got[0])
        gn_sums = add_tensor("gn_add", gn_got)
        done["gn_add"] = [gn_sums[0]]
        done["gn_sums"] = gn_sums[1:]

        def input_grad_body(s, *refs):
            sums, (x, g, gn, out) = refs[:GROUP], refs[GROUP:]
            total = sums[0][...]
            for ref in sums[1:]:
                total = total + ref[...].astype(F32)
            v = x[...].astype(F32)
            v = v - jnp.mean(v, axis=1, keepdims=True)
            scale = lax.rsqrt(jnp.mean(v * v, axis=1, keepdims=True) + 1e-05)
            hat = v * scale
            gy = total * gn[...]
            d = gy - jnp.mean(gy, axis=1, keepdims=True) - hat * jnp.mean(gy * hat, axis=1, keepdims=True)
            out[...] = (g[...].astype(F32) + d * scale).astype(BF16)

        input_grad_mine = run(
            "input_grad", input_grad_body, 1, sc,
            [(a, whole(a.shape)) for a in gn_sums]
            + [(hidden_in, mine_rows), (out_grad, mine_rows), (gain, whole(gain.shape))],
            [((part, width), BF16, whole((part, width)))],
        )[0]
        input_grad = join_rows("input_grad_rows", input_grad_mine)

        both_bias = (out_bias + down_bias).reshape(1, width)

        def hidden_out_body(s, *refs):
            sums, (x, ok, bias, out) = refs[:GROUP], refs[GROUP:]
            total = sums[0][...]
            for ref in sums[1:]:
                total = total + ref[...].astype(F32)
            out[...] = (x[...].astype(F32) + ok[...] * (total + bias[...])).astype(BF16)

        hidden_out_mine = run(
            "hidden_out", hidden_out_body, 1, sc,
            [(a, whole(a.shape)) for a in o_sums]
            + [(hidden_in, mine_rows), (valid_mine[:, None], whole((part, 1))), (both_bias, whole(both_bias.shape))],
            [((part, width), BF16, whole((part, width)))],
        )[0]
        hidden_out = join_rows("hidden_out_rows", hidden_out_mine)

        in_pieces = among_members(in_parts)

        def finish_in(s, piece, up, qkv):
            for z in range(GROUP):
                up[:, z * fz : (z + 1) * fz] = piece[z, :, :fz].astype(F32)
                for j in range(3):
                    lo = fz + j * ez
                    qkv[j, :, z * ez : (z + 1) * ez] = piece[z, :, lo : lo + ez].astype(F32)

        up_master_grad, qkv_master_grad = run(
            "finish_in", finish_in, steps_in, sc,
            [(in_pieces, in_block[2])],
            [(up_master.shape, F32, in_block[0]), (qkv_master.shape, F32, in_block[1])],
        )

        def finish_out(s, piece, down, wo):
            down[...] = piece[0, :fz].astype(F32)
            wo[...] = piece[0, fz:].astype(F32)

        down_master_grad, out_master_grad = run(
            "finish_out", finish_out, GROUP, sc,
            [(gate("finish_out", out_pieces), out_block[2])],
            [(down_master.shape, F32, out_block[0]), (out_master.shape, F32, out_block[1])],
        )

        def doubling(value, count, move):
            hop = 1
            while hop < count:
                value = value + move(value, hop)
                hop *= 2
            return value

        flat = row_sums.reshape(GROUP, width)
        bias_total = (flat[0] + flat[1]) + (flat[2] + flat[3])
        flat = wide_sums.reshape(GROUP, fw)
        wide_sum = (flat[0] + flat[1]) + (flat[2] + flat[3])
        small = gate("small", jnp.concatenate([gain_sums.reshape(-1), wide_sum, bias_total]))
        small = doubling(small, reps, to_rep)
        bias_total = small[2 * width + fw :]
        gains = doubling(gate("small_tensor", small[: 2 * width]), n_t, to_tensor)
        wide_sum = small[2 * width : 2 * width + fw]
        got = to_member(gate("small_member", jnp.concatenate([gains, wide_sum])), 2)
        gains, wide_far = gains + got[: 2 * width], got[2 * width :]
        got = to_member(jnp.concatenate([gains, wide_sum, wide_far]), 1)
        gains = gains + got[: 2 * width]
        got = got[2 * width :].reshape(2, fw)
        up_bias_grad = jnp.zeros(up_bias.shape, F32)
        qkv_bias_grad = jnp.zeros(qkv_bias.shape, F32)
        for k, piece in ((0, wide_sum), (2, wide_far), (1, got[0]), (3, got[1])):
            z = me_z ^ k
            up_bias_grad = lax.dynamic_update_slice(up_bias_grad, piece[:fz], (z * fz,))
            qkv_bias_grad = lax.dynamic_update_slice(
                qkv_bias_grad, piece[fz:].reshape(3, ez), (0, z * ez)
            )
        return (
            hidden_out, input_grad, gains[:width], gains[width:], qkv_master_grad, qkv_bias_grad,
            out_master_grad, bias_total, up_master_grad, up_bias_grad, down_master_grad, bias_total,
        )

    return per_device


def solution(mesh):
    placed = (
        P("dp", None), P("dp", None), P(), P(), P(None, "dp", "tensor"), P(None, "tensor"),
        P("tensor", "dp"), P(), P("dp", "tensor"), P("tensor"), P("tensor", "dp"), P(), P("dp", None),
    )
    return jax.shard_map(
        make(mesh.shape["dp"], mesh.shape["tensor"]),
        mesh=mesh,
        in_specs=placed,
        out_specs=(
            P("dp", None), P("dp", None), P(), P(), P(None, "dp", "tensor"), P(None, "tensor"),
            P("tensor", "dp"), P(), P("dp", "tensor"), P("tensor"), P("tensor", "dp"), P(),
        ),
        check_vma=False,
    )
```

```python
import functools
import math

import jax
import jax.numpy as jnp
from jax import lax
from jax.experimental import pallas as pl
from jax.experimental.pallas import tpu as pltpu
from jax.sharding import PartitionSpec as P

HEAD_DIM = 64
ROT_DIM = 32
GROUP = 4
CORES = 2
BF16 = jnp.bfloat16
F32 = jnp.float32
GELU_A = math.sqrt(2.0 / math.pi)
GELU_B = 0.044715
SCORE_SCALE = 1.0 / math.sqrt(HEAD_DIM)
VMEM_LIMIT = 50 * 2**20
UNIT = 2**19
(
    CAST_IN, X_FAR, L_FAR, X_FIRST, L_NEAR, G_FAR, CAST_OUT, G_FIRST, IN_STACK, X_NEAR, TABLES,
    X_REST, NORM, G_NEAR, OUT_STACK, W_IN, GRAD_ROWS, FORWARD, W_OUT, OUT_ROWS, O_GOT,
    OUT_WEIGHT_GRAD, OUT_WEIGHT_GRAD_OTHER, OUT_WEIGHT_GRAD_REP, OUT_PIECES, BACKWARD,
    NORMED_GRAD, GN_GOT, IN_WEIGHT_GRAD, IN_WEIGHT_GRAD_OTHER, IN_WEIGHT_GRAD_REP, OUT_ADD,
    OUT_ADD_NEAR, OUT_ADD_PAIR, OUT_ADD_PAIR_FAR, SUMS_LOW, SUMS, SMALL_REP, SUMS_REP,
    SUMS_SPLIT, GN_ADD, GN_ADD_NEAR, HIDDEN_OUT, HIDDEN_OUT_GOT, SMALL_TENSOR, GAINS_TENSOR,
    GN_ADD_PAIR, GN_ADD_PAIR_FAR, GAINS_SENT, HIDDEN_OUT_ROWS, FINISH_OUT, INPUT_GRAD,
    INPUT_GRAD_GOT, SMALL_FAR, GAINS_FAR, FINISH_IN, BIAS_GRADS, INPUT_GRAD_ROWS,
) = range(58)
COSTS = {
    CAST_IN: 14080,
    CAST_OUT: 1518,
    TABLES: 17160,
    NORM: 28600,
    FORWARD: 1,
    GRAD_ROWS: 1936,
    OUT_ROWS: 5082,
    OUT_WEIGHT_GRAD: 3498,
    BACKWARD: 1,
    NORMED_GRAD: 7788,
    IN_WEIGHT_GRAD: 1364,
    OUT_ADD: 4510,
    GN_ADD: 7920,
    HIDDEN_OUT: 594,
    INPUT_GRAD: 726,
    HIDDEN_OUT_ROWS: 1056,
    INPUT_GRAD_ROWS: 1056,
    FINISH_OUT: 1650,
    FINISH_IN: 1716,
    BIAS_GRADS: 10560,
    GN_ADD_PAIR: 132,
    OUT_ADD_PAIR: 1,
    SUMS_SPLIT: 220,
}
GATES = {
    IN_STACK: (X_FIRST, L_NEAR, G_FAR,),
    X_NEAR: (L_NEAR, G_FAR,),
    G_FIRST: (X_FIRST,),
    X_REST: (TABLES,),
    OUT_STACK: (G_FIRST, IN_STACK, X_NEAR,),
    W_IN: (G_FIRST, NORM,),
    G_NEAR: (IN_STACK,),
    BACKWARD: (OUT_ROWS, OUT_WEIGHT_GRAD,),
    GN_GOT: (O_GOT, OUT_PIECES,),
    IN_WEIGHT_GRAD_OTHER: (NORMED_GRAD,),
    IN_WEIGHT_GRAD: (NORMED_GRAD, O_GOT,),
    OUT_ADD: (OUT_PIECES,),
    NORMED_GRAD: (O_GOT,),
    OUT_WEIGHT_GRAD: (OUT_ROWS,),
    SUMS_LOW: (GN_ADD,),
    SMALL_FAR: (GN_ADD_PAIR,),
    GAINS_FAR: (GN_ADD_PAIR, INPUT_GRAD,),
    GRAD_ROWS: (OUT_STACK,),
    SMALL_REP: (IN_WEIGHT_GRAD,),
    GN_ADD_PAIR: (GAINS_TENSOR,),
    INPUT_GRAD_ROWS: (FINISH_IN,),
    INPUT_GRAD: (FINISH_OUT,),
    HIDDEN_OUT_GOT: (GN_ADD,),
    OUT_ADD_PAIR: (IN_WEIGHT_GRAD,),
    CAST_OUT: (X_FAR,),
    HIDDEN_OUT_ROWS: (GN_ADD_PAIR,),
}


def mm(a, b, ca=1, cb=0):
    return lax.dot_general(a, b, (((ca,), (cb,)), ((), ())), preferred_element_type=F32)


def whole(shape):
    zeros = (0,) * len(shape)
    return pl.BlockSpec(tuple(shape), lambda i, sc: zeros)


def lead(shape, index=lambda i, sc: i):
    tail = (0,) * (len(shape) - 1)
    return pl.BlockSpec(tuple(shape), lambda i, sc: (index(i, sc),) + tail)


def run(name, body, steps, scalars, ins, outs, scratch=()):
    size = lambda shape, dtype: math.prod(shape) * jnp.dtype(dtype).itemsize
    moved = sum(size(a.shape, a.dtype) for a, _ in ins) + sum(size(s, d) for s, d, _ in outs)
    return pl.pallas_call(
        body,
        out_shape=[jax.ShapeDtypeStruct(s, d) for s, d, _ in outs],
        grid_spec=pltpu.PrefetchScalarGridSpec(
            num_scalar_prefetch=1,
            grid=(steps,),
            in_specs=[spec for _, spec in ins],
            out_specs=[spec for _, _, spec in outs],
            scratch_shapes=list(scratch),
        ),
        compiler_params=pltpu.CompilerParams(vmem_limit_bytes=VMEM_LIMIT),
        cost_estimate=pl.CostEstimate(
            flops=COSTS.get(name, 500) * UNIT, bytes_accessed=moved, transcendentals=0
        ),
    )(scalars, *[a for a, _ in ins])


def after(value, *done):
    return lax.optimization_barrier((value,) + done)[0]


def rotated(x, left, right):
    h = ROT_DIM // 2
    to_left = jnp.concatenate([x[:, h:], x[:, :h]], axis=1)
    to_right = jnp.concatenate([x[:, -h:], x[:, :-h]], axis=1)
    return to_left * left + to_right * right


def gelu_parts(u):
    t = jnp.tanh(GELU_A * (u + GELU_B * u * u * u))
    return 0.5 * u * (1.0 + t), t


def layout(lengths, rows):
    slots = lengths.shape[0]
    upper = lax.iota(jnp.int32, slots)[:, None] <= lax.iota(jnp.int32, slots)[None, :]
    ends = jnp.sum(jnp.where(upper, lengths[:, None], 0), axis=0)
    ids = lax.iota(jnp.int32, rows)
    passed = ids[:, None] >= ends[None, :]
    begins = jnp.max(jnp.where(passed, ends[None, :], 0), axis=1)
    return begins, ids - begins, (ids < jnp.max(ends)).astype(F32)


def make(n_dp, n_t):
    reps = n_dp // GROUP
    block = GROUP * CORES

    def join(rep, member):
        return (rep // CORES * GROUP + member) * CORES + rep % CORES

    def parts_of(index):
        return index // block * CORES + index % CORES, (index // CORES) % GROUP

    def to_member(value, k):
        pairs = [(i, join(parts_of(i)[0], parts_of(i)[1] ^ k)) for i in range(n_dp)]
        return lax.ppermute(value, "dp", pairs)

    members = [[join(rep, z) for z in range(GROUP)] for rep in range(reps)]

    def among_members(value):
        return lax.all_to_all(value, "dp", 0, 0, axis_index_groups=members, tiled=True)

    def to_rep(value, s):
        pairs = [(i, join(parts_of(i)[0] ^ s, parts_of(i)[1])) for i in range(n_dp)]
        return lax.ppermute(value, "dp", pairs)

    def to_tensor(value, m):
        return lax.ppermute(value, "tensor", [(i, i ^ m) for i in range(n_t)])

    def per_device(
        hidden_in, seq_lengths, norm_gain, norm_bias, qkv_master, qkv_bias, out_master, out_bias,
        up_master, up_bias, down_master, down_bias, out_grad,
    ):
        rows, width = hidden_in.shape
        db = up_master.shape[0]
        fz = up_master.shape[1] // GROUP
        ez = qkv_master.shape[2] // GROUP
        heads = ez // HEAD_DIM
        fw = fz + 3 * ez
        fo = fz + ez
        part = rows // n_t
        me_dp, me_t = lax.axis_index("dp"), lax.axis_index("tensor")
        me_r, me_z = parts_of(me_dp)
        sc = jnp.stack([me_r, me_z, me_t]).astype(jnp.int32)
        all_rows = GROUP * rows
        gain, shift = norm_gain.reshape(1, width), norm_bias.reshape(1, width)

        def blk(sref, s, z):
            return join(sref[0] ^ s, z)

        done = {}

        def gate(name, value):
            waits = [a for n in GATES.get(name, ()) if n in done for a in done[n]]
            return after(value, *waits) if waits else value

        def reg(name, *arrays):
            done[name] = arrays

        def launch(name, body, steps, ins, outs, scratch=()):
            (first, spec), *rest = ins
            made = run(name, body, steps, sc, [(gate(name, first), spec)] + rest, outs, scratch)
            reg(name, made[0])
            return made

        def at(index, size):
            return pl.ds(pl.multiple_of(index * size, size), size)

        def swapped(i):
            return (i % 2) * 2 + i // 2

        def first_hop(mine):
            return to_member(mine, 2)

        def second_hop(mine, far):
            near = to_member(jnp.stack([mine, far]), 1)
            return jnp.concatenate([far[None], near], axis=0)

        paired = n_t == 4
        half = part // 2

        def exchange(b):
            return [to_tensor(b, m) for m in ((1, 2) if paired else range(1, n_t))]

        def forwarded(got):
            return [got[0][:, :half], got[1][:, half:]] if paired else []

        def pieces(got, rest, start=0):
            if not paired:
                return [(m, 0, part, start, a) for m, a in enumerate(got, 1)]
            (one, one_at), (two, two_at) = got
            (far, far_at), (near, near_at) = rest
            return [
                (1, 0, part, one_at, one),
                (2, 0, part, two_at, two),
                (3, 0, half, far_at, far),
                (3, half, half, near_at, near),
            ]

        def place(sref, step, own, first, others, metas, out):
            @pl.when(step == 0)
            def _():
                out[0] = own[...]

            @pl.when(step > 0)
            def _():
                out[0, at(sref[2], part), :] = first[0]
                for (m, off, n, lo, _), ref in zip(metas, others):
                    start = pl.multiple_of((sref[2] ^ m) * part + off, n)
                    out[0, pl.ds(start, n), :] = ref[0, lo : lo + n]

        def piece_specs(first, metas):
            prev = lambda i, s: jnp.maximum(i - 1, 0)
            return [(first, lead((1,) + first.shape[1:], prev))] + [
                (a, lead((1,) + a.shape[1:], prev)) for *_, a in metas
            ]

        member_block = lambda i, s: s[1] ^ swapped(i)

        def cast_in(s, up, qkv, out):
            for z in range(GROUP):
                out[z, :, :fz] = up[:, z * fz : (z + 1) * fz].astype(BF16)
                for j in range(3):
                    lo = fz + j * ez
                    out[z, :, lo : lo + ez] = qkv[j, :, z * ez : (z + 1) * ez].astype(BF16)

        def cast_out(s, down, wo, out):
            out[0, :fz] = down[...].astype(BF16)
            out[0, fz:] = wo[...].astype(BF16)

        def to_reps(stack):
            return [stack] + [to_rep(stack, s) for s in range(1, reps)]

        steps_in = 2
        in_block = [
            lead((db // steps_in, GROUP * fz)),
            pl.BlockSpec((3, db // steps_in, GROUP * ez), lambda i, s: (0, i, 0)),
            pl.BlockSpec((GROUP, db // steps_in, fw), lambda i, s: (0, i, 0)),
        ]
        out_block = [lead((fz, db)), lead((ez, db)), lead((1, fo, db))]
        sent_in = launch(
            CAST_IN, cast_in, steps_in,
            [(up_master, in_block[0]), (qkv_master, in_block[1])],
            [((GROUP, db, fw), BF16, in_block[2])],
        )[0]
        _, _, own_valid = layout(seq_lengths[0], rows)
        x_mine = lax.dynamic_slice_in_dim(hidden_in, me_t * part, part, 0)
        valid_mine = lax.dynamic_slice_in_dim(own_valid, me_t * part, part, 0)
        x_far = first_hop(x_mine)
        l_far = to_member(seq_lengths, 2)
        g_own = (out_grad.astype(F32) * own_valid[:, None]).astype(BF16)
        g_mine = lax.dynamic_slice_in_dim(g_own, me_t * part, part, 0)
        reg(X_FAR, x_far)
        reg(L_FAR, l_far)
        x_first = second_hop(gate(X_FIRST, x_mine), x_far)
        l_near = to_member(jnp.concatenate([seq_lengths, l_far]), 1)
        reg(X_FIRST, x_first)
        reg(L_NEAR, l_near)
        g_far = first_hop(gate(G_FAR, g_mine))
        reg(G_FAR, g_far)
        sent_out = launch(
            CAST_OUT, cast_out, GROUP,
            [(down_master, out_block[0]), (out_master, out_block[1])],
            [((GROUP, fo, db), BF16, out_block[2])],
        )[0]

        g_first = second_hop(g_mine, gate(G_FIRST, g_far))
        reg(G_FIRST, g_first)
        in_stack = among_members(gate(IN_STACK, sent_in))
        reg(IN_STACK, in_stack)
        x_near = exchange(gate(X_NEAR, x_first))
        reg(X_NEAR, *x_near)

        def table_body(s, own, far, near, cs, lf, rt, bg):
            i = pl.program_id(0)
            row = lax.broadcasted_iota(jnp.int32, (rows, ez), 0)
            begin, end = jnp.zeros((rows, ez), jnp.int32), jnp.int32(0)
            for j in range(seq_lengths.shape[1]):
                length = jnp.where(i == 0, own[0, j], jnp.where(i == 1, far[0, j], near[0, j]))
                length = jnp.where(i == 3, near[1, j], length)
                end = end + length
                begin = jnp.where(row >= end, end, begin)
            lane = lax.broadcasted_iota(jnp.int32, (rows, ez), 1) % HEAD_DIM
            halves = ROT_DIM // 2
            step = (lane % halves).astype(F32) * (-2.0 / ROT_DIM)
            rate = jnp.exp(step * math.log(10000.0))
            angle = jnp.where(lane < ROT_DIM, (row - begin).astype(F32) * rate, 0.0)
            sine = jnp.sin(angle)
            cs[0] = jnp.cos(angle)
            lf[0] = jnp.where(lane < halves, -sine, 0.0)
            rt[0] = jnp.where(lane >= halves, sine, 0.0)
            bg[0] = begin[:, 0:1]

        smem = pl.BlockSpec(memory_space=pltpu.SMEM)
        cosine, left, right, begins = launch(
            TABLES, table_body, GROUP,
            [(seq_lengths, smem), (l_far, smem), (l_near, smem)],
            [((GROUP, rows, ez), F32, lead((1, rows, ez), member_block))] * 3
            + [((GROUP, rows, 1), jnp.int32, lead((1, rows, 1), member_block))],
        )

        x_rest = [to_tensor(gate(X_REST, b), m) for b, m in zip(forwarded(x_near), (2, 1))]
        reg(X_REST, *x_rest)
        if paired:
            x_metas = pieces([(a, 0) for a in x_near], [(a, 0) for a in x_rest])
        else:
            x_metas = pieces(x_near, None)

        def norm_body(s, own, first, *rest):
            others = rest[: len(x_metas)]
            gn, bs, x_out, n_out, st_out = rest[len(x_metas) :]
            place(s, pl.program_id(0), own, first, others, x_metas, x_out)
            v = x_out[0].astype(F32)
            mean = jnp.mean(v, axis=1, keepdims=True)
            v = v - mean
            scale = lax.rsqrt(jnp.mean(v * v, axis=1, keepdims=True) + 1e-05)
            v = v * scale * gn[...] + bs[...]
            n_out[0] = v.astype(BF16)
            which = lax.broadcasted_iota(jnp.int32, (rows, 128), 1)
            st_out[0] = jnp.where(which == 0, mean, scale)

        x_all, normed, stats = launch(
            NORM, norm_body, GROUP,
            [(hidden_in, whole(hidden_in.shape))]
            + piece_specs(x_first, x_metas)
            + [(gain, whole(gain.shape)), (shift, whole(shift.shape))],
            [
                ((GROUP, rows, width), BF16, lead((1, rows, width), member_block)),
                ((GROUP, rows, width), BF16, lead((1, rows, width), member_block)),
                ((GROUP, rows, 128), F32, lead((1, rows, 128), member_block)),
            ],
        )

        g_near = [to_tensor(gate(G_NEAR, g_first), m) for m in range(1, n_t)]
        reg(G_NEAR, *g_near)
        out_stack = among_members(gate(OUT_STACK, sent_out))
        reg(OUT_STACK, out_stack)
        w_in = to_reps(gate(W_IN, in_stack))
        g_metas = [(m, 0, part, 0, a) for m, a in enumerate(g_near, 1)]

        def grad_rows_body(s, own, first, *rest):
            others, (g_out, sum_out) = rest[: len(g_metas)], rest[len(g_metas) :]
            place(s, pl.program_id(0), own, first, others, g_metas, g_out)
            sum_out[0] = jnp.sum(g_out[0].astype(F32), axis=0, keepdims=True)

        grads, row_sums = launch(
            GRAD_ROWS, grad_rows_body, GROUP,
            [(g_own, whole(g_own.shape))] + piece_specs(g_first, g_metas),
            [
                ((GROUP, rows, width), BF16, lead((1, rows, width), member_block)),
                ((GROUP, 1, width), F32, lead((1, 1, width), member_block)),
            ],
        )

        my_bias = jnp.concatenate(
            [
                lax.dynamic_slice_in_dim(up_bias, me_z * fz, fz, 0),
                lax.dynamic_slice_in_dim(qkv_bias, me_z * ez, ez, 1).reshape(-1),
            ]
        ).reshape(1, fw)
        n_w = reps

        def forward_body(s, x, cs, lf, rt, bg, bias, *rest):
            w, (branch, pre, qkv, probs, wide) = rest[:n_w], rest[n_w:]

            @pl.when(pl.program_id(0) == 0)
            def _():
                for rep in range(reps):
                    for k in range(GROUP):
                        wide[at(blk(s, rep, k), db), :] = w[rep][k]

            u = mm(x[0], wide[:, :fz]) + bias[:, :fz]
            pre[0] = u
            act = gelu_parts(u)[0]
            branch[0, :, :fz] = act.astype(BF16)
            j = mm(x[0], wide[:, fz:]) + bias[:, fz:]
            c, l, r = cs[0], lf[0], rt[0]
            q, k, v = j[:, :ez], j[:, ez : 2 * ez], j[:, 2 * ez :]
            q = (q * c + rotated(q, l, r)).astype(BF16)
            k = (k * c + rotated(k, l, r)).astype(BF16)
            v = v.astype(BF16)
            qkv[0, :, :ez] = q
            qkv[0, :, ez : 2 * ez] = k
            qkv[0, :, 2 * ez :] = v
            col = lax.broadcasted_iota(jnp.int32, (rows, rows), 1)
            row = lax.broadcasted_iota(jnp.int32, (rows, rows), 0)
            allowed = (col >= bg[0]) & (col <= row)
            for h in range(heads):
                lo, hi = h * HEAD_DIM, (h + 1) * HEAD_DIM
                sco = mm(q[:, lo:hi], k[:, lo:hi], 1, 1) * SCORE_SCALE
                sco = jnp.where(allowed, sco, -1e30)
                e = jnp.exp(sco - jnp.max(sco, axis=1, keepdims=True))
                p = e / jnp.sum(e, axis=1, keepdims=True)
                probs[0, h] = p
                ctx = mm(p.astype(BF16), v[:, lo:hi])
                branch[0, :, fz + lo : fz + hi] = ctx.astype(BF16)

        row_block = lambda n: lead((1, rows, n))
        branch, pre, qkv, probs = launch(
            FORWARD, forward_body, GROUP,
            [
                (normed, row_block(width)), (cosine, row_block(ez)), (left, row_block(ez)),
                (right, row_block(ez)), (begins, row_block(1)), (my_bias, whole(my_bias.shape)),
            ]
            + [(a, whole(a.shape)) for a in w_in],
            [
                ((GROUP, rows, fo), BF16, row_block(fo)),
                ((GROUP, rows, fz), F32, row_block(fz)),
                ((GROUP, rows, 3 * ez), BF16, row_block(3 * ez)),
                ((GROUP, heads, rows, rows), F32, lead((1, heads, rows, rows))),
            ],
            [pltpu.VMEM((width, fw), BF16)],
        )

        w_out = to_reps(gate(W_OUT, out_stack))
        def among(name, parts):
            got = [to_tensor(gate(name, parts[m]), m) for m in range(1, n_t)]
            reg(name, *got)
            return [parts[0]] + got

        def parted(sref, y, outs):
            for m in range(n_t):
                outs[m][0] = y[at(sref[2] ^ m, part), :].astype(BF16)

        part_outs = [((GROUP, part, width), BF16, lead((1, part, width)))] * n_t

        def out_body(s, br, *rest):
            w, outs, (y,) = rest[:n_w], rest[n_w:-1], rest[-1:]
            for rep in range(reps):
                for k in range(GROUP):
                    y[:, at(blk(s, rep, k), db)] = mm(br[0], w[rep][k])
            parted(s, y, outs)

        out_sums = launch(
            OUT_ROWS, out_body, GROUP,
            [(branch, row_block(fo))] + [(a, whole(a.shape)) for a in w_out],
            part_outs,
            [pltpu.VMEM((rows, width), F32)],
        )
        o_got = among(O_GOT, out_sums)

        def add_rows(name, parts, sizes):
            arrays = []
            for terms in parts:
                for a, _ in terms:
                    if not any(a is b for b in arrays):
                        arrays.append(a)
            where = [[([a is b for b in arrays].index(True), r) for a, r in terms] for terms in parts]

            def body(s, *refs):
                ins, outs = refs[: len(arrays)], refs[len(arrays) :]
                row = 0
                for n, out in zip(sizes, outs):
                    for r in range(n):
                        total = None
                        for a, at_row in where[row]:
                            v = ins[a][at_row : at_row + 1, :]
                            total = v if total is None else total + v
                        out[r : r + 1, : total.shape[1]] = total
                        row += 1

            return launch(
                name, body, 1, [(a, whole(a.shape)) for a in arrays],
                [((n, width), F32, whole((n, width))) for n in sizes],
            )

        def product(a, b):
            flat = lambda v: v.reshape(all_rows, v.shape[-1])
            return mm(flat(a[...]), flat(b[...]), 0, 0)

        def others_part(names, left_arr, left_spec, right_arr, right_spec, shape):
            got = []
            for rep in range(1, reps):
                def body(s, a, b, out):
                    out[0] = product(a, b).astype(BF16)

                sent = launch(
                    names[1], body, GROUP,
                    [(left_arr, left_spec(rep)), (right_arr, right_spec(rep))],
                    [((GROUP,) + shape, BF16, lead((1,) + shape))],
                )[0]
                got.append(to_rep(gate(names[2], sent), rep))
            return got

        def own_part(names, left_arr, left_spec, right_arr, right_spec, shape, got):
            def body(s, a, b, *refs):
                total = product(a, b)
                for ref in refs[:-1]:
                    total = total + ref[0].astype(F32)
                refs[-1][0] = total.astype(BF16)

            return launch(
                names[0], body, GROUP,
                [(left_arr, left_spec(0)), (right_arr, right_spec(0))]
                + [(a, lead((1,) + shape)) for a in got],
                [((GROUP,) + shape, BF16, lead((1,) + shape))],
            )[0]

        def columns(rep):
            return pl.BlockSpec((GROUP, rows, db), lambda i, s: (0, 0, blk(s, rep, i)))

        out_args = (
            (OUT_WEIGHT_GRAD, OUT_WEIGHT_GRAD_OTHER, OUT_WEIGHT_GRAD_REP), branch, lambda rep: whole(branch.shape), grads, columns, (fo, db)
        )
        out_parts = own_part(*out_args, others_part(*out_args))
        out_pieces = among_members(out_parts)
        reg(OUT_PIECES, out_pieces)

        def backward_body(s, g, pre, qkv, probs, cs, lf, rt, *rest):
            w, (wide_out, sum_out, w_all) = rest[:n_w], rest[n_w:]

            @pl.when(pl.program_id(0) == 0)
            def _():
                for rep in range(reps):
                    for k in range(GROUP):
                        w_all[:, at(blk(s, rep, k), db)] = w[rep][k]

            ga = mm(g[0], w_all[:fz], 1, 1)
            u = pre[0]
            t = gelu_parts(u)[1]
            slope = 0.5 * (1.0 + t) + 0.5 * u * (1.0 - t * t) * (
                GELU_A * (1.0 + 3.0 * GELU_B * u * u)
            )
            gp = (ga * slope).astype(BF16)
            wide_out[0, :, :fz] = gp
            sum_out[0, :, :fz] = jnp.sum(gp.astype(F32), axis=0, keepdims=True)
            gc = mm(g[0], w_all[fz:], 1, 1).astype(BF16)
            q, k, v = qkv[0, :, :ez], qkv[0, :, ez : 2 * ez], qkv[0, :, 2 * ez :]
            dq, dk, dv = [], [], []
            for h in range(heads):
                lo, hi = h * HEAD_DIM, (h + 1) * HEAD_DIM
                p, gch = probs[0, h], gc[:, lo:hi]
                dv.append(mm(p.astype(BF16), gch, 0, 0))
                dp = mm(gch, v[:, lo:hi], 1, 1)
                ds = (p * (dp - jnp.sum(p * dp, axis=1, keepdims=True))).astype(BF16)
                dq.append(mm(ds, k[:, lo:hi]) * SCORE_SCALE)
                dk.append(mm(ds, q[:, lo:hi], 0, 0) * SCORE_SCALE)
            c, l, r = cs[0], lf[0], rt[0]
            join_heads = lambda parts: parts[0] if heads == 1 else jnp.concatenate(parts, axis=1)
            dq, dk, dv = join_heads(dq), join_heads(dk), join_heads(dv)
            dq = dq * c - rotated(dq, l, r)
            dk = dk * c - rotated(dk, l, r)
            for j, d in enumerate((dq, dk, dv)):
                low = d.astype(BF16)
                lo = fz + j * ez
                wide_out[0, :, lo : lo + ez] = low
                sum_out[0, :, lo : lo + ez] = jnp.sum(low.astype(F32), axis=0, keepdims=True)

        wide, wide_sums = launch(
            BACKWARD, backward_body, GROUP,
            [
                (grads, row_block(width)), (pre, row_block(fz)), (qkv, row_block(3 * ez)),
                (probs, lead((1, heads, rows, rows))), (cosine, row_block(ez)),
                (left, row_block(ez)), (right, row_block(ez)),
            ]
            + [(a, whole(a.shape)) for a in w_out],
            [((GROUP, rows, fw), BF16, row_block(fw)), ((GROUP, 1, fw), F32, lead((1, 1, fw)))],
            [pltpu.VMEM((fo, width), BF16)],
        )

        def normed_grad_body(s, gw, x, st, *rest):
            w, outs, (sums, y) = rest[:n_w], rest[n_w:-2], rest[-2:]
            for rep in range(reps):
                for k in range(GROUP):
                    y[:, at(blk(s, rep, k), db)] = mm(gw[0], w[rep][k], 1, 1)
            parted(s, y, outs)
            v = y[...]
            hat = (x[0].astype(F32) - st[0, :, 0:1]) * st[0, :, 1:2]

            @pl.when(pl.program_id(0) == 0)
            def _():
                sums[...] = jnp.zeros(sums.shape, F32)

            sums[0:1] += jnp.sum(v * hat, axis=0, keepdims=True)
            sums[1:2] += jnp.sum(v, axis=0, keepdims=True)

        *gn_parts, gain_sums = launch(
            NORMED_GRAD, normed_grad_body, GROUP,
            [(wide, row_block(fw)), (x_all, row_block(width)), (stats, row_block(128))]
            + [(a, whole(a.shape)) for a in w_in],
            part_outs + [((2, width), F32, whole((2, width)))],
            [pltpu.VMEM((rows, width), F32)],
        )

        own_block = lambda i, s: s[1] ^ i

        two = (2, part, width)

        def add_tensor(name, near_name, got):
            def body(s, *refs):
                ins, outs = refs[:n_t], refs[n_t:]
                total = ins[0][0].astype(F32)
                for ref in ins[1:]:
                    total = total + ref[0].astype(F32)
                for k in range(GROUP):
                    @pl.when(pl.program_id(0) == k)
                    def _(k=k):
                        outs[k % 2][k // 2] = total.astype(outs[k % 2].dtype)

            keep, send = launch(
                name, body, GROUP,
                [(a, lead((1, part, width), own_block)) for a in got],
                [(two, F32, whole(two)), (two, BF16, whole(two))],
            )
            near = to_member(gate(near_name, send), 1)
            reg(near_name, near)
            return keep, near

        def add_near(name, far_name, keep, near):
            def body(s, keep, near, own, send):
                own[...] = keep[0] + near[0].astype(F32)
                send[...] = (keep[1] + near[1].astype(F32)).astype(BF16)

            own, send = launch(
                name, body, 1, [(keep, whole(two)), (near, whole(two))],
                [((part, width), F32, whole((part, width))), ((part, width), BF16, whole((part, width)))],
            )
            far = to_member(gate(far_name, send), 2)
            reg(far_name, far)
            return own, far

        mine_rows = lead((part, width), lambda i, s: s[2])

        def join_rows(name, mine, got):
            def body(s, first, *rest):
                for m, ref in enumerate((first,) + rest[:-1]):
                    rest[-1][at(s[2] ^ m, part), :] = ref[...]

            return launch(
                name, body, 1,
                [(mine, whole(mine.shape))] + [(a, whole(a.shape)) for a in got],
                [((rows, width), BF16, whole((rows, width)))],
            )[0]

        gn_got = among(GN_GOT, gn_parts)
        in_args = (
            (IN_WEIGHT_GRAD, IN_WEIGHT_GRAD_OTHER, IN_WEIGHT_GRAD_REP), normed, columns, wide, lambda rep: whole(wide.shape), (db, fw)
        )
        out_keep, out_near = add_tensor(OUT_ADD, OUT_ADD_NEAR, o_got)
        in_got = others_part(*in_args)
        in_parts = own_part(*in_args, in_got)
        in_pieces = among_members(in_parts)
        o_sums = add_near(OUT_ADD_PAIR, OUT_ADD_PAIR_FAR, out_keep, out_near)
        flat = [row_sums.reshape(GROUP, width), wide_sums.reshape(GROUP, fw)]
        order = ((0, 1), (2, 3))
        low = add_rows(SUMS_LOW, [[(flat[n], a), (flat[n], b)] for n in (0, 1) for a, b in order], (4,))[0]
        small = add_rows(
            SUMS, [[(gain_sums, 0)], [(gain_sums, 1)], [(low, 0), (low, 1)], [(low, 2), (low, 3)]], (4,)
        )[0]
        hop = 1
        while hop < reps:
            got = to_rep(gate(SMALL_REP, small), hop)
            small = add_rows(SUMS_REP, [[(small, r), (got, r)] for r in range(4)], (4,))[0]
            hop *= 2
        gains, bias_total, wide_sum = add_rows(SUMS_SPLIT, [[(small, r)] for r in range(4)], (2, 1, 1))
        bias_total = bias_total[0]
        gn_keep, gn_near = add_tensor(GN_ADD, GN_ADD_NEAR, gn_got)

        both_bias = (out_bias + down_bias).reshape(1, width)

        def hidden_out_body(s, *refs):
            sums, (x, ok, bias, out) = refs[:2], refs[2:]
            total = sums[0][...] + sums[1][...].astype(F32)
            out[...] = (x[...].astype(F32) + ok[...] * (total + bias[...])).astype(BF16)

        hidden_out_mine = launch(
            HIDDEN_OUT, hidden_out_body, 1,
            [(a, whole(a.shape)) for a in o_sums]
            + [(hidden_in, mine_rows), (valid_mine[:, None], whole((part, 1))), (both_bias, whole(both_bias.shape))],
            [((part, width), BF16, whole((part, width)))],
        )[0]
        hidden_out_got = among(HIDDEN_OUT_GOT, [hidden_out_mine] * n_t)[1:]

        for hop in range(1, n_t):
            if hop & (hop - 1) == 0:
                got = to_tensor(gate(SMALL_TENSOR, gains), hop)
                gains = add_rows(GAINS_TENSOR, [[(gains, r), (got, r)] for r in range(2)], (2,))[0]
        gn_sums = add_near(GN_ADD_PAIR, GN_ADD_PAIR_FAR, gn_keep, gn_near)
        sent = add_rows(GAINS_SENT, [[(gains, 0)], [(gains, 1)], [(wide_sum, 0)]], (3,))[0]
        hidden_out = join_rows(HIDDEN_OUT_ROWS, hidden_out_mine, hidden_out_got)
        def finish_out(s, piece, down, wo):
            down[...] = piece[0, :fz].astype(F32)
            wo[...] = piece[0, fz:].astype(F32)

        down_master_grad, out_master_grad = launch(
            FINISH_OUT, finish_out, GROUP,
            [(out_pieces, out_block[2])],
            [(down_master.shape, F32, out_block[0]), (out_master.shape, F32, out_block[1])],
        )
        def input_grad_body(s, *refs):
            sums, (x, g, gn, out) = refs[:2], refs[2:]
            total = sums[0][...] + sums[1][...].astype(F32)
            v = x[...].astype(F32)
            v = v - jnp.mean(v, axis=1, keepdims=True)
            scale = lax.rsqrt(jnp.mean(v * v, axis=1, keepdims=True) + 1e-05)
            hat = v * scale
            gy = total * gn[...]
            d = gy - jnp.mean(gy, axis=1, keepdims=True) - hat * jnp.mean(gy * hat, axis=1, keepdims=True)
            out[...] = (g[...].astype(F32) + d * scale).astype(BF16)

        input_grad_mine = launch(
            INPUT_GRAD, input_grad_body, 1,
            [(a, whole(a.shape)) for a in gn_sums]
            + [(hidden_in, mine_rows), (out_grad, mine_rows), (gain, whole(gain.shape))],
            [((part, width), BF16, whole((part, width)))],
        )[0]
        input_grad_got = among(INPUT_GRAD_GOT, [input_grad_mine] * n_t)[1:]

        got = to_member(gate(SMALL_FAR, sent), 2)
        sent = add_rows(
            GAINS_FAR, [[(sent, 0), (got, 0)], [(sent, 1), (got, 1)], [(sent, 2)], [(got, 2)]], (4,)
        )[0]
        got = to_member(sent, 1)
        def finish_in(s, piece, up, qkv):
            for z in range(GROUP):
                up[:, z * fz : (z + 1) * fz] = piece[z, :, :fz].astype(F32)
                for j in range(3):
                    lo = fz + j * ez
                    qkv[j, :, z * ez : (z + 1) * ez] = piece[z, :, lo : lo + ez].astype(F32)

        up_master_grad, qkv_master_grad = launch(
            FINISH_IN, finish_in, steps_in,
            [(in_pieces, in_block[2])],
            [(up_master.shape, F32, in_block[0]), (qkv_master.shape, F32, in_block[1])],
        )


        def bias_body(s, mine, got, gains, up, qkv, scr):
            gains[...] = mine[0:2, :] + got[0:2, :]
            for k, ref, row in ((0, mine, 2), (2, mine, 3), (1, got, 2), (3, got, 3)):
                scr[pl.ds(s[1] ^ k, 1), :] = ref[row : row + 1, :]
            for z in range(GROUP):
                up[z : z + 1, :] = scr[z : z + 1, :fz]
                for j in range(3):
                    lo = fz + j * ez
                    qkv[j : j + 1, z * ez : (z + 1) * ez] = scr[z : z + 1, lo : lo + ez]

        gains, up_bias_grad, qkv_bias_grad = launch(
            BIAS_GRADS, bias_body, 1, [(sent, whole(sent.shape)), (got, whole(got.shape))],
            [
                ((2, width), F32, whole((2, width))), ((GROUP, fz), F32, whole((GROUP, fz))),
                (qkv_bias.shape, F32, whole(qkv_bias.shape)),
            ],
            [pltpu.VMEM((GROUP, width), F32)],
        )
        up_bias_grad = up_bias_grad.reshape(up_bias.shape)
        input_grad = join_rows(INPUT_GRAD_ROWS, input_grad_mine, input_grad_got)
        return (
            hidden_out, input_grad, gains[0], gains[1], qkv_master_grad, qkv_bias_grad,
            out_master_grad, bias_total, up_master_grad, up_bias_grad, down_master_grad, bias_total,
        )

    return per_device


def solution(mesh):
    placed = (
        P("dp", None), P("dp", None), P(), P(), P(None, "dp", "tensor"), P(None, "tensor"),
        P("tensor", "dp"), P(), P("dp", "tensor"), P("tensor"), P("tensor", "dp"), P(), P("dp", None),
    )
    return jax.shard_map(
        make(mesh.shape["dp"], mesh.shape["tensor"]),
        mesh=mesh,
        in_specs=placed,
        out_specs=(
            P("dp", None), P("dp", None), P(), P(), P(None, "dp", "tensor"), P(None, "tensor"),
            P("tensor", "dp"), P(), P("dp", "tensor"), P("tensor"), P("tensor", "dp"), P(),
        ),
        check_vma=False,
    )
```

```python
import functools
import math

import jax
import jax.numpy as jnp
from jax import lax
from jax.experimental import pallas as pl
from jax.experimental.pallas import tpu as pltpu
from jax.sharding import PartitionSpec as P

HEAD_DIM = 64
ROT_DIM = 32
GROUP = 4
CORES = 2
BF16 = jnp.bfloat16
F32 = jnp.float32
GELU_A = math.sqrt(2.0 / math.pi)
GELU_B = 0.044715
SCORE_SCALE = 1.0 / math.sqrt(HEAD_DIM)
VMEM_LIMIT = 50 * 2**20
UNIT = 2**19
(
    CAST_IN, X_FAR, L_FAR, X_FIRST, L_NEAR, G_FAR, CAST_OUT, G_FIRST, IN_STACK, X_NEAR, TABLES,
    X_REST, NORM, G_NEAR, OUT_STACK, W_IN, GRAD_ROWS, FORWARD, W_OUT, OUT_ROWS, O_GOT,
    OUT_WEIGHT_GRAD, OUT_WEIGHT_GRAD_OTHER, OUT_WEIGHT_GRAD_REP, OUT_PIECES, BACKWARD,
    NORMED_GRAD, GN_GOT, IN_WEIGHT_GRAD, IN_WEIGHT_GRAD_OTHER, IN_WEIGHT_GRAD_REP, OUT_ADD,
    OUT_ADD_NEAR, OUT_ADD_PAIR, OUT_ADD_PAIR_FAR, SUMS_LOW, SUMS, SMALL_REP, SUMS_REP,
    SUMS_SPLIT, GN_ADD, GN_ADD_NEAR, HIDDEN_OUT, HIDDEN_OUT_GOT, SMALL_TENSOR, GAINS_TENSOR,
    GN_ADD_PAIR, GN_ADD_PAIR_FAR, GAINS_SENT, HIDDEN_OUT_ROWS, FINISH_OUT, INPUT_GRAD,
    INPUT_GRAD_GOT, SMALL_FAR, GAINS_FAR, FINISH_IN, BIAS_GRADS, INPUT_GRAD_ROWS,
) = range(58)
COSTS = {
    CAST_IN: 14080,
    CAST_OUT: 1518,
    TABLES: 1716,
    NORM: 28600,
    FORWARD: 1,
    GRAD_ROWS: 1936,
    OUT_ROWS: 5082,
    OUT_WEIGHT_GRAD: 3498,
    BACKWARD: 1,
    NORMED_GRAD: 7788,
    IN_WEIGHT_GRAD: 1364,
    OUT_ADD: 4510,
    GN_ADD: 7920,
    HIDDEN_OUT: 594,
    INPUT_GRAD: 726,
    HIDDEN_OUT_ROWS: 704,
    INPUT_GRAD_ROWS: 352,
    FINISH_OUT: 1650,
    FINISH_IN: 1716,
    BIAS_GRADS: 10560,
    GN_ADD_PAIR: 132,
    OUT_ADD_PAIR: 1,
    SUMS_SPLIT: 220,
    SUMS: 2200,
    SUMS_REP: 8800,
}
GATES = {
    IN_STACK: (X_FIRST, L_NEAR, G_FAR,),
    X_NEAR: (L_NEAR, G_FAR,),
    G_FIRST: (X_FIRST,),
    X_REST: (TABLES,),
    OUT_STACK: (G_FIRST, IN_STACK, X_NEAR,),
    W_IN: (G_FIRST, NORM,),
    G_NEAR: (IN_STACK, X_REST,),
    FORWARD: (OUT_STACK,),
    BACKWARD: (OUT_ROWS, OUT_WEIGHT_GRAD,),
    GN_GOT: (O_GOT, OUT_PIECES,),
    IN_WEIGHT_GRAD_OTHER: (NORMED_GRAD,),
    IN_WEIGHT_GRAD: (NORMED_GRAD, O_GOT,),
    OUT_ADD: (OUT_PIECES,),
    NORMED_GRAD: (O_GOT,),
    OUT_WEIGHT_GRAD: (OUT_ROWS,),
    SUMS_LOW: (GN_ADD,),
    GAINS_FAR: (GN_ADD_PAIR, INPUT_GRAD,),
    GRAD_ROWS: (OUT_STACK,),
    SMALL_REP: (IN_WEIGHT_GRAD,),
    GN_ADD_PAIR: (GAINS_TENSOR,),
    INPUT_GRAD_ROWS: (FINISH_IN,),
    INPUT_GRAD: (FINISH_OUT,),
    HIDDEN_OUT_GOT: (GN_ADD,),
    OUT_ADD_PAIR: (IN_WEIGHT_GRAD,),
    CAST_OUT: (X_FAR,),
    HIDDEN_OUT_ROWS: (GN_ADD_PAIR,),
    TABLES: (CAST_OUT,),
    OUT_ROWS: (G_NEAR,),
}


def mm(a, b, ca=1, cb=0):
    return lax.dot_general(a, b, (((ca,), (cb,)), ((), ())), preferred_element_type=F32)


def whole(shape):
    zeros = (0,) * len(shape)
    return pl.BlockSpec(tuple(shape), lambda i, sc: zeros)


def lead(shape, index=lambda i, sc: i):
    tail = (0,) * (len(shape) - 1)
    return pl.BlockSpec(tuple(shape), lambda i, sc: (index(i, sc),) + tail)


def run(name, body, steps, scalars, ins, outs, scratch=()):
    size = lambda shape, dtype: math.prod(shape) * jnp.dtype(dtype).itemsize
    moved = sum(size(a.shape, a.dtype) for a, _ in ins) + sum(size(s, d) for s, d, _ in outs)
    return pl.pallas_call(
        body,
        out_shape=[jax.ShapeDtypeStruct(s, d) for s, d, _ in outs],
        grid_spec=pltpu.PrefetchScalarGridSpec(
            num_scalar_prefetch=1,
            grid=(steps,),
            in_specs=[spec for _, spec in ins],
            out_specs=[spec for _, _, spec in outs],
            scratch_shapes=list(scratch),
        ),
        compiler_params=pltpu.CompilerParams(vmem_limit_bytes=VMEM_LIMIT),
        cost_estimate=pl.CostEstimate(
            flops=COSTS.get(name, 500) * UNIT, bytes_accessed=moved, transcendentals=0
        ),
    )(scalars, *[a for a, _ in ins])


def after(value, *done):
    return lax.optimization_barrier((value,) + done)[0]


def rotated(x, left, right):
    h = ROT_DIM // 2
    to_left = jnp.concatenate([x[:, h:], x[:, :h]], axis=1)
    to_right = jnp.concatenate([x[:, -h:], x[:, :-h]], axis=1)
    return to_left * left + to_right * right


def gelu_parts(u):
    t = jnp.tanh(GELU_A * (u + GELU_B * u * u * u))
    return 0.5 * u * (1.0 + t), t


def layout(lengths, rows):
    slots = lengths.shape[0]
    upper = lax.iota(jnp.int32, slots)[:, None] <= lax.iota(jnp.int32, slots)[None, :]
    ends = jnp.sum(jnp.where(upper, lengths[:, None], 0), axis=0)
    ids = lax.iota(jnp.int32, rows)
    passed = ids[:, None] >= ends[None, :]
    begins = jnp.max(jnp.where(passed, ends[None, :], 0), axis=1)
    return begins, ids - begins, (ids < jnp.max(ends)).astype(F32)


def make(n_dp, n_t):
    reps = n_dp // GROUP
    block = GROUP * CORES

    def join(rep, member):
        return (rep // CORES * GROUP + member) * CORES + rep % CORES

    def parts_of(index):
        return index // block * CORES + index % CORES, (index // CORES) % GROUP

    def to_member(value, k):
        pairs = [(i, join(parts_of(i)[0], parts_of(i)[1] ^ k)) for i in range(n_dp)]
        return lax.ppermute(value, "dp", pairs)

    members = [[join(rep, z) for z in range(GROUP)] for rep in range(reps)]

    def among_members(value):
        return lax.all_to_all(value, "dp", 0, 0, axis_index_groups=members, tiled=True)

    def to_rep(value, s):
        pairs = [(i, join(parts_of(i)[0] ^ s, parts_of(i)[1])) for i in range(n_dp)]
        return lax.ppermute(value, "dp", pairs)

    def to_tensor(value, m):
        return lax.ppermute(value, "tensor", [(i, i ^ m) for i in range(n_t)])

    def per_device(
        hidden_in, seq_lengths, norm_gain, norm_bias, qkv_master, qkv_bias, out_master, out_bias,
        up_master, up_bias, down_master, down_bias, out_grad,
    ):
        rows, width = hidden_in.shape
        db = up_master.shape[0]
        fz = up_master.shape[1] // GROUP
        ez = qkv_master.shape[2] // GROUP
        heads = ez // HEAD_DIM
        fw = fz + 3 * ez
        fo = fz + ez
        part = rows // n_t
        me_dp, me_t = lax.axis_index("dp"), lax.axis_index("tensor")
        me_r, me_z = parts_of(me_dp)
        sc = jnp.stack([me_r, me_z, me_t]).astype(jnp.int32)
        all_rows = GROUP * rows
        gain, shift = norm_gain.reshape(1, width), norm_bias.reshape(1, width)

        def blk(sref, s, z):
            return join(sref[0] ^ s, z)

        done = {}

        def gate(name, value):
            waits = [a for n in GATES.get(name, ()) if n in done for a in done[n]]
            return after(value, *waits) if waits else value

        def reg(name, *arrays):
            done[name] = arrays

        def launch(name, body, steps, ins, outs, scratch=()):
            (first, spec), *rest = ins
            made = run(name, body, steps, sc, [(gate(name, first), spec)] + rest, outs, scratch)
            reg(name, made[0])
            return made

        def at(index, size):
            return pl.ds(pl.multiple_of(index * size, size), size)

        def swapped(i):
            return (i % 2) * 2 + i // 2

        def first_hop(mine):
            return to_member(mine, 2)

        def second_hop(mine, far):
            near = to_member(jnp.stack([mine, far]), 1)
            return jnp.concatenate([far[None], near], axis=0)

        paired = n_t == 4
        half = part // 2

        def exchange(b):
            return [to_tensor(b, m) for m in ((1, 2) if paired else range(1, n_t))]

        def forwarded(got):
            return [got[0][:, :half], got[1][:, half:]] if paired else []

        def pieces(got, rest, start=0):
            if not paired:
                return [(m, 0, part, start, a) for m, a in enumerate(got, 1)]
            (one, one_at), (two, two_at) = got
            (far, far_at), (near, near_at) = rest
            return [
                (1, 0, part, one_at, one),
                (2, 0, part, two_at, two),
                (3, 0, half, far_at, far),
                (3, half, half, near_at, near),
            ]

        def place(sref, step, own, first, others, metas, out):
            @pl.when(step == 0)
            def _():
                out[0] = own[...]

            @pl.when(step > 0)
            def _():
                out[0, at(sref[2], part), :] = first[0]
                for (m, off, n, lo, _), ref in zip(metas, others):
                    start = pl.multiple_of((sref[2] ^ m) * part + off, n)
                    out[0, pl.ds(start, n), :] = ref[0, lo : lo + n]

        def piece_specs(first, metas):
            prev = lambda i, s: jnp.maximum(i - 1, 0)
            return [(first, lead((1,) + first.shape[1:], prev))] + [
                (a, lead((1,) + a.shape[1:], prev)) for *_, a in metas
            ]

        member_block = lambda i, s: s[1] ^ swapped(i)

        def cast_in(s, up, qkv, out):
            for z in range(GROUP):
                out[z, :, :fz] = up[:, z * fz : (z + 1) * fz].astype(BF16)
                for j in range(3):
                    lo = fz + j * ez
                    out[z, :, lo : lo + ez] = qkv[j, :, z * ez : (z + 1) * ez].astype(BF16)

        def cast_out(s, down, wo, out):
            out[0, :fz] = down[...].astype(BF16)
            out[0, fz:] = wo[...].astype(BF16)

        def to_reps(stack):
            return [stack] + [to_rep(stack, s) for s in range(1, reps)]

        steps_in = 2
        in_block = [
            lead((db // steps_in, GROUP * fz)),
            pl.BlockSpec((3, db // steps_in, GROUP * ez), lambda i, s: (0, i, 0)),
            pl.BlockSpec((GROUP, db // steps_in, fw), lambda i, s: (0, i, 0)),
        ]
        out_block = [lead((fz, db)), lead((ez, db)), lead((1, fo, db))]
        sent_in = launch(
            CAST_IN, cast_in, steps_in,
            [(up_master, in_block[0]), (qkv_master, in_block[1])],
            [((GROUP, db, fw), BF16, in_block[2])],
        )[0]
        _, _, own_valid = layout(seq_lengths[0], rows)
        x_mine = lax.dynamic_slice_in_dim(hidden_in, me_t * part, part, 0)
        valid_mine = lax.dynamic_slice_in_dim(own_valid, me_t * part, part, 0)
        x_far = first_hop(x_mine)
        l_far = to_member(seq_lengths, 2)
        g_own = (out_grad.astype(F32) * own_valid[:, None]).astype(BF16)
        g_mine = lax.dynamic_slice_in_dim(g_own, me_t * part, part, 0)
        reg(X_FAR, x_far)
        reg(L_FAR, l_far)
        x_first = second_hop(gate(X_FIRST, x_mine), x_far)
        l_near = to_member(jnp.concatenate([seq_lengths, l_far]), 1)
        reg(X_FIRST, x_first)
        reg(L_NEAR, l_near)
        g_far = first_hop(gate(G_FAR, g_mine))
        reg(G_FAR, g_far)
        sent_out = launch(
            CAST_OUT, cast_out, GROUP,
            [(down_master, out_block[0]), (out_master, out_block[1])],
            [((GROUP, fo, db), BF16, out_block[2])],
        )[0]

        g_first = second_hop(g_mine, gate(G_FIRST, g_far))
        reg(G_FIRST, g_first)
        in_stack = among_members(gate(IN_STACK, sent_in))
        reg(IN_STACK, in_stack)
        x_near = exchange(gate(X_NEAR, x_first))
        reg(X_NEAR, *x_near)

        def table_body(s, own, far, near, cs, lf, rt, bg):
            i = pl.program_id(0)
            row = lax.broadcasted_iota(jnp.int32, (rows, ez), 0)
            begin, end = jnp.zeros((rows, ez), jnp.int32), jnp.int32(0)
            for j in range(seq_lengths.shape[1]):
                length = jnp.where(i == 0, own[0, j], jnp.where(i == 1, far[0, j], near[0, j]))
                length = jnp.where(i == 3, near[1, j], length)
                end = end + length
                begin = jnp.where(row >= end, end, begin)
            lane = lax.broadcasted_iota(jnp.int32, (rows, ez), 1) % HEAD_DIM
            halves = ROT_DIM // 2
            step = (lane % halves).astype(F32) * (-2.0 / ROT_DIM)
            rate = jnp.exp(step * math.log(10000.0))
            angle = jnp.where(lane < ROT_DIM, (row - begin).astype(F32) * rate, 0.0)
            sine = jnp.sin(angle)
            cs[0] = jnp.cos(angle)
            lf[0] = jnp.where(lane < halves, -sine, 0.0)
            rt[0] = jnp.where(lane >= halves, sine, 0.0)
            bg[0] = begin[:, 0:1]

        smem = pl.BlockSpec(memory_space=pltpu.SMEM)
        cosine, left, right, begins = launch(
            TABLES, table_body, GROUP,
            [(seq_lengths, smem), (l_far, smem), (l_near, smem)],
            [((GROUP, rows, ez), F32, lead((1, rows, ez), member_block))] * 3
            + [((GROUP, rows, 1), jnp.int32, lead((1, rows, 1), member_block))],
        )

        x_rest = [to_tensor(gate(X_REST, b), m) for b, m in zip(forwarded(x_near), (2, 1))]
        reg(X_REST, *x_rest)
        if paired:
            x_metas = pieces([(a, 0) for a in x_near], [(a, 0) for a in x_rest])
        else:
            x_metas = pieces(x_near, None)

        def norm_body(s, own, first, *rest):
            others = rest[: len(x_metas)]
            gn, bs, x_out, n_out, st_out = rest[len(x_metas) :]
            place(s, pl.program_id(0), own, first, others, x_metas, x_out)
            v = x_out[0].astype(F32)
            mean = jnp.mean(v, axis=1, keepdims=True)
            v = v - mean
            scale = lax.rsqrt(jnp.mean(v * v, axis=1, keepdims=True) + 1e-05)
            v = v * scale * gn[...] + bs[...]
            n_out[0] = v.astype(BF16)
            which = lax.broadcasted_iota(jnp.int32, (rows, 128), 1)
            st_out[0] = jnp.where(which == 0, mean, scale)

        x_all, normed, stats = launch(
            NORM, norm_body, GROUP,
            [(hidden_in, whole(hidden_in.shape))]
            + piece_specs(x_first, x_metas)
            + [(gain, whole(gain.shape)), (shift, whole(shift.shape))],
            [
                ((GROUP, rows, width), BF16, lead((1, rows, width), member_block)),
                ((GROUP, rows, width), BF16, lead((1, rows, width), member_block)),
                ((GROUP, rows, 128), F32, lead((1, rows, 128), member_block)),
            ],
        )

        g_near = [to_tensor(gate(G_NEAR, g_first), m) for m in range(1, n_t)]
        reg(G_NEAR, *g_near)
        out_stack = among_members(gate(OUT_STACK, sent_out))
        reg(OUT_STACK, out_stack)
        w_in = to_reps(gate(W_IN, in_stack))
        g_metas = [(m, 0, part, 0, a) for m, a in enumerate(g_near, 1)]

        def grad_rows_body(s, own, first, *rest):
            others, (g_out, sum_out) = rest[: len(g_metas)], rest[len(g_metas) :]
            place(s, pl.program_id(0), own, first, others, g_metas, g_out)
            sum_out[0] = jnp.sum(g_out[0].astype(F32), axis=0, keepdims=True)

        grads, row_sums = launch(
            GRAD_ROWS, grad_rows_body, GROUP,
            [(g_own, whole(g_own.shape))] + piece_specs(g_first, g_metas),
            [
                ((GROUP, rows, width), BF16, lead((1, rows, width), member_block)),
                ((GROUP, 1, width), F32, lead((1, 1, width), member_block)),
            ],
        )

        my_bias = jnp.concatenate(
            [
                lax.dynamic_slice_in_dim(up_bias, me_z * fz, fz, 0),
                lax.dynamic_slice_in_dim(qkv_bias, me_z * ez, ez, 1).reshape(-1),
            ]
        ).reshape(1, fw)
        n_w = reps

        def forward_body(s, x, cs, lf, rt, bg, bias, *rest):
            w, (branch, pre, qkv, probs, wide) = rest[:n_w], rest[n_w:]

            @pl.when(pl.program_id(0) == 0)
            def _():
                for rep in range(reps):
                    for k in range(GROUP):
                        wide[at(blk(s, rep, k), db), :] = w[rep][k]

            u = mm(x[0], wide[:, :fz]) + bias[:, :fz]
            pre[0] = u
            act = gelu_parts(u)[0]
            branch[0, :, :fz] = act.astype(BF16)
            j = mm(x[0], wide[:, fz:]) + bias[:, fz:]
            c, l, r = cs[0], lf[0], rt[0]
            q, k, v = j[:, :ez], j[:, ez : 2 * ez], j[:, 2 * ez :]
            q = (q * c + rotated(q, l, r)).astype(BF16)
            k = (k * c + rotated(k, l, r)).astype(BF16)
            v = v.astype(BF16)
            qkv[0, :, :ez] = q
            qkv[0, :, ez : 2 * ez] = k
            qkv[0, :, 2 * ez :] = v
            col = lax.broadcasted_iota(jnp.int32, (rows, rows), 1)
            row = lax.broadcasted_iota(jnp.int32, (rows, rows), 0)
            allowed = (col >= bg[0]) & (col <= row)
            for h in range(heads):
                lo, hi = h * HEAD_DIM, (h + 1) * HEAD_DIM
                sco = mm(q[:, lo:hi], k[:, lo:hi], 1, 1) * SCORE_SCALE
                sco = jnp.where(allowed, sco, -1e30)
                e = jnp.exp(sco - jnp.max(sco, axis=1, keepdims=True))
                p = e / jnp.sum(e, axis=1, keepdims=True)
                probs[0, h] = p
                ctx = mm(p.astype(BF16), v[:, lo:hi])
                branch[0, :, fz + lo : fz + hi] = ctx.astype(BF16)

        row_block = lambda n: lead((1, rows, n))
        branch, pre, qkv, probs = launch(
            FORWARD, forward_body, GROUP,
            [
                (normed, row_block(width)), (cosine, row_block(ez)), (left, row_block(ez)),
                (right, row_block(ez)), (begins, row_block(1)), (my_bias, whole(my_bias.shape)),
            ]
            + [(a, whole(a.shape)) for a in w_in],
            [
                ((GROUP, rows, fo), BF16, row_block(fo)),
                ((GROUP, rows, fz), F32, row_block(fz)),
                ((GROUP, rows, 3 * ez), BF16, row_block(3 * ez)),
                ((GROUP, heads, rows, rows), F32, lead((1, heads, rows, rows))),
            ],
            [pltpu.VMEM((width, fw), BF16)],
        )

        w_out = to_reps(gate(W_OUT, out_stack))
        def among(name, parts):
            got = [to_tensor(gate(name, parts[m]), m) for m in range(1, n_t)]
            reg(name, *got)
            return [parts[0]] + got

        def parted(sref, y, outs):
            for m in range(n_t):
                outs[m][0] = y[at(sref[2] ^ m, part), :].astype(BF16)

        part_outs = [((GROUP, part, width), BF16, lead((1, part, width)))] * n_t

        def out_body(s, br, *rest):
            w, outs, (y,) = rest[:n_w], rest[n_w:-1], rest[-1:]
            for rep in range(reps):
                for k in range(GROUP):
                    y[:, at(blk(s, rep, k), db)] = mm(br[0], w[rep][k])
            parted(s, y, outs)

        out_sums = launch(
            OUT_ROWS, out_body, GROUP,
            [(branch, row_block(fo))] + [(a, whole(a.shape)) for a in w_out],
            part_outs,
            [pltpu.VMEM((rows, width), F32)],
        )
        o_got = among(O_GOT, out_sums)

        def add_rows(name, parts, sizes):
            arrays = []
            for terms in parts:
                for a, _ in terms:
                    if not any(a is b for b in arrays):
                        arrays.append(a)
            where = [[([a is b for b in arrays].index(True), r) for a, r in terms] for terms in parts]

            def body(s, *refs):
                ins, outs = refs[: len(arrays)], refs[len(arrays) :]
                row = 0
                for n, out in zip(sizes, outs):
                    for r in range(n):
                        total = None
                        for a, at_row in where[row]:
                            v = ins[a][at_row : at_row + 1, :]
                            total = v if total is None else total + v
                        out[r : r + 1, : total.shape[1]] = total
                        row += 1

            return launch(
                name, body, 1, [(a, whole(a.shape)) for a in arrays],
                [((n, width), F32, whole((n, width))) for n in sizes],
            )

        def product(a, b):
            flat = lambda v: v.reshape(all_rows, v.shape[-1])
            return mm(flat(a[...]), flat(b[...]), 0, 0)

        def others_part(names, left_arr, left_spec, right_arr, right_spec, shape):
            got = []
            for rep in range(1, reps):
                def body(s, a, b, out):
                    out[0] = product(a, b).astype(BF16)

                sent = launch(
                    names[1], body, GROUP,
                    [(left_arr, left_spec(rep)), (right_arr, right_spec(rep))],
                    [((GROUP,) + shape, BF16, lead((1,) + shape))],
                )[0]
                got.append(to_rep(gate(names[2], sent), rep))
            return got

        def own_part(names, left_arr, left_spec, right_arr, right_spec, shape, got):
            def body(s, a, b, *refs):
                total = product(a, b)
                for ref in refs[:-1]:
                    total = total + ref[0].astype(F32)
                refs[-1][0] = total.astype(BF16)

            return launch(
                names[0], body, GROUP,
                [(left_arr, left_spec(0)), (right_arr, right_spec(0))]
                + [(a, lead((1,) + shape)) for a in got],
                [((GROUP,) + shape, BF16, lead((1,) + shape))],
            )[0]

        def columns(rep):
            return pl.BlockSpec((GROUP, rows, db), lambda i, s: (0, 0, blk(s, rep, i)))

        out_args = (
            (OUT_WEIGHT_GRAD, OUT_WEIGHT_GRAD_OTHER, OUT_WEIGHT_GRAD_REP), branch, lambda rep: whole(branch.shape), grads, columns, (fo, db)
        )
        out_parts = own_part(*out_args, others_part(*out_args))
        out_pieces = among_members(out_parts)
        reg(OUT_PIECES, out_pieces)

        def backward_body(s, g, pre, qkv, probs, cs, lf, rt, *rest):
            w, (wide_out, sum_out, w_all) = rest[:n_w], rest[n_w:]

            @pl.when(pl.program_id(0) == 0)
            def _():
                for rep in range(reps):
                    for k in range(GROUP):
                        w_all[:, at(blk(s, rep, k), db)] = w[rep][k]

            ga = mm(g[0], w_all[:fz], 1, 1)
            u = pre[0]
            t = gelu_parts(u)[1]
            slope = 0.5 * (1.0 + t) + 0.5 * u * (1.0 - t * t) * (
                GELU_A * (1.0 + 3.0 * GELU_B * u * u)
            )
            gp = (ga * slope).astype(BF16)
            wide_out[0, :, :fz] = gp
            sum_out[0, :, :fz] = jnp.sum(gp.astype(F32), axis=0, keepdims=True)
            gc = mm(g[0], w_all[fz:], 1, 1).astype(BF16)
            q, k, v = qkv[0, :, :ez], qkv[0, :, ez : 2 * ez], qkv[0, :, 2 * ez :]
            dq, dk, dv = [], [], []
            for h in range(heads):
                lo, hi = h * HEAD_DIM, (h + 1) * HEAD_DIM
                p, gch = probs[0, h], gc[:, lo:hi]
                dv.append(mm(p.astype(BF16), gch, 0, 0))
                dp = mm(gch, v[:, lo:hi], 1, 1)
                ds = (p * (dp - jnp.sum(p * dp, axis=1, keepdims=True))).astype(BF16)
                dq.append(mm(ds, k[:, lo:hi]) * SCORE_SCALE)
                dk.append(mm(ds, q[:, lo:hi], 0, 0) * SCORE_SCALE)
            c, l, r = cs[0], lf[0], rt[0]
            join_heads = lambda parts: parts[0] if heads == 1 else jnp.concatenate(parts, axis=1)
            dq, dk, dv = join_heads(dq), join_heads(dk), join_heads(dv)
            dq = dq * c - rotated(dq, l, r)
            dk = dk * c - rotated(dk, l, r)
            for j, d in enumerate((dq, dk, dv)):
                low = d.astype(BF16)
                lo = fz + j * ez
                wide_out[0, :, lo : lo + ez] = low
                sum_out[0, :, lo : lo + ez] = jnp.sum(low.astype(F32), axis=0, keepdims=True)

        wide, wide_sums = launch(
            BACKWARD, backward_body, GROUP,
            [
                (grads, row_block(width)), (pre, row_block(fz)), (qkv, row_block(3 * ez)),
                (probs, lead((1, heads, rows, rows))), (cosine, row_block(ez)),
                (left, row_block(ez)), (right, row_block(ez)),
            ]
            + [(a, whole(a.shape)) for a in w_out],
            [((GROUP, rows, fw), BF16, row_block(fw)), ((GROUP, 1, fw), F32, lead((1, 1, fw)))],
            [pltpu.VMEM((fo, width), BF16)],
        )

        def normed_grad_body(s, gw, x, st, *rest):
            w, outs, (sums, y) = rest[:n_w], rest[n_w:-2], rest[-2:]
            for rep in range(reps):
                for k in range(GROUP):
                    y[:, at(blk(s, rep, k), db)] = mm(gw[0], w[rep][k], 1, 1)
            parted(s, y, outs)
            v = y[...]
            hat = (x[0].astype(F32) - st[0, :, 0:1]) * st[0, :, 1:2]

            @pl.when(pl.program_id(0) == 0)
            def _():
                sums[...] = jnp.zeros(sums.shape, F32)

            sums[0:1] += jnp.sum(v * hat, axis=0, keepdims=True)
            sums[1:2] += jnp.sum(v, axis=0, keepdims=True)

        *gn_parts, gain_sums = launch(
            NORMED_GRAD, normed_grad_body, GROUP,
            [(wide, row_block(fw)), (x_all, row_block(width)), (stats, row_block(128))]
            + [(a, whole(a.shape)) for a in w_in],
            part_outs + [((2, width), F32, whole((2, width)))],
            [pltpu.VMEM((rows, width), F32)],
        )

        own_block = lambda i, s: s[1] ^ i

        two = (2, part, width)

        def add_tensor(name, near_name, got):
            def body(s, *refs):
                ins, outs = refs[:n_t], refs[n_t:]
                total = ins[0][0].astype(F32)
                for ref in ins[1:]:
                    total = total + ref[0].astype(F32)
                for k in range(GROUP):
                    @pl.when(pl.program_id(0) == k)
                    def _(k=k):
                        outs[k % 2][k // 2] = total.astype(outs[k % 2].dtype)

            keep, send = launch(
                name, body, GROUP,
                [(a, lead((1, part, width), own_block)) for a in got],
                [(two, F32, whole(two)), (two, BF16, whole(two))],
            )
            near = to_member(gate(near_name, send), 1)
            reg(near_name, near)
            return keep, near

        def add_near(name, far_name, keep, near):
            def body(s, keep, near, own, send):
                own[...] = keep[0] + near[0].astype(F32)
                send[...] = (keep[1] + near[1].astype(F32)).astype(BF16)

            own, send = launch(
                name, body, 1, [(keep, whole(two)), (near, whole(two))],
                [((part, width), F32, whole((part, width))), ((part, width), BF16, whole((part, width)))],
            )
            far = to_member(gate(far_name, send), 2)
            reg(far_name, far)
            return own, far

        mine_rows = lead((part, width), lambda i, s: s[2])

        def join_rows(name, mine, got):
            def body(s, first, *rest):
                for m, ref in enumerate((first,) + rest[:-1]):
                    rest[-1][at(s[2] ^ m, part), :] = ref[...]

            return launch(
                name, body, 1,
                [(mine, whole(mine.shape))] + [(a, whole(a.shape)) for a in got],
                [((rows, width), BF16, whole((rows, width)))],
            )[0]

        gn_got = among(GN_GOT, gn_parts)
        in_args = (
            (IN_WEIGHT_GRAD, IN_WEIGHT_GRAD_OTHER, IN_WEIGHT_GRAD_REP), normed, columns, wide, lambda rep: whole(wide.shape), (db, fw)
        )
        out_keep, out_near = add_tensor(OUT_ADD, OUT_ADD_NEAR, o_got)
        in_got = others_part(*in_args)
        in_parts = own_part(*in_args, in_got)
        in_pieces = among_members(in_parts)
        o_sums = add_near(OUT_ADD_PAIR, OUT_ADD_PAIR_FAR, out_keep, out_near)
        flat = [row_sums.reshape(GROUP, width), wide_sums.reshape(GROUP, fw)]
        order = ((0, 1), (2, 3))
        low = add_rows(SUMS_LOW, [[(flat[n], a), (flat[n], b)] for n in (0, 1) for a, b in order], (4,))[0]
        small = add_rows(
            SUMS, [[(gain_sums, 0)], [(gain_sums, 1)], [(low, 0), (low, 1)], [(low, 2), (low, 3)]], (4,)
        )[0]
        hop = 1
        while hop < reps:
            got = to_rep(gate(SMALL_REP, small), hop)
            small = add_rows(SUMS_REP, [[(small, r), (got, r)] for r in range(4)], (4,))[0]
            hop *= 2
        gains, bias_total, wide_sum = add_rows(SUMS_SPLIT, [[(small, r)] for r in range(4)], (2, 1, 1))
        bias_total = bias_total[0]
        gn_keep, gn_near = add_tensor(GN_ADD, GN_ADD_NEAR, gn_got)

        both_bias = (out_bias + down_bias).reshape(1, width)

        def hidden_out_body(s, *refs):
            sums, (x, ok, bias, out) = refs[:2], refs[2:]
            total = sums[0][...] + sums[1][...].astype(F32)
            out[...] = (x[...].astype(F32) + ok[...] * (total + bias[...])).astype(BF16)

        hidden_out_mine = launch(
            HIDDEN_OUT, hidden_out_body, 1,
            [(a, whole(a.shape)) for a in o_sums]
            + [(hidden_in, mine_rows), (valid_mine[:, None], whole((part, 1))), (both_bias, whole(both_bias.shape))],
            [((part, width), BF16, whole((part, width)))],
        )[0]
        hidden_out_got = among(HIDDEN_OUT_GOT, [hidden_out_mine] * n_t)[1:]

        for hop in range(1, n_t):
            if hop & (hop - 1) == 0:
                got = to_tensor(gate(SMALL_TENSOR, gains), hop)
                gains = add_rows(GAINS_TENSOR, [[(gains, r), (got, r)] for r in range(2)], (2,))[0]
        gn_sums = add_near(GN_ADD_PAIR, GN_ADD_PAIR_FAR, gn_keep, gn_near)
        sent = add_rows(GAINS_SENT, [[(gains, 0)], [(gains, 1)], [(wide_sum, 0)]], (3,))[0]
        hidden_out = join_rows(HIDDEN_OUT_ROWS, hidden_out_mine, hidden_out_got)
        def finish_out(s, piece, down, wo):
            down[...] = piece[0, :fz].astype(F32)
            wo[...] = piece[0, fz:].astype(F32)

        down_master_grad, out_master_grad = launch(
            FINISH_OUT, finish_out, GROUP,
            [(out_pieces, out_block[2])],
            [(down_master.shape, F32, out_block[0]), (out_master.shape, F32, out_block[1])],
        )
        def input_grad_body(s, *refs):
            sums, (x, g, gn, out) = refs[:2], refs[2:]
            total = sums[0][...] + sums[1][...].astype(F32)
            v = x[...].astype(F32)
            v = v - jnp.mean(v, axis=1, keepdims=True)
            scale = lax.rsqrt(jnp.mean(v * v, axis=1, keepdims=True) + 1e-05)
            hat = v * scale
            gy = total * gn[...]
            d = gy - jnp.mean(gy, axis=1, keepdims=True) - hat * jnp.mean(gy * hat, axis=1, keepdims=True)
            out[...] = (g[...].astype(F32) + d * scale).astype(BF16)

        input_grad_mine = launch(
            INPUT_GRAD, input_grad_body, 1,
            [(a, whole(a.shape)) for a in gn_sums]
            + [(hidden_in, mine_rows), (out_grad, mine_rows), (gain, whole(gain.shape))],
            [((part, width), BF16, whole((part, width)))],
        )[0]
        input_grad_got = among(INPUT_GRAD_GOT, [input_grad_mine] * n_t)[1:]

        got = to_member(gate(SMALL_FAR, sent), 2)
        sent = add_rows(
            GAINS_FAR, [[(sent, 0), (got, 0)], [(sent, 1), (got, 1)], [(sent, 2)], [(got, 2)]], (4,)
        )[0]
        got = to_member(sent, 1)
        def finish_in(s, piece, up, qkv):
            for z in range(GROUP):
                up[:, z * fz : (z + 1) * fz] = piece[z, :, :fz].astype(F32)
                for j in range(3):
                    lo = fz + j * ez
                    qkv[j, :, z * ez : (z + 1) * ez] = piece[z, :, lo : lo + ez].astype(F32)

        up_master_grad, qkv_master_grad = launch(
            FINISH_IN, finish_in, steps_in,
            [(in_pieces, in_block[2])],
            [(up_master.shape, F32, in_block[0]), (qkv_master.shape, F32, in_block[1])],
        )


        def bias_body(s, mine, got, gains, up, qkv, scr):
            gains[...] = mine[0:2, :] + got[0:2, :]
            for k, ref, row in ((0, mine, 2), (2, mine, 3), (1, got, 2), (3, got, 3)):
                scr[pl.ds(s[1] ^ k, 1), :] = ref[row : row + 1, :]
            for z in range(GROUP):
                up[z : z + 1, :] = scr[z : z + 1, :fz]
                for j in range(3):
                    lo = fz + j * ez
                    qkv[j : j + 1, z * ez : (z + 1) * ez] = scr[z : z + 1, lo : lo + ez]

        gains, up_bias_grad, qkv_bias_grad = launch(
            BIAS_GRADS, bias_body, 1, [(sent, whole(sent.shape)), (got, whole(got.shape))],
            [
                ((2, width), F32, whole((2, width))), ((GROUP, fz), F32, whole((GROUP, fz))),
                (qkv_bias.shape, F32, whole(qkv_bias.shape)),
            ],
            [pltpu.VMEM((GROUP, width), F32)],
        )
        up_bias_grad = up_bias_grad.reshape(up_bias.shape)
        input_grad = join_rows(INPUT_GRAD_ROWS, input_grad_mine, input_grad_got)
        return (
            hidden_out, input_grad, gains[0], gains[1], qkv_master_grad, qkv_bias_grad,
            out_master_grad, bias_total, up_master_grad, up_bias_grad, down_master_grad, bias_total,
        )

    return per_device


def solution(mesh):
    placed = (
        P("dp", None), P("dp", None), P(), P(), P(None, "dp", "tensor"), P(None, "tensor"),
        P("tensor", "dp"), P(), P("dp", "tensor"), P("tensor"), P("tensor", "dp"), P(), P("dp", None),
    )
    return jax.shard_map(
        make(mesh.shape["dp"], mesh.shape["tensor"]),
        mesh=mesh,
        in_specs=placed,
        out_specs=(
            P("dp", None), P("dp", None), P(), P(), P(None, "dp", "tensor"), P(None, "tensor"),
            P("tensor", "dp"), P(), P("dp", "tensor"), P("tensor"), P("tensor", "dp"), P(),
        ),
        check_vma=False,
    )
```

```python
import functools
import math

import jax
import jax.numpy as jnp
from jax import lax
from jax.experimental import pallas as pl
from jax.experimental.pallas import tpu as pltpu
from jax.sharding import PartitionSpec as P

HEAD_DIM = 64
ROT_DIM = 32
GROUP = 4
CORES = 2
BF16 = jnp.bfloat16
F32 = jnp.float32
GELU_A = math.sqrt(2.0 / math.pi)
GELU_B = 0.044715
SCORE_SCALE = 1.0 / math.sqrt(HEAD_DIM)
VMEM_LIMIT = 50 * 2**20
UNIT = 2**19
(
    CAST_IN, X_FAR, L_FAR, X_FIRST, L_NEAR, G_FAR, CAST_OUT, G_FIRST, IN_STACK, X_NEAR, TABLES,
    X_REST, NORM, G_NEAR, OUT_STACK, W_IN, GRAD_ROWS, FORWARD, W_OUT, OUT_ROWS, O_GOT,
    OUT_WEIGHT_GRAD, OUT_WEIGHT_GRAD_OTHER, OUT_WEIGHT_GRAD_REP, OUT_PIECES, BACKWARD,
    IN_WEIGHT_GRAD, IN_WEIGHT_GRAD_OTHER, IN_WEIGHT_GRAD_REP, NORMED_GRAD, GN_GOT, OUT_ADD,
    OUT_ADD_NEAR, OUT_ADD_PAIR, OUT_ADD_PAIR_FAR, SUMS_LOW, SUMS, SMALL_REP, SUMS_REP,
    SUMS_SPLIT, GN_ADD, GN_ADD_NEAR, HIDDEN_OUT, HIDDEN_OUT_GOT, SMALL_TENSOR, GAINS_TENSOR,
    GN_ADD_PAIR, GN_ADD_PAIR_FAR, GAINS_SENT, HIDDEN_OUT_ROWS, FINISH_OUT, INPUT_GRAD,
    INPUT_GRAD_GOT, SMALL_FAR, GAINS_FAR, FINISH_IN, BIAS_GRADS, INPUT_GRAD_ROWS,
) = range(58)
COSTS = {
    CAST_IN: 14080,
    CAST_OUT: 1518,
    TABLES: 1716,
    NORM: 715,
    FORWARD: 1,
    GRAD_ROWS: 1936,
    OUT_ROWS: 5082,
    OUT_WEIGHT_GRAD: 3498,
    BACKWARD: 1,
    NORMED_GRAD: 5192,
    IN_WEIGHT_GRAD: 1364,
    OUT_ADD: 4510,
    GN_ADD: 7920,
    HIDDEN_OUT: 594,
    INPUT_GRAD: 726,
    HIDDEN_OUT_ROWS: 704,
    INPUT_GRAD_ROWS: 352,
    FINISH_OUT: 1650,
    FINISH_IN: 1716,
    BIAS_GRADS: 10560,
    GN_ADD_PAIR: 132,
    OUT_ADD_PAIR: 528,
    SUMS_SPLIT: 220,
    SUMS: 2200,
    SUMS_REP: 8800,
}
GATES = {
    IN_STACK: (X_FIRST, L_NEAR, G_FAR,),
    G_FIRST: (X_FIRST,),
    X_REST: (TABLES,),
    OUT_STACK: (G_FIRST, IN_STACK, X_NEAR,),
    W_IN: (G_FIRST, NORM,),
    G_NEAR: (IN_STACK, X_REST,),
    FORWARD: (OUT_STACK,),
    BACKWARD: (OUT_ROWS, OUT_WEIGHT_GRAD,),
    GN_GOT: (O_GOT,),
    IN_WEIGHT_GRAD_OTHER: (BACKWARD,),
    IN_WEIGHT_GRAD: (NORMED_GRAD,),
    OUT_ADD: (NORMED_GRAD, OUT_PIECES,),
    NORMED_GRAD: (IN_WEIGHT_GRAD_OTHER, OUT_PIECES,),
    OUT_WEIGHT_GRAD: (OUT_ROWS,),
    SUMS_LOW: (GN_ADD,),
    GAINS_FAR: (GN_ADD_PAIR, INPUT_GRAD,),
    GRAD_ROWS: (OUT_STACK,),
    SMALL_REP: (IN_WEIGHT_GRAD,),
    GN_ADD_PAIR: (GAINS_TENSOR,),
    INPUT_GRAD_ROWS: (FINISH_IN,),
    INPUT_GRAD: (FINISH_OUT,),
    HIDDEN_OUT_GOT: (GN_ADD,),
    OUT_ADD_PAIR: (IN_WEIGHT_GRAD,),
    CAST_OUT: (X_FAR,),
    HIDDEN_OUT_ROWS: (GN_ADD_PAIR,),
    TABLES: (CAST_OUT,),
    OUT_ROWS: (G_NEAR,),
    NORM: (G_FIRST,),
    FINISH_IN: (GN_ADD_PAIR,),
}


def mm(a, b, ca=1, cb=0):
    return lax.dot_general(a, b, (((ca,), (cb,)), ((), ())), preferred_element_type=F32)


def whole(shape):
    zeros = (0,) * len(shape)
    return pl.BlockSpec(tuple(shape), lambda i, sc: zeros)


def lead(shape, index=lambda i, sc: i):
    tail = (0,) * (len(shape) - 1)
    return pl.BlockSpec(tuple(shape), lambda i, sc: (index(i, sc),) + tail)


def run(name, body, steps, scalars, ins, outs, scratch=()):
    size = lambda shape, dtype: math.prod(shape) * jnp.dtype(dtype).itemsize
    moved = sum(size(a.shape, a.dtype) for a, _ in ins) + sum(size(s, d) for s, d, _ in outs)
    return pl.pallas_call(
        body,
        out_shape=[jax.ShapeDtypeStruct(s, d) for s, d, _ in outs],
        grid_spec=pltpu.PrefetchScalarGridSpec(
            num_scalar_prefetch=1,
            grid=(steps,),
            in_specs=[spec for _, spec in ins],
            out_specs=[spec for _, _, spec in outs],
            scratch_shapes=list(scratch),
        ),
        compiler_params=pltpu.CompilerParams(vmem_limit_bytes=VMEM_LIMIT),
        cost_estimate=pl.CostEstimate(
            flops=COSTS.get(name, 500) * UNIT, bytes_accessed=moved, transcendentals=0
        ),
    )(scalars, *[a for a, _ in ins])


def after(value, *done):
    return lax.optimization_barrier((value,) + done)[0]


def rotated(x, left, right):
    h = ROT_DIM // 2
    to_left = jnp.concatenate([x[:, h:], x[:, :h]], axis=1)
    to_right = jnp.concatenate([x[:, -h:], x[:, :-h]], axis=1)
    return to_left * left + to_right * right


def gelu_parts(u):
    t = jnp.tanh(GELU_A * (u + GELU_B * u * u * u))
    return 0.5 * u * (1.0 + t), t


def layout(lengths, rows):
    slots = lengths.shape[0]
    upper = lax.iota(jnp.int32, slots)[:, None] <= lax.iota(jnp.int32, slots)[None, :]
    ends = jnp.sum(jnp.where(upper, lengths[:, None], 0), axis=0)
    ids = lax.iota(jnp.int32, rows)
    passed = ids[:, None] >= ends[None, :]
    begins = jnp.max(jnp.where(passed, ends[None, :], 0), axis=1)
    return begins, ids - begins, (ids < jnp.max(ends)).astype(F32)


def make(n_dp, n_t):
    reps = n_dp // GROUP
    block = GROUP * CORES

    def join(rep, member):
        return (rep // CORES * GROUP + member) * CORES + rep % CORES

    def parts_of(index):
        return index // block * CORES + index % CORES, (index // CORES) % GROUP

    def to_member(value, k):
        pairs = [(i, join(parts_of(i)[0], parts_of(i)[1] ^ k)) for i in range(n_dp)]
        return lax.ppermute(value, "dp", pairs)

    members = [[join(rep, z) for z in range(GROUP)] for rep in range(reps)]

    def among_members(value):
        return lax.all_to_all(value, "dp", 0, 0, axis_index_groups=members, tiled=True)

    def to_rep(value, s):
        pairs = [(i, join(parts_of(i)[0] ^ s, parts_of(i)[1])) for i in range(n_dp)]
        return lax.ppermute(value, "dp", pairs)

    def to_tensor(value, m):
        return lax.ppermute(value, "tensor", [(i, i ^ m) for i in range(n_t)])

    def per_device(
        hidden_in, seq_lengths, norm_gain, norm_bias, qkv_master, qkv_bias, out_master, out_bias,
        up_master, up_bias, down_master, down_bias, out_grad,
    ):
        rows, width = hidden_in.shape
        db = up_master.shape[0]
        fz = up_master.shape[1] // GROUP
        ez = qkv_master.shape[2] // GROUP
        heads = ez // HEAD_DIM
        fw = fz + 3 * ez
        fo = fz + ez
        part = rows // n_t
        me_dp, me_t = lax.axis_index("dp"), lax.axis_index("tensor")
        me_r, me_z = parts_of(me_dp)
        sc = jnp.stack([me_r, me_z, me_t]).astype(jnp.int32)
        all_rows = GROUP * rows
        gain, shift = norm_gain.reshape(1, width), norm_bias.reshape(1, width)

        def blk(sref, s, z):
            return join(sref[0] ^ s, z)

        done = {}

        def gate(name, value):
            waits = [a for n in GATES.get(name, ()) if n in done for a in done[n]]
            return after(value, *waits) if waits else value

        def reg(name, *arrays):
            done[name] = arrays

        def launch(name, body, steps, ins, outs, scratch=()):
            (first, spec), *rest = ins
            made = run(name, body, steps, sc, [(gate(name, first), spec)] + rest, outs, scratch)
            reg(name, made[0])
            return made

        def at(index, size):
            return pl.ds(pl.multiple_of(index * size, size), size)

        def swapped(i):
            return (i % 2) * 2 + i // 2

        def first_hop(mine):
            return to_member(mine, 2)

        def second_hop(mine, far):
            near = to_member(jnp.stack([mine, far]), 1)
            return jnp.concatenate([far[None], near], axis=0)

        paired = n_t == 4
        half = part // 2

        def exchange(b):
            return [to_tensor(b, m) for m in ((1, 2) if paired else range(1, n_t))]

        def forwarded(got):
            return [got[0][:, :half], got[1][:, half:]] if paired else []

        def pieces(got, rest, start=0):
            if not paired:
                return [(m, 0, part, start, a) for m, a in enumerate(got, 1)]
            (one, one_at), (two, two_at) = got
            (far, far_at), (near, near_at) = rest
            return [
                (1, 0, part, one_at, one),
                (2, 0, part, two_at, two),
                (3, 0, half, far_at, far),
                (3, half, half, near_at, near),
            ]

        def place(sref, step, own, first, others, metas, out):
            @pl.when(step == 0)
            def _():
                out[0] = own[...]

            @pl.when(step > 0)
            def _():
                out[0, at(sref[2], part), :] = first[0]
                for (m, off, n, lo, _), ref in zip(metas, others):
                    start = pl.multiple_of((sref[2] ^ m) * part + off, n)
                    out[0, pl.ds(start, n), :] = ref[0, lo : lo + n]

        def piece_specs(first, metas):
            prev = lambda i, s: jnp.maximum(i - 1, 0)
            return [(first, lead((1,) + first.shape[1:], prev))] + [
                (a, lead((1,) + a.shape[1:], prev)) for *_, a in metas
            ]

        member_block = lambda i, s: s[1] ^ swapped(i)

        def cast_in(s, up, qkv, out):
            for z in range(GROUP):
                out[z, :, :fz] = up[:, z * fz : (z + 1) * fz].astype(BF16)
                for j in range(3):
                    lo = fz + j * ez
                    out[z, :, lo : lo + ez] = qkv[j, :, z * ez : (z + 1) * ez].astype(BF16)

        def cast_out(s, down, wo, out):
            out[0, :fz] = down[...].astype(BF16)
            out[0, fz:] = wo[...].astype(BF16)

        def to_reps(stack):
            return [stack] + [to_rep(stack, s) for s in range(1, reps)]

        steps_in = 2
        in_block = [
            lead((db // steps_in, GROUP * fz)),
            pl.BlockSpec((3, db // steps_in, GROUP * ez), lambda i, s: (0, i, 0)),
            pl.BlockSpec((GROUP, db // steps_in, fw), lambda i, s: (0, i, 0)),
        ]
        out_block = [lead((fz, db)), lead((ez, db)), lead((1, fo, db))]
        sent_in = launch(
            CAST_IN, cast_in, steps_in,
            [(up_master, in_block[0]), (qkv_master, in_block[1])],
            [((GROUP, db, fw), BF16, in_block[2])],
        )[0]
        _, _, own_valid = layout(seq_lengths[0], rows)
        x_mine = lax.dynamic_slice_in_dim(hidden_in, me_t * part, part, 0)
        valid_mine = lax.dynamic_slice_in_dim(own_valid, me_t * part, part, 0)
        x_far = first_hop(x_mine)
        l_far = to_member(seq_lengths, 2)
        g_own = (out_grad.astype(F32) * own_valid[:, None]).astype(BF16)
        g_mine = lax.dynamic_slice_in_dim(g_own, me_t * part, part, 0)
        reg(X_FAR, x_far)
        reg(L_FAR, l_far)
        x_first = second_hop(gate(X_FIRST, x_mine), x_far)
        l_near = to_member(jnp.concatenate([seq_lengths, l_far]), 1)
        reg(X_FIRST, x_first)
        reg(L_NEAR, l_near)
        g_far = first_hop(gate(G_FAR, g_mine))
        reg(G_FAR, g_far)
        sent_out = launch(
            CAST_OUT, cast_out, GROUP,
            [(down_master, out_block[0]), (out_master, out_block[1])],
            [((GROUP, fo, db), BF16, out_block[2])],
        )[0]

        g_first = second_hop(g_mine, gate(G_FIRST, g_far))
        reg(G_FIRST, g_first)
        in_stack = among_members(gate(IN_STACK, sent_in))
        reg(IN_STACK, in_stack)
        x_near = exchange(gate(X_NEAR, x_first))
        reg(X_NEAR, *x_near)

        def table_body(s, own, far, near, cs, lf, rt, bg):
            i = pl.program_id(0)
            row = lax.broadcasted_iota(jnp.int32, (rows, ez), 0)
            begin, end = jnp.zeros((rows, ez), jnp.int32), jnp.int32(0)
            for j in range(seq_lengths.shape[1]):
                length = jnp.where(i == 0, own[0, j], jnp.where(i == 1, far[0, j], near[0, j]))
                length = jnp.where(i == 3, near[1, j], length)
                end = end + length
                begin = jnp.where(row >= end, end, begin)
            lane = lax.broadcasted_iota(jnp.int32, (rows, ez), 1) % HEAD_DIM
            halves = ROT_DIM // 2
            step = (lane % halves).astype(F32) * (-2.0 / ROT_DIM)
            rate = jnp.exp(step * math.log(10000.0))
            angle = jnp.where(lane < ROT_DIM, (row - begin).astype(F32) * rate, 0.0)
            sine = jnp.sin(angle)
            cs[0] = jnp.cos(angle)
            lf[0] = jnp.where(lane < halves, -sine, 0.0)
            rt[0] = jnp.where(lane >= halves, sine, 0.0)
            bg[0] = begin[:, 0:1]

        smem = pl.BlockSpec(memory_space=pltpu.SMEM)
        cosine, left, right, begins = launch(
            TABLES, table_body, GROUP,
            [(seq_lengths, smem), (l_far, smem), (l_near, smem)],
            [((GROUP, rows, ez), F32, lead((1, rows, ez), member_block))] * 3
            + [((GROUP, rows, 1), jnp.int32, lead((1, rows, 1), member_block))],
        )

        x_rest = [to_tensor(gate(X_REST, b), m) for b, m in zip(forwarded(x_near), (2, 1))]
        reg(X_REST, *x_rest)
        if paired:
            x_metas = pieces([(a, 0) for a in x_near], [(a, 0) for a in x_rest])
        else:
            x_metas = pieces(x_near, None)

        def norm_body(s, own, first, *rest):
            others = rest[: len(x_metas)]
            gn, bs, x_out, n_out, st_out = rest[len(x_metas) :]
            place(s, pl.program_id(0), own, first, others, x_metas, x_out)
            v = x_out[0].astype(F32)
            mean = jnp.mean(v, axis=1, keepdims=True)
            v = v - mean
            scale = lax.rsqrt(jnp.mean(v * v, axis=1, keepdims=True) + 1e-05)
            v = v * scale * gn[...] + bs[...]
            n_out[0] = v.astype(BF16)
            which = lax.broadcasted_iota(jnp.int32, (rows, 128), 1)
            st_out[0] = jnp.where(which == 0, mean, scale)

        x_all, normed, stats = launch(
            NORM, norm_body, GROUP,
            [(hidden_in, whole(hidden_in.shape))]
            + piece_specs(x_first, x_metas)
            + [(gain, whole(gain.shape)), (shift, whole(shift.shape))],
            [
                ((GROUP, rows, width), BF16, lead((1, rows, width), member_block)),
                ((GROUP, rows, width), BF16, lead((1, rows, width), member_block)),
                ((GROUP, rows, 128), F32, lead((1, rows, 128), member_block)),
            ],
        )

        g_near = [to_tensor(gate(G_NEAR, g_first), m) for m in range(1, n_t)]
        reg(G_NEAR, *g_near)
        out_stack = among_members(gate(OUT_STACK, sent_out))
        reg(OUT_STACK, out_stack)
        w_in = to_reps(gate(W_IN, in_stack))
        g_metas = [(m, 0, part, 0, a) for m, a in enumerate(g_near, 1)]

        def grad_rows_body(s, own, first, *rest):
            others, (g_out, sum_out) = rest[: len(g_metas)], rest[len(g_metas) :]
            place(s, pl.program_id(0), own, first, others, g_metas, g_out)
            sum_out[0] = jnp.sum(g_out[0].astype(F32), axis=0, keepdims=True)

        grads, row_sums = launch(
            GRAD_ROWS, grad_rows_body, GROUP,
            [(g_own, whole(g_own.shape))] + piece_specs(g_first, g_metas),
            [
                ((GROUP, rows, width), BF16, lead((1, rows, width), member_block)),
                ((GROUP, 1, width), F32, lead((1, 1, width), member_block)),
            ],
        )

        my_bias = jnp.concatenate(
            [
                lax.dynamic_slice_in_dim(up_bias, me_z * fz, fz, 0),
                lax.dynamic_slice_in_dim(qkv_bias, me_z * ez, ez, 1).reshape(-1),
            ]
        ).reshape(1, fw)
        n_w = reps

        def forward_body(s, x, cs, lf, rt, bg, bias, *rest):
            w, (branch, pre, qkv, probs, wide) = rest[:n_w], rest[n_w:]

            @pl.when(pl.program_id(0) == 0)
            def _():
                for rep in range(reps):
                    for k in range(GROUP):
                        wide[at(blk(s, rep, k), db), :] = w[rep][k]

            u = mm(x[0], wide[:, :fz]) + bias[:, :fz]
            pre[0] = u
            act = gelu_parts(u)[0]
            branch[0, :, :fz] = act.astype(BF16)
            j = mm(x[0], wide[:, fz:]) + bias[:, fz:]
            c, l, r = cs[0], lf[0], rt[0]
            q, k, v = j[:, :ez], j[:, ez : 2 * ez], j[:, 2 * ez :]
            q = (q * c + rotated(q, l, r)).astype(BF16)
            k = (k * c + rotated(k, l, r)).astype(BF16)
            v = v.astype(BF16)
            qkv[0, :, :ez] = q
            qkv[0, :, ez : 2 * ez] = k
            qkv[0, :, 2 * ez :] = v
            col = lax.broadcasted_iota(jnp.int32, (rows, rows), 1)
            row = lax.broadcasted_iota(jnp.int32, (rows, rows), 0)
            allowed = (col >= bg[0]) & (col <= row)
            for h in range(heads):
                lo, hi = h * HEAD_DIM, (h + 1) * HEAD_DIM
                sco = mm(q[:, lo:hi], k[:, lo:hi], 1, 1) * SCORE_SCALE
                sco = jnp.where(allowed, sco, -1e30)
                e = jnp.exp(sco - jnp.max(sco, axis=1, keepdims=True))
                p = e / jnp.sum(e, axis=1, keepdims=True)
                probs[0, h] = p
                ctx = mm(p.astype(BF16), v[:, lo:hi])
                branch[0, :, fz + lo : fz + hi] = ctx.astype(BF16)

        row_block = lambda n: lead((1, rows, n))
        branch, pre, qkv, probs = launch(
            FORWARD, forward_body, GROUP,
            [
                (normed, row_block(width)), (cosine, row_block(ez)), (left, row_block(ez)),
                (right, row_block(ez)), (begins, row_block(1)), (my_bias, whole(my_bias.shape)),
            ]
            + [(a, whole(a.shape)) for a in w_in],
            [
                ((GROUP, rows, fo), BF16, row_block(fo)),
                ((GROUP, rows, fz), F32, row_block(fz)),
                ((GROUP, rows, 3 * ez), BF16, row_block(3 * ez)),
                ((GROUP, heads, rows, rows), F32, lead((1, heads, rows, rows))),
            ],
            [pltpu.VMEM((width, fw), BF16)],
        )

        w_out = to_reps(gate(W_OUT, out_stack))
        def among(name, parts):
            got = [to_tensor(gate(name, parts[m]), m) for m in range(1, n_t)]
            reg(name, *got)
            return [parts[0]] + got

        def parted(sref, y, outs):
            for m in range(n_t):
                outs[m][0] = y[at(sref[2] ^ m, part), :].astype(BF16)

        part_outs = [((GROUP, part, width), BF16, lead((1, part, width)))] * n_t

        def out_body(s, br, *rest):
            w, outs, (y,) = rest[:n_w], rest[n_w:-1], rest[-1:]
            for rep in range(reps):
                for k in range(GROUP):
                    y[:, at(blk(s, rep, k), db)] = mm(br[0], w[rep][k])
            parted(s, y, outs)

        out_sums = launch(
            OUT_ROWS, out_body, GROUP,
            [(branch, row_block(fo))] + [(a, whole(a.shape)) for a in w_out],
            part_outs,
            [pltpu.VMEM((rows, width), F32)],
        )
        o_got = among(O_GOT, out_sums)

        def add_rows(name, parts, sizes):
            arrays = []
            for terms in parts:
                for a, _ in terms:
                    if not any(a is b for b in arrays):
                        arrays.append(a)
            where = [[([a is b for b in arrays].index(True), r) for a, r in terms] for terms in parts]

            def body(s, *refs):
                ins, outs = refs[: len(arrays)], refs[len(arrays) :]
                row = 0
                for n, out in zip(sizes, outs):
                    for r in range(n):
                        total = None
                        for a, at_row in where[row]:
                            v = ins[a][at_row : at_row + 1, :]
                            total = v if total is None else total + v
                        out[r : r + 1, : total.shape[1]] = total
                        row += 1

            return launch(
                name, body, 1, [(a, whole(a.shape)) for a in arrays],
                [((n, width), F32, whole((n, width))) for n in sizes],
            )

        def product(a, b):
            flat = lambda v: v.reshape(all_rows, v.shape[-1])
            return mm(flat(a[...]), flat(b[...]), 0, 0)

        def half_block(shape, h):
            return lead((1,) + shape, lambda i, s: jnp.clip(i - 2 * h, 0, 1))

        def others_halves(names, left_arr, left_spec, right_arr, right_spec, shape):
            got = []
            for rep in range(1, reps):
                def body(s, a, b, *outs):
                    made = product(a, b).astype(BF16)
                    for h in (0, 1):
                        @pl.when(pl.program_id(0) // 2 == h)
                        def _(h=h):
                            outs[h][0] = made

                sent = launch(
                    names[1], body, GROUP,
                    [(left_arr, left_spec(rep)), (right_arr, right_spec(rep))],
                    [((2,) + shape, BF16, half_block(shape, h)) for h in (0, 1)],
                )
                got += [to_rep(gate(names[2], a), rep) for a in sent]
            return got

        def others_part(names, left_arr, left_spec, right_arr, right_spec, shape):
            got = []
            for rep in range(1, reps):
                def body(s, a, b, out):
                    out[0] = product(a, b).astype(BF16)

                sent = launch(
                    names[1], body, GROUP,
                    [(left_arr, left_spec(rep)), (right_arr, right_spec(rep))],
                    [((GROUP,) + shape, BF16, lead((1,) + shape))],
                )[0]
                got.append(to_rep(gate(names[2], sent), rep))
            return got

        def own_part(names, left_arr, left_spec, right_arr, right_spec, shape, got, parts=1):
            def body(s, a, b, *refs):
                total = product(a, b)
                for n, ref in enumerate(refs[:-1]):
                    if parts == 1:
                        total = total + ref[0].astype(F32)
                    elif n % 2 == 0:
                        v = jnp.where(pl.program_id(0) < 2, ref[0], refs[n + 1][0])
                        total = total + v.astype(F32)
                refs[-1][0] = total.astype(BF16)

            return launch(
                names[0], body, GROUP,
                [(left_arr, left_spec(0)), (right_arr, right_spec(0))]
                + [(a, lead((1,) + shape) if parts == 1 else half_block(shape, n % 2)) for n, a in enumerate(got)],
                [((GROUP,) + shape, BF16, lead((1,) + shape))],
            )[0]

        def columns(rep):
            return pl.BlockSpec((GROUP, rows, db), lambda i, s: (0, 0, blk(s, rep, i)))

        out_args = (
            (OUT_WEIGHT_GRAD, OUT_WEIGHT_GRAD_OTHER, OUT_WEIGHT_GRAD_REP), branch, lambda rep: whole(branch.shape), grads, columns, (fo, db)
        )
        out_parts = own_part(*out_args, others_part(*out_args))
        out_pieces = among_members(out_parts)
        reg(OUT_PIECES, out_pieces)

        def backward_body(s, g, pre, qkv, probs, cs, lf, rt, *rest):
            w, (wide_out, sum_out, w_all) = rest[:n_w], rest[n_w:]

            @pl.when(pl.program_id(0) == 0)
            def _():
                for rep in range(reps):
                    for k in range(GROUP):
                        w_all[:, at(blk(s, rep, k), db)] = w[rep][k]

            ga = mm(g[0], w_all[:fz], 1, 1)
            u = pre[0]
            t = gelu_parts(u)[1]
            slope = 0.5 * (1.0 + t) + 0.5 * u * (1.0 - t * t) * (
                GELU_A * (1.0 + 3.0 * GELU_B * u * u)
            )
            gp = (ga * slope).astype(BF16)
            wide_out[0, :, :fz] = gp
            sum_out[0, :, :fz] = jnp.sum(gp.astype(F32), axis=0, keepdims=True)
            gc = mm(g[0], w_all[fz:], 1, 1).astype(BF16)
            q, k, v = qkv[0, :, :ez], qkv[0, :, ez : 2 * ez], qkv[0, :, 2 * ez :]
            dq, dk, dv = [], [], []
            for h in range(heads):
                lo, hi = h * HEAD_DIM, (h + 1) * HEAD_DIM
                p, gch = probs[0, h], gc[:, lo:hi]
                dv.append(mm(p.astype(BF16), gch, 0, 0))
                dp = mm(gch, v[:, lo:hi], 1, 1)
                ds = (p * (dp - jnp.sum(p * dp, axis=1, keepdims=True))).astype(BF16)
                dq.append(mm(ds, k[:, lo:hi]) * SCORE_SCALE)
                dk.append(mm(ds, q[:, lo:hi], 0, 0) * SCORE_SCALE)
            c, l, r = cs[0], lf[0], rt[0]
            join_heads = lambda parts: parts[0] if heads == 1 else jnp.concatenate(parts, axis=1)
            dq, dk, dv = join_heads(dq), join_heads(dk), join_heads(dv)
            dq = dq * c - rotated(dq, l, r)
            dk = dk * c - rotated(dk, l, r)
            for j, d in enumerate((dq, dk, dv)):
                low = d.astype(BF16)
                lo = fz + j * ez
                wide_out[0, :, lo : lo + ez] = low
                sum_out[0, :, lo : lo + ez] = jnp.sum(low.astype(F32), axis=0, keepdims=True)

        wide, wide_sums = launch(
            BACKWARD, backward_body, GROUP,
            [
                (grads, row_block(width)), (pre, row_block(fz)), (qkv, row_block(3 * ez)),
                (probs, lead((1, heads, rows, rows))), (cosine, row_block(ez)),
                (left, row_block(ez)), (right, row_block(ez)),
            ]
            + [(a, whole(a.shape)) for a in w_out],
            [((GROUP, rows, fw), BF16, row_block(fw)), ((GROUP, 1, fw), F32, lead((1, 1, fw)))],
            [pltpu.VMEM((fo, width), BF16)],
        )

        in_args = (
            (IN_WEIGHT_GRAD, IN_WEIGHT_GRAD_OTHER, IN_WEIGHT_GRAD_REP), normed, columns, wide, lambda rep: whole(wide.shape), (db, fw)
        )
        in_got = others_halves(*in_args)

        def normed_grad_body(s, gw, x, st, *rest):
            w, outs, (sums, y) = rest[:n_w], rest[n_w:-2], rest[-2:]
            for rep in range(reps):
                for k in range(GROUP):
                    y[:, at(blk(s, rep, k), db)] = mm(gw[0], w[rep][k], 1, 1)
            parted(s, y, outs)
            v = y[...]
            hat = (x[0].astype(F32) - st[0, :, 0:1]) * st[0, :, 1:2]

            @pl.when(pl.program_id(0) == 0)
            def _():
                sums[...] = jnp.zeros(sums.shape, F32)

            sums[0:1] += jnp.sum(v * hat, axis=0, keepdims=True)
            sums[1:2] += jnp.sum(v, axis=0, keepdims=True)

        *gn_parts, gain_sums = launch(
            NORMED_GRAD, normed_grad_body, GROUP,
            [(wide, row_block(fw)), (x_all, row_block(width)), (stats, row_block(128))]
            + [(a, whole(a.shape)) for a in w_in],
            part_outs + [((2, width), F32, whole((2, width)))],
            [pltpu.VMEM((rows, width), F32)],
        )

        own_block = lambda i, s: s[1] ^ i

        two = (2, part, width)

        def add_tensor(name, near_name, got):
            def body(s, *refs):
                ins, outs = refs[:n_t], refs[n_t:]
                total = ins[0][0].astype(F32)
                for ref in ins[1:]:
                    total = total + ref[0].astype(F32)
                for k in range(GROUP):
                    @pl.when(pl.program_id(0) == k)
                    def _(k=k):
                        outs[k % 2][k // 2] = total.astype(outs[k % 2].dtype)

            keep, send = launch(
                name, body, GROUP,
                [(a, lead((1, part, width), own_block)) for a in got],
                [(two, F32, whole(two)), (two, BF16, whole(two))],
            )
            near = to_member(gate(near_name, send), 1)
            reg(near_name, near)
            return keep, near

        def add_near(name, far_name, keep, near):
            def body(s, keep, near, own, send):
                own[...] = keep[0] + near[0].astype(F32)
                send[...] = (keep[1] + near[1].astype(F32)).astype(BF16)

            own, send = launch(
                name, body, 1, [(keep, whole(two)), (near, whole(two))],
                [((part, width), F32, whole((part, width))), ((part, width), BF16, whole((part, width)))],
            )
            far = to_member(gate(far_name, send), 2)
            reg(far_name, far)
            return own, far

        mine_rows = lead((part, width), lambda i, s: s[2])

        def join_rows(name, mine, got):
            def body(s, first, *rest):
                for m, ref in enumerate((first,) + rest[:-1]):
                    rest[-1][at(s[2] ^ m, part), :] = ref[...]

            return launch(
                name, body, 1,
                [(mine, whole(mine.shape))] + [(a, whole(a.shape)) for a in got],
                [((rows, width), BF16, whole((rows, width)))],
            )[0]

        gn_got = among(GN_GOT, gn_parts)
        out_keep, out_near = add_tensor(OUT_ADD, OUT_ADD_NEAR, o_got)
        in_parts = own_part(*in_args, in_got, 2)
        in_pieces = among_members(in_parts)
        o_sums = add_near(OUT_ADD_PAIR, OUT_ADD_PAIR_FAR, out_keep, out_near)
        flat = [row_sums.reshape(GROUP, width), wide_sums.reshape(GROUP, fw)]
        order = ((0, 1), (2, 3))
        low = add_rows(SUMS_LOW, [[(flat[n], a), (flat[n], b)] for n in (0, 1) for a, b in order], (4,))[0]
        small = add_rows(
            SUMS, [[(gain_sums, 0)], [(gain_sums, 1)], [(low, 0), (low, 1)], [(low, 2), (low, 3)]], (4,)
        )[0]
        hop = 1
        while hop < reps:
            got = to_rep(gate(SMALL_REP, small), hop)
            small = add_rows(SUMS_REP, [[(small, r), (got, r)] for r in range(4)], (4,))[0]
            hop *= 2
        gains, bias_total, wide_sum = add_rows(SUMS_SPLIT, [[(small, r)] for r in range(4)], (2, 1, 1))
        bias_total = bias_total[0]
        gn_keep, gn_near = add_tensor(GN_ADD, GN_ADD_NEAR, gn_got)

        both_bias = (out_bias + down_bias).reshape(1, width)

        def hidden_out_body(s, *refs):
            sums, (x, ok, bias, out) = refs[:2], refs[2:]
            total = sums[0][...] + sums[1][...].astype(F32)
            out[...] = (x[...].astype(F32) + ok[...] * (total + bias[...])).astype(BF16)

        hidden_out_mine = launch(
            HIDDEN_OUT, hidden_out_body, 1,
            [(a, whole(a.shape)) for a in o_sums]
            + [(hidden_in, mine_rows), (valid_mine[:, None], whole((part, 1))), (both_bias, whole(both_bias.shape))],
            [((part, width), BF16, whole((part, width)))],
        )[0]
        hidden_out_got = among(HIDDEN_OUT_GOT, [hidden_out_mine] * n_t)[1:]

        for hop in range(1, n_t):
            if hop & (hop - 1) == 0:
                got = to_tensor(gate(SMALL_TENSOR, gains), hop)
                gains = add_rows(GAINS_TENSOR, [[(gains, r), (got, r)] for r in range(2)], (2,))[0]
        gn_sums = add_near(GN_ADD_PAIR, GN_ADD_PAIR_FAR, gn_keep, gn_near)
        sent = add_rows(GAINS_SENT, [[(gains, 0)], [(gains, 1)], [(wide_sum, 0)]], (3,))[0]
        hidden_out = join_rows(HIDDEN_OUT_ROWS, hidden_out_mine, hidden_out_got)
        def finish_out(s, piece, down, wo):
            down[...] = piece[0, :fz].astype(F32)
            wo[...] = piece[0, fz:].astype(F32)

        down_master_grad, out_master_grad = launch(
            FINISH_OUT, finish_out, GROUP,
            [(out_pieces, out_block[2])],
            [(down_master.shape, F32, out_block[0]), (out_master.shape, F32, out_block[1])],
        )
        def input_grad_body(s, *refs):
            sums, (x, g, gn, out) = refs[:2], refs[2:]
            total = sums[0][...] + sums[1][...].astype(F32)
            v = x[...].astype(F32)
            v = v - jnp.mean(v, axis=1, keepdims=True)
            scale = lax.rsqrt(jnp.mean(v * v, axis=1, keepdims=True) + 1e-05)
            hat = v * scale
            gy = total * gn[...]
            d = gy - jnp.mean(gy, axis=1, keepdims=True) - hat * jnp.mean(gy * hat, axis=1, keepdims=True)
            out[...] = (g[...].astype(F32) + d * scale).astype(BF16)

        input_grad_mine = launch(
            INPUT_GRAD, input_grad_body, 1,
            [(a, whole(a.shape)) for a in gn_sums]
            + [(hidden_in, mine_rows), (out_grad, mine_rows), (gain, whole(gain.shape))],
            [((part, width), BF16, whole((part, width)))],
        )[0]
        input_grad_got = among(INPUT_GRAD_GOT, [input_grad_mine] * n_t)[1:]

        got = to_member(gate(SMALL_FAR, sent), 2)
        sent = add_rows(
            GAINS_FAR, [[(sent, 0), (got, 0)], [(sent, 1), (got, 1)], [(sent, 2)], [(got, 2)]], (4,)
        )[0]
        got = to_member(sent, 1)
        def finish_in(s, piece, up, qkv):
            for z in range(GROUP):
                up[:, z * fz : (z + 1) * fz] = piece[z, :, :fz].astype(F32)
                for j in range(3):
                    lo = fz + j * ez
                    qkv[j, :, z * ez : (z + 1) * ez] = piece[z, :, lo : lo + ez].astype(F32)

        up_master_grad, qkv_master_grad = launch(
            FINISH_IN, finish_in, steps_in,
            [(in_pieces, in_block[2])],
            [(up_master.shape, F32, in_block[0]), (qkv_master.shape, F32, in_block[1])],
        )


        def bias_body(s, mine, got, gains, up, qkv, scr):
            gains[...] = mine[0:2, :] + got[0:2, :]
            for k, ref, row in ((0, mine, 2), (2, mine, 3), (1, got, 2), (3, got, 3)):
                scr[pl.ds(s[1] ^ k, 1), :] = ref[row : row + 1, :]
            for z in range(GROUP):
                up[z : z + 1, :] = scr[z : z + 1, :fz]
                for j in range(3):
                    lo = fz + j * ez
                    qkv[j : j + 1, z * ez : (z + 1) * ez] = scr[z : z + 1, lo : lo + ez]

        gains, up_bias_grad, qkv_bias_grad = launch(
            BIAS_GRADS, bias_body, 1, [(sent, whole(sent.shape)), (got, whole(got.shape))],
            [
                ((2, width), F32, whole((2, width))), ((GROUP, fz), F32, whole((GROUP, fz))),
                (qkv_bias.shape, F32, whole(qkv_bias.shape)),
            ],
            [pltpu.VMEM((GROUP, width), F32)],
        )
        up_bias_grad = up_bias_grad.reshape(up_bias.shape)
        input_grad = join_rows(INPUT_GRAD_ROWS, input_grad_mine, input_grad_got)
        return (
            hidden_out, input_grad, gains[0], gains[1], qkv_master_grad, qkv_bias_grad,
            out_master_grad, bias_total, up_master_grad, up_bias_grad, down_master_grad, bias_total,
        )

    return per_device


def solution(mesh):
    placed = (
        P("dp", None), P("dp", None), P(), P(), P(None, "dp", "tensor"), P(None, "tensor"),
        P("tensor", "dp"), P(), P("dp", "tensor"), P("tensor"), P("tensor", "dp"), P(), P("dp", None),
    )
    return jax.shard_map(
        make(mesh.shape["dp"], mesh.shape["tensor"]),
        mesh=mesh,
        in_specs=placed,
        out_specs=(
            P("dp", None), P("dp", None), P(), P(), P(None, "dp", "tensor"), P(None, "tensor"),
            P("tensor", "dp"), P(), P("dp", "tensor"), P("tensor"), P("tensor", "dp"), P(),
        ),
        check_vma=False,
    )
```

```python
import functools
import math

import jax
import jax.numpy as jnp
from jax import lax
from jax.experimental import pallas as pl
from jax.experimental.pallas import tpu as pltpu
from jax.sharding import PartitionSpec as P

HEAD_DIM = 64
ROT_DIM = 32
GROUP = 4
CORES = 2
BF16 = jnp.bfloat16
F32 = jnp.float32
GELU_A = math.sqrt(2.0 / math.pi)
GELU_B = 0.044715
SCORE_SCALE = 1.0 / math.sqrt(HEAD_DIM)
VMEM_LIMIT = 50 * 2**20
UNIT = 2**19
(
    CAST_IN, X_FAR, L_FAR, X_FIRST, L_NEAR, G_FAR, CAST_OUT, G_FIRST, IN_STACK, X_NEAR, TABLES,
    X_REST, NORM, G_NEAR, OUT_STACK, W_IN, GRAD_ROWS, FORWARD, W_OUT, OUT_ROWS, O_GOT,
    OUT_WEIGHT_GRAD, OUT_WEIGHT_GRAD_OTHER, OUT_WEIGHT_GRAD_REP, OUT_PIECES, BACKWARD,
    IN_WEIGHT_GRAD, IN_WEIGHT_GRAD_OTHER, IN_WEIGHT_GRAD_REP, NORMED_GRAD, GN_GOT, OUT_ADD,
    OUT_ADD_NEAR, OUT_ADD_PAIR, OUT_ADD_PAIR_FAR, SUMS_LOW, SUMS, SMALL_REP, SUMS_REP,
    SUMS_SPLIT, GN_ADD, GN_ADD_NEAR, HIDDEN_OUT, HIDDEN_OUT_GOT, SMALL_TENSOR, GAINS_TENSOR,
    GN_ADD_PAIR, GN_ADD_PAIR_FAR, GAINS_SENT, HIDDEN_OUT_ROWS, FINISH_OUT, INPUT_GRAD,
    INPUT_GRAD_GOT, SMALL_FAR, GAINS_FAR, FINISH_IN, BIAS_GRADS, INPUT_GRAD_ROWS,
) = range(58)
COSTS = {
    CAST_IN: 14080,
    CAST_OUT: 1518,
    TABLES: 1716,
    NORM: 28600,
    FORWARD: 1,
    GRAD_ROWS: 1936,
    OUT_ROWS: 5082,
    OUT_WEIGHT_GRAD: 3498,
    BACKWARD: 1,
    NORMED_GRAD: 5192,
    IN_WEIGHT_GRAD: 1364,
    OUT_ADD: 4510,
    GN_ADD: 7920,
    HIDDEN_OUT: 594,
    INPUT_GRAD: 121,
    HIDDEN_OUT_ROWS: 704,
    INPUT_GRAD_ROWS: 352,
    FINISH_OUT: 1650,
    FINISH_IN: 1716,
    BIAS_GRADS: 10560,
    GN_ADD_PAIR: 132,
    OUT_ADD_PAIR: 528,
    SUMS_SPLIT: 220,
    SUMS: 2200,
    SUMS_REP: 8800,
}
GATES = {
    IN_STACK: (X_FIRST, L_NEAR, G_FAR,),
    G_FIRST: (X_FIRST,),
    X_REST: (TABLES,),
    OUT_STACK: (G_FIRST, IN_STACK, X_NEAR,),
    W_IN: (G_FIRST, NORM,),
    G_NEAR: (IN_STACK, X_REST,),
    FORWARD: (OUT_STACK,),
    BACKWARD: (OUT_ROWS, OUT_WEIGHT_GRAD,),
    IN_WEIGHT_GRAD_OTHER: (BACKWARD,),
    IN_WEIGHT_GRAD: (NORMED_GRAD,),
    OUT_ADD: (NORMED_GRAD, OUT_PIECES,),
    NORMED_GRAD: (IN_WEIGHT_GRAD_OTHER, OUT_PIECES,),
    OUT_WEIGHT_GRAD: (OUT_ROWS,),
    SUMS_LOW: (GN_ADD,),
    GAINS_FAR: (GN_ADD_PAIR, INPUT_GRAD,),
    GRAD_ROWS: (OUT_STACK,),
    SMALL_REP: (IN_WEIGHT_GRAD,),
    GN_ADD_PAIR: (GAINS_TENSOR,),
    INPUT_GRAD_ROWS: (BIAS_GRADS, FINISH_IN,),
    INPUT_GRAD: (FINISH_OUT,),
    HIDDEN_OUT_GOT: (GN_ADD,),
    CAST_OUT: (X_FAR,),
    HIDDEN_OUT_ROWS: (GN_ADD_PAIR,),
    TABLES: (CAST_OUT,),
    OUT_ROWS: (G_NEAR,),
    NORM: (G_FIRST,),
    FINISH_IN: (GN_ADD_PAIR,),
    SMALL_TENSOR: (GN_GOT,),
}


def mm(a, b, ca=1, cb=0):
    return lax.dot_general(a, b, (((ca,), (cb,)), ((), ())), preferred_element_type=F32)


def whole(shape):
    zeros = (0,) * len(shape)
    return pl.BlockSpec(tuple(shape), lambda i, sc: zeros)


def lead(shape, index=lambda i, sc: i):
    tail = (0,) * (len(shape) - 1)
    return pl.BlockSpec(tuple(shape), lambda i, sc: (index(i, sc),) + tail)


def run(name, body, steps, scalars, ins, outs, scratch=()):
    size = lambda shape, dtype: math.prod(shape) * jnp.dtype(dtype).itemsize
    moved = sum(size(a.shape, a.dtype) for a, _ in ins) + sum(size(s, d) for s, d, _ in outs)
    return pl.pallas_call(
        body,
        out_shape=[jax.ShapeDtypeStruct(s, d) for s, d, _ in outs],
        grid_spec=pltpu.PrefetchScalarGridSpec(
            num_scalar_prefetch=1,
            grid=(steps,),
            in_specs=[spec for _, spec in ins],
            out_specs=[spec for _, _, spec in outs],
            scratch_shapes=list(scratch),
        ),
        compiler_params=pltpu.CompilerParams(vmem_limit_bytes=VMEM_LIMIT),
        cost_estimate=pl.CostEstimate(
            flops=COSTS.get(name, 500) * UNIT, bytes_accessed=moved, transcendentals=0
        ),
    )(scalars, *[a for a, _ in ins])


def after(value, *done):
    return lax.optimization_barrier((value,) + done)[0]


def rotated(x, left, right):
    h = ROT_DIM // 2
    to_left = jnp.concatenate([x[:, h:], x[:, :h]], axis=1)
    to_right = jnp.concatenate([x[:, -h:], x[:, :-h]], axis=1)
    return to_left * left + to_right * right


def gelu_parts(u):
    t = jnp.tanh(GELU_A * (u + GELU_B * u * u * u))
    return 0.5 * u * (1.0 + t), t


def layout(lengths, rows):
    slots = lengths.shape[0]
    upper = lax.iota(jnp.int32, slots)[:, None] <= lax.iota(jnp.int32, slots)[None, :]
    ends = jnp.sum(jnp.where(upper, lengths[:, None], 0), axis=0)
    ids = lax.iota(jnp.int32, rows)
    passed = ids[:, None] >= ends[None, :]
    begins = jnp.max(jnp.where(passed, ends[None, :], 0), axis=1)
    return begins, ids - begins, (ids < jnp.max(ends)).astype(F32)


def make(n_dp, n_t):
    reps = n_dp // GROUP
    block = GROUP * CORES

    def join(rep, member):
        return (rep // CORES * GROUP + member) * CORES + rep % CORES

    def parts_of(index):
        return index // block * CORES + index % CORES, (index // CORES) % GROUP

    def to_member(value, k):
        pairs = [(i, join(parts_of(i)[0], parts_of(i)[1] ^ k)) for i in range(n_dp)]
        return lax.ppermute(value, "dp", pairs)

    members = [[join(rep, z) for z in range(GROUP)] for rep in range(reps)]

    def among_members(value):
        return lax.all_to_all(value, "dp", 0, 0, axis_index_groups=members, tiled=True)

    def to_rep(value, s):
        pairs = [(i, join(parts_of(i)[0] ^ s, parts_of(i)[1])) for i in range(n_dp)]
        return lax.ppermute(value, "dp", pairs)

    def to_tensor(value, m):
        return lax.ppermute(value, "tensor", [(i, i ^ m) for i in range(n_t)])

    def per_device(
        hidden_in, seq_lengths, norm_gain, norm_bias, qkv_master, qkv_bias, out_master, out_bias,
        up_master, up_bias, down_master, down_bias, out_grad,
    ):
        rows, width = hidden_in.shape
        db = up_master.shape[0]
        fz = up_master.shape[1] // GROUP
        ez = qkv_master.shape[2] // GROUP
        heads = ez // HEAD_DIM
        fw = fz + 3 * ez
        fo = fz + ez
        part = rows // n_t
        me_dp, me_t = lax.axis_index("dp"), lax.axis_index("tensor")
        me_r, me_z = parts_of(me_dp)
        sc = jnp.stack([me_r, me_z, me_t]).astype(jnp.int32)
        all_rows = GROUP * rows
        gain, shift = norm_gain.reshape(1, width), norm_bias.reshape(1, width)

        def blk(sref, s, z):
            return join(sref[0] ^ s, z)

        done = {}

        def gate(name, value):
            waits = [a for n in GATES.get(name, ()) if n in done for a in done[n]]
            return after(value, *waits) if waits else value

        def reg(name, *arrays):
            done[name] = arrays

        def launch(name, body, steps, ins, outs, scratch=()):
            (first, spec), *rest = ins
            made = run(name, body, steps, sc, [(gate(name, first), spec)] + rest, outs, scratch)
            reg(name, made[0])
            return made

        def at(index, size):
            return pl.ds(pl.multiple_of(index * size, size), size)

        def swapped(i):
            return (i % 2) * 2 + i // 2

        def first_hop(mine):
            return to_member(mine, 2)

        def second_hop(mine, far):
            near = to_member(jnp.stack([mine, far]), 1)
            return jnp.concatenate([far[None], near], axis=0)

        paired = n_t == 4
        half = part // 2

        def exchange(b):
            return [to_tensor(b, m) for m in ((1, 2) if paired else range(1, n_t))]

        def forwarded(got):
            return [got[0][:, :half], got[1][:, half:]] if paired else []

        def pieces(got, rest, start=0):
            if not paired:
                return [(m, 0, part, start, a) for m, a in enumerate(got, 1)]
            (one, one_at), (two, two_at) = got
            (far, far_at), (near, near_at) = rest
            return [
                (1, 0, part, one_at, one),
                (2, 0, part, two_at, two),
                (3, 0, half, far_at, far),
                (3, half, half, near_at, near),
            ]

        def place(sref, step, own, first, others, metas, out):
            @pl.when(step == 0)
            def _():
                out[0] = own[...]

            @pl.when(step > 0)
            def _():
                out[0, at(sref[2], part), :] = first[0]
                for (m, off, n, lo, _), ref in zip(metas, others):
                    start = pl.multiple_of((sref[2] ^ m) * part + off, n)
                    out[0, pl.ds(start, n), :] = ref[0, lo : lo + n]

        def piece_specs(first, metas):
            prev = lambda i, s: jnp.maximum(i - 1, 0)
            return [(first, lead((1,) + first.shape[1:], prev))] + [
                (a, lead((1,) + a.shape[1:], prev)) for *_, a in metas
            ]

        member_block = lambda i, s: s[1] ^ swapped(i)

        def cast_in(s, up, qkv, out):
            for z in range(GROUP):
                out[z, :, :fz] = up[:, z * fz : (z + 1) * fz].astype(BF16)
                for j in range(3):
                    lo = fz + j * ez
                    out[z, :, lo : lo + ez] = qkv[j, :, z * ez : (z + 1) * ez].astype(BF16)

        def cast_out(s, down, wo, out):
            out[0, :fz] = down[...].astype(BF16)
            out[0, fz:] = wo[...].astype(BF16)

        def to_reps(stack):
            return [stack] + [to_rep(stack, s) for s in range(1, reps)]

        steps_in = 2
        in_block = [
            lead((db // steps_in, GROUP * fz)),
            pl.BlockSpec((3, db // steps_in, GROUP * ez), lambda i, s: (0, i, 0)),
            pl.BlockSpec((GROUP, db // steps_in, fw), lambda i, s: (0, i, 0)),
        ]
        out_block = [lead((fz, db)), lead((ez, db)), lead((1, fo, db))]
        sent_in = launch(
            CAST_IN, cast_in, steps_in,
            [(up_master, in_block[0]), (qkv_master, in_block[1])],
            [((GROUP, db, fw), BF16, in_block[2])],
        )[0]
        _, _, own_valid = layout(seq_lengths[0], rows)
        x_mine = lax.dynamic_slice_in_dim(hidden_in, me_t * part, part, 0)
        valid_mine = lax.dynamic_slice_in_dim(own_valid, me_t * part, part, 0)
        x_far = first_hop(x_mine)
        l_far = to_member(seq_lengths, 2)
        g_own = (out_grad.astype(F32) * own_valid[:, None]).astype(BF16)
        g_mine = lax.dynamic_slice_in_dim(g_own, me_t * part, part, 0)
        reg(X_FAR, x_far)
        reg(L_FAR, l_far)
        x_first = second_hop(gate(X_FIRST, x_mine), x_far)
        l_near = to_member(jnp.concatenate([seq_lengths, l_far]), 1)
        reg(X_FIRST, x_first)
        reg(L_NEAR, l_near)
        g_far = first_hop(gate(G_FAR, g_mine))
        reg(G_FAR, g_far)
        sent_out = launch(
            CAST_OUT, cast_out, GROUP,
            [(down_master, out_block[0]), (out_master, out_block[1])],
            [((GROUP, fo, db), BF16, out_block[2])],
        )[0]

        g_first = second_hop(g_mine, gate(G_FIRST, g_far))
        reg(G_FIRST, g_first)
        in_stack = among_members(gate(IN_STACK, sent_in))
        reg(IN_STACK, in_stack)
        x_near = exchange(gate(X_NEAR, x_first))
        reg(X_NEAR, *x_near)

        def table_body(s, own, far, near, cs, lf, rt, bg):
            i = pl.program_id(0)
            row = lax.broadcasted_iota(jnp.int32, (rows, ez), 0)
            begin, end = jnp.zeros((rows, ez), jnp.int32), jnp.int32(0)
            for j in range(seq_lengths.shape[1]):
                length = jnp.where(i == 0, own[0, j], jnp.where(i == 1, far[0, j], near[0, j]))
                length = jnp.where(i == 3, near[1, j], length)
                end = end + length
                begin = jnp.where(row >= end, end, begin)
            lane = lax.broadcasted_iota(jnp.int32, (rows, ez), 1) % HEAD_DIM
            halves = ROT_DIM // 2
            step = (lane % halves).astype(F32) * (-2.0 / ROT_DIM)
            rate = jnp.exp(step * math.log(10000.0))
            angle = jnp.where(lane < ROT_DIM, (row - begin).astype(F32) * rate, 0.0)
            sine = jnp.sin(angle)
            cs[0] = jnp.cos(angle)
            lf[0] = jnp.where(lane < halves, -sine, 0.0)
            rt[0] = jnp.where(lane >= halves, sine, 0.0)
            bg[0] = begin[:, 0:1]

        smem = pl.BlockSpec(memory_space=pltpu.SMEM)
        cosine, left, right, begins = launch(
            TABLES, table_body, GROUP,
            [(seq_lengths, smem), (l_far, smem), (l_near, smem)],
            [((GROUP, rows, ez), F32, lead((1, rows, ez), member_block))] * 3
            + [((GROUP, rows, 1), jnp.int32, lead((1, rows, 1), member_block))],
        )

        x_rest = [to_tensor(gate(X_REST, b), m) for b, m in zip(forwarded(x_near), (2, 1))]
        reg(X_REST, *x_rest)
        if paired:
            x_metas = pieces([(a, 0) for a in x_near], [(a, 0) for a in x_rest])
        else:
            x_metas = pieces(x_near, None)

        def norm_body(s, own, first, *rest):
            others = rest[: len(x_metas)]
            gn, bs, x_out, n_out, st_out = rest[len(x_metas) :]
            place(s, pl.program_id(0), own, first, others, x_metas, x_out)
            v = x_out[0].astype(F32)
            mean = jnp.mean(v, axis=1, keepdims=True)
            v = v - mean
            scale = lax.rsqrt(jnp.mean(v * v, axis=1, keepdims=True) + 1e-05)
            v = v * scale * gn[...] + bs[...]
            n_out[0] = v.astype(BF16)
            which = lax.broadcasted_iota(jnp.int32, (rows, 128), 1)
            st_out[0] = jnp.where(which == 0, mean, scale)

        x_all, normed, stats = launch(
            NORM, norm_body, GROUP,
            [(hidden_in, whole(hidden_in.shape))]
            + piece_specs(x_first, x_metas)
            + [(gain, whole(gain.shape)), (shift, whole(shift.shape))],
            [
                ((GROUP, rows, width), BF16, lead((1, rows, width), member_block)),
                ((GROUP, rows, width), BF16, lead((1, rows, width), member_block)),
                ((GROUP, rows, 128), F32, lead((1, rows, 128), member_block)),
            ],
        )

        g_near = [to_tensor(gate(G_NEAR, g_first), m) for m in range(1, n_t)]
        reg(G_NEAR, *g_near)
        out_stack = among_members(gate(OUT_STACK, sent_out))
        reg(OUT_STACK, out_stack)
        w_in = to_reps(gate(W_IN, in_stack))
        g_metas = [(m, 0, part, 0, a) for m, a in enumerate(g_near, 1)]

        def grad_rows_body(s, own, first, *rest):
            others, (g_out, sum_out) = rest[: len(g_metas)], rest[len(g_metas) :]
            place(s, pl.program_id(0), own, first, others, g_metas, g_out)
            sum_out[0] = jnp.sum(g_out[0].astype(F32), axis=0, keepdims=True)

        grads, row_sums = launch(
            GRAD_ROWS, grad_rows_body, GROUP,
            [(g_own, whole(g_own.shape))] + piece_specs(g_first, g_metas),
            [
                ((GROUP, rows, width), BF16, lead((1, rows, width), member_block)),
                ((GROUP, 1, width), F32, lead((1, 1, width), member_block)),
            ],
        )

        my_bias = jnp.concatenate(
            [
                lax.dynamic_slice_in_dim(up_bias, me_z * fz, fz, 0),
                lax.dynamic_slice_in_dim(qkv_bias, me_z * ez, ez, 1).reshape(-1),
            ]
        ).reshape(1, fw)
        n_w = reps

        def forward_body(s, x, cs, lf, rt, bg, bias, *rest):
            w, (branch, pre, qkv, probs, wide) = rest[:n_w], rest[n_w:]

            @pl.when(pl.program_id(0) == 0)
            def _():
                for rep in range(reps):
                    for k in range(GROUP):
                        wide[at(blk(s, rep, k), db), :] = w[rep][k]

            u = mm(x[0], wide[:, :fz]) + bias[:, :fz]
            pre[0] = u
            act = gelu_parts(u)[0]
            branch[0, :, :fz] = act.astype(BF16)
            j = mm(x[0], wide[:, fz:]) + bias[:, fz:]
            c, l, r = cs[0], lf[0], rt[0]
            q, k, v = j[:, :ez], j[:, ez : 2 * ez], j[:, 2 * ez :]
            q = (q * c + rotated(q, l, r)).astype(BF16)
            k = (k * c + rotated(k, l, r)).astype(BF16)
            v = v.astype(BF16)
            qkv[0, :, :ez] = q
            qkv[0, :, ez : 2 * ez] = k
            qkv[0, :, 2 * ez :] = v
            col = lax.broadcasted_iota(jnp.int32, (rows, rows), 1)
            row = lax.broadcasted_iota(jnp.int32, (rows, rows), 0)
            allowed = (col >= bg[0]) & (col <= row)
            for h in range(heads):
                lo, hi = h * HEAD_DIM, (h + 1) * HEAD_DIM
                sco = mm(q[:, lo:hi], k[:, lo:hi], 1, 1) * SCORE_SCALE
                sco = jnp.where(allowed, sco, -1e30)
                e = jnp.exp(sco - jnp.max(sco, axis=1, keepdims=True))
                p = e / jnp.sum(e, axis=1, keepdims=True)
                probs[0, h] = p
                ctx = mm(p.astype(BF16), v[:, lo:hi])
                branch[0, :, fz + lo : fz + hi] = ctx.astype(BF16)

        row_block = lambda n: lead((1, rows, n))
        branch, pre, qkv, probs = launch(
            FORWARD, forward_body, GROUP,
            [
                (normed, row_block(width)), (cosine, row_block(ez)), (left, row_block(ez)),
                (right, row_block(ez)), (begins, row_block(1)), (my_bias, whole(my_bias.shape)),
            ]
            + [(a, whole(a.shape)) for a in w_in],
            [
                ((GROUP, rows, fo), BF16, row_block(fo)),
                ((GROUP, rows, fz), F32, row_block(fz)),
                ((GROUP, rows, 3 * ez), BF16, row_block(3 * ez)),
                ((GROUP, heads, rows, rows), F32, lead((1, heads, rows, rows))),
            ],
            [pltpu.VMEM((width, fw), BF16)],
        )

        w_out = to_reps(gate(W_OUT, out_stack))
        def among(name, parts):
            got = [to_tensor(gate(name, parts[m]), m) for m in range(1, n_t)]
            reg(name, *got)
            return [parts[0]] + got

        def parted(sref, y, outs):
            for m in range(n_t):
                outs[m][0] = y[at(sref[2] ^ m, part), :].astype(BF16)

        part_outs = [((GROUP, part, width), BF16, lead((1, part, width)))] * n_t

        def out_body(s, br, *rest):
            w, outs, (y,) = rest[:n_w], rest[n_w:-1], rest[-1:]
            for rep in range(reps):
                for k in range(GROUP):
                    y[:, at(blk(s, rep, k), db)] = mm(br[0], w[rep][k])
            parted(s, y, outs)

        out_sums = launch(
            OUT_ROWS, out_body, GROUP,
            [(branch, row_block(fo))] + [(a, whole(a.shape)) for a in w_out],
            part_outs,
            [pltpu.VMEM((rows, width), F32)],
        )
        o_got = among(O_GOT, out_sums)

        def add_rows(name, parts, sizes):
            arrays = []
            for terms in parts:
                for a, _ in terms:
                    if not any(a is b for b in arrays):
                        arrays.append(a)
            where = [[([a is b for b in arrays].index(True), r) for a, r in terms] for terms in parts]

            def body(s, *refs):
                ins, outs = refs[: len(arrays)], refs[len(arrays) :]
                row = 0
                for n, out in zip(sizes, outs):
                    for r in range(n):
                        total = None
                        for a, at_row in where[row]:
                            v = ins[a][at_row : at_row + 1, :]
                            total = v if total is None else total + v
                        out[r : r + 1, : total.shape[1]] = total
                        row += 1

            return launch(
                name, body, 1, [(a, whole(a.shape)) for a in arrays],
                [((n, width), F32, whole((n, width))) for n in sizes],
            )

        def product(a, b):
            flat = lambda v: v.reshape(all_rows, v.shape[-1])
            return mm(flat(a[...]), flat(b[...]), 0, 0)

        def half_block(shape, h):
            return lead((1,) + shape, lambda i, s: jnp.clip(i - 2 * h, 0, 1))

        def others_halves(names, left_arr, left_spec, right_arr, right_spec, shape):
            got = []
            for rep in range(1, reps):
                def body(s, a, b, *outs):
                    made = product(a, b).astype(BF16)
                    for h in (0, 1):
                        @pl.when(pl.program_id(0) // 2 == h)
                        def _(h=h):
                            outs[h][0] = made

                sent = launch(
                    names[1], body, GROUP,
                    [(left_arr, left_spec(rep)), (right_arr, right_spec(rep))],
                    [((2,) + shape, BF16, half_block(shape, h)) for h in (0, 1)],
                )
                got += [to_rep(gate(names[2], a), rep) for a in sent]
            return got

        def others_part(names, left_arr, left_spec, right_arr, right_spec, shape):
            got = []
            for rep in range(1, reps):
                def body(s, a, b, out):
                    out[0] = product(a, b).astype(BF16)

                sent = launch(
                    names[1], body, GROUP,
                    [(left_arr, left_spec(rep)), (right_arr, right_spec(rep))],
                    [((GROUP,) + shape, BF16, lead((1,) + shape))],
                )[0]
                got.append(to_rep(gate(names[2], sent), rep))
            return got

        def own_part(names, left_arr, left_spec, right_arr, right_spec, shape, got, parts=1):
            def body(s, a, b, *refs):
                total = product(a, b)
                for n, ref in enumerate(refs[:-1]):
                    if parts == 1:
                        total = total + ref[0].astype(F32)
                    elif n % 2 == 0:
                        v = jnp.where(pl.program_id(0) < 2, ref[0], refs[n + 1][0])
                        total = total + v.astype(F32)
                refs[-1][0] = total.astype(BF16)

            return launch(
                names[0], body, GROUP,
                [(left_arr, left_spec(0)), (right_arr, right_spec(0))]
                + [(a, lead((1,) + shape) if parts == 1 else half_block(shape, n % 2)) for n, a in enumerate(got)],
                [((GROUP,) + shape, BF16, lead((1,) + shape))],
            )[0]

        def columns(rep):
            return pl.BlockSpec((GROUP, rows, db), lambda i, s: (0, 0, blk(s, rep, i)))

        out_args = (
            (OUT_WEIGHT_GRAD, OUT_WEIGHT_GRAD_OTHER, OUT_WEIGHT_GRAD_REP), branch, lambda rep: whole(branch.shape), grads, columns, (fo, db)
        )
        out_parts = own_part(*out_args, others_part(*out_args))
        out_pieces = among_members(out_parts)
        reg(OUT_PIECES, out_pieces)

        def backward_body(s, g, pre, qkv, probs, cs, lf, rt, *rest):
            w, (wide_out, sum_out, w_all) = rest[:n_w], rest[n_w:]

            @pl.when(pl.program_id(0) == 0)
            def _():
                for rep in range(reps):
                    for k in range(GROUP):
                        w_all[:, at(blk(s, rep, k), db)] = w[rep][k]

            ga = mm(g[0], w_all[:fz], 1, 1)
            u = pre[0]
            t = gelu_parts(u)[1]
            slope = 0.5 * (1.0 + t) + 0.5 * u * (1.0 - t * t) * (
                GELU_A * (1.0 + 3.0 * GELU_B * u * u)
            )
            gp = (ga * slope).astype(BF16)
            wide_out[0, :, :fz] = gp
            sum_out[0, :, :fz] = jnp.sum(gp.astype(F32), axis=0, keepdims=True)
            gc = mm(g[0], w_all[fz:], 1, 1).astype(BF16)
            q, k, v = qkv[0, :, :ez], qkv[0, :, ez : 2 * ez], qkv[0, :, 2 * ez :]
            dq, dk, dv = [], [], []
            for h in range(heads):
                lo, hi = h * HEAD_DIM, (h + 1) * HEAD_DIM
                p, gch = probs[0, h], gc[:, lo:hi]
                dv.append(mm(p.astype(BF16), gch, 0, 0))
                dp = mm(gch, v[:, lo:hi], 1, 1)
                ds = (p * (dp - jnp.sum(p * dp, axis=1, keepdims=True))).astype(BF16)
                dq.append(mm(ds, k[:, lo:hi]) * SCORE_SCALE)
                dk.append(mm(ds, q[:, lo:hi], 0, 0) * SCORE_SCALE)
            c, l, r = cs[0], lf[0], rt[0]
            join_heads = lambda parts: parts[0] if heads == 1 else jnp.concatenate(parts, axis=1)
            dq, dk, dv = join_heads(dq), join_heads(dk), join_heads(dv)
            dq = dq * c - rotated(dq, l, r)
            dk = dk * c - rotated(dk, l, r)
            for j, d in enumerate((dq, dk, dv)):
                low = d.astype(BF16)
                lo = fz + j * ez
                wide_out[0, :, lo : lo + ez] = low
                sum_out[0, :, lo : lo + ez] = jnp.sum(low.astype(F32), axis=0, keepdims=True)

        wide, wide_sums = launch(
            BACKWARD, backward_body, GROUP,
            [
                (grads, row_block(width)), (pre, row_block(fz)), (qkv, row_block(3 * ez)),
                (probs, lead((1, heads, rows, rows))), (cosine, row_block(ez)),
                (left, row_block(ez)), (right, row_block(ez)),
            ]
            + [(a, whole(a.shape)) for a in w_out],
            [((GROUP, rows, fw), BF16, row_block(fw)), ((GROUP, 1, fw), F32, lead((1, 1, fw)))],
            [pltpu.VMEM((fo, width), BF16)],
        )

        in_args = (
            (IN_WEIGHT_GRAD, IN_WEIGHT_GRAD_OTHER, IN_WEIGHT_GRAD_REP), normed, columns, wide, lambda rep: whole(wide.shape), (db, fw)
        )
        in_got = others_halves(*in_args)

        def normed_grad_body(s, gw, x, st, *rest):
            w, outs, (sums, y) = rest[:n_w], rest[n_w:-2], rest[-2:]
            for rep in range(reps):
                for k in range(GROUP):
                    y[:, at(blk(s, rep, k), db)] = mm(gw[0], w[rep][k], 1, 1)
            parted(s, y, outs)
            v = y[...]
            hat = (x[0].astype(F32) - st[0, :, 0:1]) * st[0, :, 1:2]

            @pl.when(pl.program_id(0) == 0)
            def _():
                sums[...] = jnp.zeros(sums.shape, F32)

            sums[0:1] += jnp.sum(v * hat, axis=0, keepdims=True)
            sums[1:2] += jnp.sum(v, axis=0, keepdims=True)

        *gn_parts, gain_sums = launch(
            NORMED_GRAD, normed_grad_body, GROUP,
            [(wide, row_block(fw)), (x_all, row_block(width)), (stats, row_block(128))]
            + [(a, whole(a.shape)) for a in w_in],
            part_outs + [((2, width), F32, whole((2, width)))],
            [pltpu.VMEM((rows, width), F32)],
        )

        own_block = lambda i, s: s[1] ^ i

        two = (2, part, width)

        def add_tensor(name, near_name, got):
            def body(s, *refs):
                ins, outs = refs[:n_t], refs[n_t:]
                total = ins[0][0].astype(F32)
                for ref in ins[1:]:
                    total = total + ref[0].astype(F32)
                for k in range(GROUP):
                    @pl.when(pl.program_id(0) == k)
                    def _(k=k):
                        outs[k % 2][k // 2] = total.astype(outs[k % 2].dtype)

            keep, send = launch(
                name, body, GROUP,
                [(a, lead((1, part, width), own_block)) for a in got],
                [(two, F32, whole(two)), (two, BF16, whole(two))],
            )
            near = to_member(gate(near_name, send), 1)
            reg(near_name, near)
            return keep, near

        def add_near(name, far_name, keep, near):
            def body(s, keep, near, own, send):
                own[...] = keep[0] + near[0].astype(F32)
                send[...] = (keep[1] + near[1].astype(F32)).astype(BF16)

            own, send = launch(
                name, body, 1, [(keep, whole(two)), (near, whole(two))],
                [((part, width), F32, whole((part, width))), ((part, width), BF16, whole((part, width)))],
            )
            far = to_member(gate(far_name, send), 2)
            reg(far_name, far)
            return own, far

        mine_rows = lead((part, width), lambda i, s: s[2])

        def join_rows(name, mine, got):
            def body(s, first, *rest):
                for m, ref in enumerate((first,) + rest[:-1]):
                    rest[-1][at(s[2] ^ m, part), :] = ref[...]

            return launch(
                name, body, 1,
                [(mine, whole(mine.shape))] + [(a, whole(a.shape)) for a in got],
                [((rows, width), BF16, whole((rows, width)))],
            )[0]

        gn_got = among(GN_GOT, gn_parts)
        out_keep, out_near = add_tensor(OUT_ADD, OUT_ADD_NEAR, o_got)
        in_parts = own_part(*in_args, in_got, 2)
        in_pieces = among_members(in_parts)
        o_sums = add_near(OUT_ADD_PAIR, OUT_ADD_PAIR_FAR, out_keep, out_near)
        flat = [row_sums.reshape(GROUP, width), wide_sums.reshape(GROUP, fw)]
        order = ((0, 1), (2, 3))
        low = add_rows(SUMS_LOW, [[(flat[n], a), (flat[n], b)] for n in (0, 1) for a, b in order], (4,))[0]
        small = add_rows(
            SUMS, [[(gain_sums, 0)], [(gain_sums, 1)], [(low, 0), (low, 1)], [(low, 2), (low, 3)]], (4,)
        )[0]
        hop = 1
        while hop < reps:
            got = to_rep(gate(SMALL_REP, small), hop)
            small = add_rows(SUMS_REP, [[(small, r), (got, r)] for r in range(4)], (4,))[0]
            hop *= 2
        gains, bias_total, wide_sum = add_rows(SUMS_SPLIT, [[(small, r)] for r in range(4)], (2, 1, 1))
        bias_total = bias_total[0]
        gn_keep, gn_near = add_tensor(GN_ADD, GN_ADD_NEAR, gn_got)

        both_bias = (out_bias + down_bias).reshape(1, width)

        def hidden_out_body(s, *refs):
            sums, (x, ok, bias, out) = refs[:2], refs[2:]
            total = sums[0][...] + sums[1][...].astype(F32)
            out[...] = (x[...].astype(F32) + ok[...] * (total + bias[...])).astype(BF16)

        hidden_out_mine = launch(
            HIDDEN_OUT, hidden_out_body, 1,
            [(a, whole(a.shape)) for a in o_sums]
            + [(hidden_in, mine_rows), (valid_mine[:, None], whole((part, 1))), (both_bias, whole(both_bias.shape))],
            [((part, width), BF16, whole((part, width)))],
        )[0]
        hidden_out_got = among(HIDDEN_OUT_GOT, [hidden_out_mine] * n_t)[1:]

        for hop in range(1, n_t):
            if hop & (hop - 1) == 0:
                got = to_tensor(gate(SMALL_TENSOR, gains), hop)
                gains = add_rows(GAINS_TENSOR, [[(gains, r), (got, r)] for r in range(2)], (2,))[0]
        gn_sums = add_near(GN_ADD_PAIR, GN_ADD_PAIR_FAR, gn_keep, gn_near)
        sent = add_rows(GAINS_SENT, [[(gains, 0)], [(gains, 1)], [(wide_sum, 0)]], (3,))[0]
        hidden_out = join_rows(HIDDEN_OUT_ROWS, hidden_out_mine, hidden_out_got)
        def finish_out(s, piece, down, wo):
            down[...] = piece[0, :fz].astype(F32)
            wo[...] = piece[0, fz:].astype(F32)

        down_master_grad, out_master_grad = launch(
            FINISH_OUT, finish_out, GROUP,
            [(out_pieces, out_block[2])],
            [(down_master.shape, F32, out_block[0]), (out_master.shape, F32, out_block[1])],
        )
        def input_grad_body(s, *refs):
            sums, (x, g, gn, out) = refs[:2], refs[2:]
            total = sums[0][...] + sums[1][...].astype(F32)
            v = x[...].astype(F32)
            v = v - jnp.mean(v, axis=1, keepdims=True)
            scale = lax.rsqrt(jnp.mean(v * v, axis=1, keepdims=True) + 1e-05)
            hat = v * scale
            gy = total * gn[...]
            d = gy - jnp.mean(gy, axis=1, keepdims=True) - hat * jnp.mean(gy * hat, axis=1, keepdims=True)
            out[...] = (g[...].astype(F32) + d * scale).astype(BF16)

        input_grad_mine = launch(
            INPUT_GRAD, input_grad_body, 1,
            [(a, whole(a.shape)) for a in gn_sums]
            + [(hidden_in, mine_rows), (out_grad, mine_rows), (gain, whole(gain.shape))],
            [((part, width), BF16, whole((part, width)))],
        )[0]
        input_grad_got = among(INPUT_GRAD_GOT, [input_grad_mine] * n_t)[1:]

        got = to_member(gate(SMALL_FAR, sent), 2)
        sent = add_rows(
            GAINS_FAR, [[(sent, 0), (got, 0)], [(sent, 1), (got, 1)], [(sent, 2)], [(got, 2)]], (4,)
        )[0]
        got = to_member(sent, 1)
        def finish_in(s, piece, up, qkv):
            for z in range(GROUP):
                up[:, z * fz : (z + 1) * fz] = piece[z, :, :fz].astype(F32)
                for j in range(3):
                    lo = fz + j * ez
                    qkv[j, :, z * ez : (z + 1) * ez] = piece[z, :, lo : lo + ez].astype(F32)

        up_master_grad, qkv_master_grad = launch(
            FINISH_IN, finish_in, steps_in,
            [(in_pieces, in_block[2])],
            [(up_master.shape, F32, in_block[0]), (qkv_master.shape, F32, in_block[1])],
        )


        def bias_body(s, mine, got, gains, up, qkv, scr):
            gains[...] = mine[0:2, :] + got[0:2, :]
            for k, ref, row in ((0, mine, 2), (2, mine, 3), (1, got, 2), (3, got, 3)):
                scr[pl.ds(s[1] ^ k, 1), :] = ref[row : row + 1, :]
            for z in range(GROUP):
                up[z : z + 1, :] = scr[z : z + 1, :fz]
                for j in range(3):
                    lo = fz + j * ez
                    qkv[j : j + 1, z * ez : (z + 1) * ez] = scr[z : z + 1, lo : lo + ez]

        gains, up_bias_grad, qkv_bias_grad = launch(
            BIAS_GRADS, bias_body, 1, [(sent, whole(sent.shape)), (got, whole(got.shape))],
            [
                ((2, width), F32, whole((2, width))), ((GROUP, fz), F32, whole((GROUP, fz))),
                (qkv_bias.shape, F32, whole(qkv_bias.shape)),
            ],
            [pltpu.VMEM((GROUP, width), F32)],
        )
        up_bias_grad = up_bias_grad.reshape(up_bias.shape)
        input_grad = join_rows(INPUT_GRAD_ROWS, input_grad_mine, input_grad_got)
        return (
            hidden_out, input_grad, gains[0], gains[1], qkv_master_grad, qkv_bias_grad,
            out_master_grad, bias_total, up_master_grad, up_bias_grad, down_master_grad, bias_total,
        )

    return per_device


def solution(mesh):
    placed = (
        P("dp", None), P("dp", None), P(), P(), P(None, "dp", "tensor"), P(None, "tensor"),
        P("tensor", "dp"), P(), P("dp", "tensor"), P("tensor"), P("tensor", "dp"), P(), P("dp", None),
    )
    return jax.shard_map(
        make(mesh.shape["dp"], mesh.shape["tensor"]),
        mesh=mesh,
        in_specs=placed,
        out_specs=(
            P("dp", None), P("dp", None), P(), P(), P(None, "dp", "tensor"), P(None, "tensor"),
            P("tensor", "dp"), P(), P("dp", "tensor"), P("tensor"), P("tensor", "dp"), P(),
        ),
        check_vma=False,
    )
```

```python
import functools
import math

import jax
import jax.numpy as jnp
from jax import lax
from jax.experimental import pallas as pl
from jax.experimental.pallas import tpu as pltpu
from jax.sharding import PartitionSpec as P

HEAD_DIM = 64
ROT_DIM = 32
GROUP = 4
CORES = 2
BF16 = jnp.bfloat16
F32 = jnp.float32
GELU_A = math.sqrt(2.0 / math.pi)
GELU_B = 0.044715
SCORE_SCALE = 1.0 / math.sqrt(HEAD_DIM)
VMEM_LIMIT = 44 * 2**20
UNIT = 2**19
(
    CAST_IN, X_FAR, L_FAR, X_FIRST, L_NEAR, G_FAR, CAST_OUT, G_FIRST, IN_STACK, X_NEAR, TABLES,
    X_REST, NORM, G_NEAR, OUT_STACK, W_IN, GRAD_ROWS, FORWARD, W_OUT, OUT_ROWS, O_GOT,
    OUT_WEIGHT_GRAD, OUT_WEIGHT_GRAD_OTHER, OUT_WEIGHT_GRAD_REP, OUT_PIECES, BACKWARD,
    IN_WEIGHT_GRAD, IN_WEIGHT_GRAD_OTHER, IN_WEIGHT_GRAD_REP, NORMED_GRAD, GN_GOT, OUT_ADD,
    OUT_ADD_NEAR, OUT_ADD_PAIR, OUT_ADD_PAIR_FAR, SUMS_LOW, SUMS, SMALL_REP, SUMS_REP,
    SUMS_SPLIT, GN_ADD, GN_ADD_NEAR, HIDDEN_OUT, HIDDEN_OUT_GOT, SMALL_TENSOR, GAINS_TENSOR,
    GN_ADD_PAIR, GN_ADD_PAIR_FAR, GAINS_SENT, HIDDEN_OUT_ROWS, FINISH_OUT, INPUT_GRAD,
    INPUT_GRAD_GOT, SMALL_FAR, GAINS_FAR, FINISH_IN, BIAS_GRADS, INPUT_GRAD_ROWS,
) = range(58)
COSTS = {
    CAST_IN: 14080,
    CAST_OUT: 1518,
    TABLES: 1716,
    NORM: 28600,
    FORWARD: 1,
    GRAD_ROWS: 1936,
    OUT_ROWS: 5082,
    OUT_WEIGHT_GRAD: 3498,
    BACKWARD: 1,
    NORMED_GRAD: 5192,
    IN_WEIGHT_GRAD: 1364,
    OUT_ADD: 4510,
    GN_ADD: 7920,
    HIDDEN_OUT: 594,
    INPUT_GRAD: 121,
    HIDDEN_OUT_ROWS: 704,
    INPUT_GRAD_ROWS: 352,
    FINISH_OUT: 1650,
    FINISH_IN: 1716,
    BIAS_GRADS: 10560,
    GN_ADD_PAIR: 132,
    OUT_ADD_PAIR: 528,
    SUMS_SPLIT: 220,
    SUMS: 2200,
    SUMS_REP: 8800,
}
GATES = {
    IN_STACK: (X_FIRST, L_NEAR, G_FAR,),
    G_FIRST: (X_FIRST,),
    X_REST: (TABLES,),
    OUT_STACK: (G_FIRST, IN_STACK, X_NEAR,),
    W_IN: (G_FIRST, NORM,),
    G_NEAR: (IN_STACK, X_REST,),
    FORWARD: (OUT_STACK,),
    BACKWARD: (OUT_ROWS, OUT_WEIGHT_GRAD,),
    IN_WEIGHT_GRAD_OTHER: (BACKWARD,),
    IN_WEIGHT_GRAD: (NORMED_GRAD,),
    OUT_ADD: (NORMED_GRAD, OUT_PIECES,),
    NORMED_GRAD: (IN_WEIGHT_GRAD_OTHER, OUT_PIECES,),
    OUT_WEIGHT_GRAD: (OUT_ROWS,),
    SUMS_LOW: (GN_ADD,),
    GAINS_FAR: (GN_ADD_PAIR, INPUT_GRAD,),
    GRAD_ROWS: (OUT_STACK,),
    SMALL_REP: (IN_WEIGHT_GRAD,),
    GN_ADD_PAIR: (GAINS_TENSOR,),
    INPUT_GRAD_ROWS: (BIAS_GRADS, FINISH_IN,),
    INPUT_GRAD: (FINISH_OUT,),
    HIDDEN_OUT_GOT: (GN_ADD,),
    CAST_OUT: (X_FAR,),
    HIDDEN_OUT_ROWS: (GN_ADD_PAIR,),
    TABLES: (CAST_OUT,),
    OUT_ROWS: (G_NEAR,),
    NORM: (G_FIRST,),
    FINISH_IN: (GN_ADD_PAIR,),
    SMALL_TENSOR: (GN_GOT,),
}


def mm(a, b, ca=1, cb=0):
    return lax.dot_general(a, b, (((ca,), (cb,)), ((), ())), preferred_element_type=F32)


def whole(shape):
    zeros = (0,) * len(shape)
    return pl.BlockSpec(tuple(shape), lambda i, sc: zeros)


def lead(shape, index=lambda i, sc: i):
    tail = (0,) * (len(shape) - 1)
    return pl.BlockSpec(tuple(shape), lambda i, sc: (index(i, sc),) + tail)


def run(name, body, steps, scalars, ins, outs, scratch=()):
    size = lambda shape, dtype: math.prod(shape) * jnp.dtype(dtype).itemsize
    moved = sum(size(a.shape, a.dtype) for a, _ in ins) + sum(size(s, d) for s, d, _ in outs)
    return pl.pallas_call(
        body,
        out_shape=[jax.ShapeDtypeStruct(s, d) for s, d, _ in outs],
        grid_spec=pltpu.PrefetchScalarGridSpec(
            num_scalar_prefetch=1,
            grid=(steps,),
            in_specs=[spec for _, spec in ins],
            out_specs=[spec for _, _, spec in outs],
            scratch_shapes=list(scratch),
        ),
        compiler_params=pltpu.CompilerParams(vmem_limit_bytes=VMEM_LIMIT),
        cost_estimate=pl.CostEstimate(
            flops=COSTS.get(name, 500) * UNIT, bytes_accessed=moved, transcendentals=0
        ),
    )(scalars, *[a for a, _ in ins])


def after(value, *done):
    return lax.optimization_barrier((value,) + done)[0]


def rotated(x, left, right):
    h = ROT_DIM // 2
    to_left = jnp.concatenate([x[:, h:], x[:, :h]], axis=1)
    to_right = jnp.concatenate([x[:, -h:], x[:, :-h]], axis=1)
    return to_left * left + to_right * right


def gelu_parts(u):
    t = jnp.tanh(GELU_A * (u + GELU_B * u * u * u))
    return 0.5 * u * (1.0 + t), t


def layout(lengths, rows):
    slots = lengths.shape[0]
    upper = lax.iota(jnp.int32, slots)[:, None] <= lax.iota(jnp.int32, slots)[None, :]
    ends = jnp.sum(jnp.where(upper, lengths[:, None], 0), axis=0)
    ids = lax.iota(jnp.int32, rows)
    passed = ids[:, None] >= ends[None, :]
    begins = jnp.max(jnp.where(passed, ends[None, :], 0), axis=1)
    return begins, ids - begins, (ids < jnp.max(ends)).astype(F32)


def make(n_dp, n_t):
    reps = n_dp // GROUP
    block = GROUP * CORES

    def join(rep, member):
        return (rep // CORES * GROUP + member) * CORES + rep % CORES

    def parts_of(index):
        return index // block * CORES + index % CORES, (index // CORES) % GROUP

    def to_member(value, k):
        pairs = [(i, join(parts_of(i)[0], parts_of(i)[1] ^ k)) for i in range(n_dp)]
        return lax.ppermute(value, "dp", pairs)

    members = [[join(rep, z) for z in range(GROUP)] for rep in range(reps)]

    def among_members(value):
        return lax.all_to_all(value, "dp", 0, 0, axis_index_groups=members, tiled=True)

    def to_rep(value, s):
        pairs = [(i, join(parts_of(i)[0] ^ s, parts_of(i)[1])) for i in range(n_dp)]
        return lax.ppermute(value, "dp", pairs)

    def to_tensor(value, m):
        return lax.ppermute(value, "tensor", [(i, i ^ m) for i in range(n_t)])

    def per_device(
        hidden_in, seq_lengths, norm_gain, norm_bias, qkv_master, qkv_bias, out_master, out_bias,
        up_master, up_bias, down_master, down_bias, out_grad,
    ):
        rows, width = hidden_in.shape
        db = up_master.shape[0]
        fz = up_master.shape[1] // GROUP
        ez = qkv_master.shape[2] // GROUP
        heads = ez // HEAD_DIM
        fw = fz + 3 * ez
        fo = fz + ez
        part = rows // n_t
        me_dp, me_t = lax.axis_index("dp"), lax.axis_index("tensor")
        me_r, me_z = parts_of(me_dp)
        sc = jnp.stack([me_r, me_z, me_t]).astype(jnp.int32)
        all_rows = GROUP * rows
        gain, shift = norm_gain.reshape(1, width), norm_bias.reshape(1, width)

        def blk(sref, s, z):
            return join(sref[0] ^ s, z)

        done = {}

        def gate(name, value):
            waits = [a for n in GATES.get(name, ()) if n in done for a in done[n]]
            return after(value, *waits) if waits else value

        def reg(name, *arrays):
            done[name] = arrays

        def launch(name, body, steps, ins, outs, scratch=()):
            (first, spec), *rest = ins
            made = run(name, body, steps, sc, [(gate(name, first), spec)] + rest, outs, scratch)
            reg(name, made[0])
            return made

        def at(index, size):
            return pl.ds(pl.multiple_of(index * size, size), size)

        def swapped(i):
            return (i % 2) * 2 + i // 2

        def first_hop(mine):
            return to_member(mine, 2)

        def second_hop(mine, far):
            near = to_member(jnp.stack([mine, far]), 1)
            return jnp.concatenate([far[None], near], axis=0)

        paired = n_t == 4
        half = part // 2

        def exchange(b):
            return [to_tensor(b, m) for m in ((1, 2) if paired else range(1, n_t))]

        def forwarded(got):
            return [got[0][:, :half], got[1][:, half:]] if paired else []

        def pieces(got, rest, start=0):
            if not paired:
                return [(m, 0, part, start, a) for m, a in enumerate(got, 1)]
            (one, one_at), (two, two_at) = got
            (far, far_at), (near, near_at) = rest
            return [
                (1, 0, part, one_at, one),
                (2, 0, part, two_at, two),
                (3, 0, half, far_at, far),
                (3, half, half, near_at, near),
            ]

        def place(sref, step, own, first, others, metas, out):
            @pl.when(step == 0)
            def _():
                out[0] = own[...]

            @pl.when(step > 0)
            def _():
                out[0, at(sref[2], part), :] = first[0]
                for (m, off, n, lo, _), ref in zip(metas, others):
                    start = pl.multiple_of((sref[2] ^ m) * part + off, n)
                    out[0, pl.ds(start, n), :] = ref[0, lo : lo + n]

        def piece_specs(first, metas):
            prev = lambda i, s: jnp.maximum(i - 1, 0)
            return [(first, lead((1,) + first.shape[1:], prev))] + [
                (a, lead((1,) + a.shape[1:], prev)) for *_, a in metas
            ]

        member_block = lambda i, s: s[1] ^ swapped(i)

        def cast_in(s, up, qkv, out):
            for z in range(GROUP):
                out[z, :, :fz] = up[:, z * fz : (z + 1) * fz].astype(BF16)
                for j in range(3):
                    lo = fz + j * ez
                    out[z, :, lo : lo + ez] = qkv[j, :, z * ez : (z + 1) * ez].astype(BF16)

        def cast_out(s, down, wo, out):
            out[0, :fz] = down[...].astype(BF16)
            out[0, fz:] = wo[...].astype(BF16)

        def to_reps(stack):
            return [stack] + [to_rep(stack, s) for s in range(1, reps)]

        steps_in = 2
        in_block = [
            lead((db // steps_in, GROUP * fz)),
            pl.BlockSpec((3, db // steps_in, GROUP * ez), lambda i, s: (0, i, 0)),
            pl.BlockSpec((GROUP, db // steps_in, fw), lambda i, s: (0, i, 0)),
        ]
        out_block = [lead((fz, db)), lead((ez, db)), lead((1, fo, db))]
        sent_in = launch(
            CAST_IN, cast_in, steps_in,
            [(up_master, in_block[0]), (qkv_master, in_block[1])],
            [((GROUP, db, fw), BF16, in_block[2])],
        )[0]
        _, _, own_valid = layout(seq_lengths[0], rows)
        x_mine = lax.dynamic_slice_in_dim(hidden_in, me_t * part, part, 0)
        valid_mine = lax.dynamic_slice_in_dim(own_valid, me_t * part, part, 0)
        x_far = first_hop(x_mine)
        l_far = to_member(seq_lengths, 2)
        g_own = (out_grad.astype(F32) * own_valid[:, None]).astype(BF16)
        g_mine = lax.dynamic_slice_in_dim(g_own, me_t * part, part, 0)
        reg(X_FAR, x_far)
        reg(L_FAR, l_far)
        x_first = second_hop(gate(X_FIRST, x_mine), x_far)
        l_near = to_member(jnp.concatenate([seq_lengths, l_far]), 1)
        reg(X_FIRST, x_first)
        reg(L_NEAR, l_near)
        g_far = first_hop(gate(G_FAR, g_mine))
        reg(G_FAR, g_far)
        sent_out = launch(
            CAST_OUT, cast_out, GROUP,
            [(down_master, out_block[0]), (out_master, out_block[1])],
            [((GROUP, fo, db), BF16, out_block[2])],
        )[0]

        g_first = second_hop(g_mine, gate(G_FIRST, g_far))
        reg(G_FIRST, g_first)
        in_stack = among_members(gate(IN_STACK, sent_in))
        reg(IN_STACK, in_stack)
        x_near = exchange(gate(X_NEAR, x_first))
        reg(X_NEAR, *x_near)

        def table_body(s, own, far, near, cs, lf, rt, bg):
            i = pl.program_id(0)
            row = lax.broadcasted_iota(jnp.int32, (rows, ez), 0)
            begin, end = jnp.zeros((rows, ez), jnp.int32), jnp.int32(0)
            for j in range(seq_lengths.shape[1]):
                length = jnp.where(i == 0, own[0, j], jnp.where(i == 1, far[0, j], near[0, j]))
                length = jnp.where(i == 3, near[1, j], length)
                end = end + length
                begin = jnp.where(row >= end, end, begin)
            lane = lax.broadcasted_iota(jnp.int32, (rows, ez), 1) % HEAD_DIM
            halves = ROT_DIM // 2
            step = (lane % halves).astype(F32) * (-2.0 / ROT_DIM)
            rate = jnp.exp(step * math.log(10000.0))
            angle = jnp.where(lane < ROT_DIM, (row - begin).astype(F32) * rate, 0.0)
            sine = jnp.sin(angle)
            cs[0] = jnp.cos(angle)
            lf[0] = jnp.where(lane < halves, -sine, 0.0)
            rt[0] = jnp.where(lane >= halves, sine, 0.0)
            bg[0] = begin[:, 0:1]

        smem = pl.BlockSpec(memory_space=pltpu.SMEM)
        cosine, left, right, begins = launch(
            TABLES, table_body, GROUP,
            [(seq_lengths, smem), (l_far, smem), (l_near, smem)],
            [((GROUP, rows, ez), F32, lead((1, rows, ez), member_block))] * 3
            + [((GROUP, rows, 1), jnp.int32, lead((1, rows, 1), member_block))],
        )

        x_rest = [to_tensor(gate(X_REST, b), m) for b, m in zip(forwarded(x_near), (2, 1))]
        reg(X_REST, *x_rest)
        if paired:
            x_metas = pieces([(a, 0) for a in x_near], [(a, 0) for a in x_rest])
        else:
            x_metas = pieces(x_near, None)

        def norm_body(s, own, first, *rest):
            others = rest[: len(x_metas)]
            gn, bs, x_out, n_out, st_out = rest[len(x_metas) :]
            place(s, pl.program_id(0), own, first, others, x_metas, x_out)
            v = x_out[0].astype(F32)
            mean = jnp.mean(v, axis=1, keepdims=True)
            v = v - mean
            scale = lax.rsqrt(jnp.mean(v * v, axis=1, keepdims=True) + 1e-05)
            v = v * scale * gn[...] + bs[...]
            n_out[0] = v.astype(BF16)
            which = lax.broadcasted_iota(jnp.int32, (rows, 128), 1)
            st_out[0] = jnp.where(which == 0, mean, scale)

        x_all, normed, stats = launch(
            NORM, norm_body, GROUP,
            [(hidden_in, whole(hidden_in.shape))]
            + piece_specs(x_first, x_metas)
            + [(gain, whole(gain.shape)), (shift, whole(shift.shape))],
            [
                ((GROUP, rows, width), BF16, lead((1, rows, width), member_block)),
                ((GROUP, rows, width), BF16, lead((1, rows, width), member_block)),
                ((GROUP, rows, 128), F32, lead((1, rows, 128), member_block)),
            ],
        )

        g_near = [to_tensor(gate(G_NEAR, g_first), m) for m in range(1, n_t)]
        reg(G_NEAR, *g_near)
        out_stack = among_members(gate(OUT_STACK, sent_out))
        reg(OUT_STACK, out_stack)
        w_in = to_reps(gate(W_IN, in_stack))
        g_metas = [(m, 0, part, 0, a) for m, a in enumerate(g_near, 1)]

        def grad_rows_body(s, own, first, *rest):
            others, (g_out, sum_out) = rest[: len(g_metas)], rest[len(g_metas) :]
            place(s, pl.program_id(0), own, first, others, g_metas, g_out)
            sum_out[0] = jnp.sum(g_out[0].astype(F32), axis=0, keepdims=True)

        grads, row_sums = launch(
            GRAD_ROWS, grad_rows_body, GROUP,
            [(g_own, whole(g_own.shape))] + piece_specs(g_first, g_metas),
            [
                ((GROUP, rows, width), BF16, lead((1, rows, width), member_block)),
                ((GROUP, 1, width), F32, lead((1, 1, width), member_block)),
            ],
        )

        my_bias = jnp.concatenate(
            [
                lax.dynamic_slice_in_dim(up_bias, me_z * fz, fz, 0),
                lax.dynamic_slice_in_dim(qkv_bias, me_z * ez, ez, 1).reshape(-1),
            ]
        ).reshape(1, fw)
        n_w = reps

        def forward_body(s, x, cs, lf, rt, bg, bias, *rest):
            w, (branch, pre, qkv, probs, wide) = rest[:n_w], rest[n_w:]

            @pl.when(pl.program_id(0) == 0)
            def _():
                for rep in range(reps):
                    for k in range(GROUP):
                        wide[at(blk(s, rep, k), db), :] = w[rep][k]

            u = mm(x[0], wide[:, :fz]) + bias[:, :fz]
            pre[0] = u
            act = gelu_parts(u)[0]
            branch[0, :, :fz] = act.astype(BF16)
            j = mm(x[0], wide[:, fz:]) + bias[:, fz:]
            c, l, r = cs[0], lf[0], rt[0]
            q, k, v = j[:, :ez], j[:, ez : 2 * ez], j[:, 2 * ez :]
            q = (q * c + rotated(q, l, r)).astype(BF16)
            k = (k * c + rotated(k, l, r)).astype(BF16)
            v = v.astype(BF16)
            qkv[0, :, :ez] = q
            qkv[0, :, ez : 2 * ez] = k
            qkv[0, :, 2 * ez :] = v
            col = lax.broadcasted_iota(jnp.int32, (rows, rows), 1)
            row = lax.broadcasted_iota(jnp.int32, (rows, rows), 0)
            allowed = (col >= bg[0]) & (col <= row)
            for h in range(heads):
                lo, hi = h * HEAD_DIM, (h + 1) * HEAD_DIM
                sco = mm(q[:, lo:hi], k[:, lo:hi], 1, 1) * SCORE_SCALE
                sco = jnp.where(allowed, sco, -1e30)
                e = jnp.exp(sco - jnp.max(sco, axis=1, keepdims=True))
                p = e / jnp.sum(e, axis=1, keepdims=True)
                probs[0, h] = p
                ctx = mm(p.astype(BF16), v[:, lo:hi])
                branch[0, :, fz + lo : fz + hi] = ctx.astype(BF16)

        row_block = lambda n: lead((1, rows, n))
        branch, pre, qkv, probs = launch(
            FORWARD, forward_body, GROUP,
            [
                (normed, row_block(width)), (cosine, row_block(ez)), (left, row_block(ez)),
                (right, row_block(ez)), (begins, row_block(1)), (my_bias, whole(my_bias.shape)),
            ]
            + [(a, whole(a.shape)) for a in w_in],
            [
                ((GROUP, rows, fo), BF16, row_block(fo)),
                ((GROUP, rows, fz), F32, row_block(fz)),
                ((GROUP, rows, 3 * ez), BF16, row_block(3 * ez)),
                ((GROUP, heads, rows, rows), F32, lead((1, heads, rows, rows))),
            ],
            [pltpu.VMEM((width, fw), BF16)],
        )

        w_out = to_reps(gate(W_OUT, out_stack))
        def among(name, parts):
            got = [to_tensor(gate(name, parts[m]), m) for m in range(1, n_t)]
            reg(name, *got)
            return [parts[0]] + got

        def parted(sref, y, outs):
            for m in range(n_t):
                outs[m][0] = y[at(sref[2] ^ m, part), :].astype(BF16)

        part_outs = [((GROUP, part, width), BF16, lead((1, part, width)))] * n_t

        def out_body(s, br, *rest):
            w, outs, (y,) = rest[:n_w], rest[n_w:-1], rest[-1:]
            for rep in range(reps):
                for k in range(GROUP):
                    y[:, at(blk(s, rep, k), db)] = mm(br[0], w[rep][k])
            parted(s, y, outs)

        out_sums = launch(
            OUT_ROWS, out_body, GROUP,
            [(branch, row_block(fo))] + [(a, whole(a.shape)) for a in w_out],
            part_outs,
            [pltpu.VMEM((rows, width), F32)],
        )
        o_got = among(O_GOT, out_sums)

        def add_rows(name, parts, sizes):
            arrays = []
            for terms in parts:
                for a, _ in terms:
                    if not any(a is b for b in arrays):
                        arrays.append(a)
            where = [[([a is b for b in arrays].index(True), r) for a, r in terms] for terms in parts]

            def body(s, *refs):
                ins, outs = refs[: len(arrays)], refs[len(arrays) :]
                row = 0
                for n, out in zip(sizes, outs):
                    for r in range(n):
                        total = None
                        for a, at_row in where[row]:
                            v = ins[a][at_row : at_row + 1, :]
                            total = v if total is None else total + v
                        out[r : r + 1, : total.shape[1]] = total
                        row += 1

            return launch(
                name, body, 1, [(a, whole(a.shape)) for a in arrays],
                [((n, width), F32, whole((n, width))) for n in sizes],
            )

        def product(a, b):
            flat = lambda v: v.reshape(all_rows, v.shape[-1])
            return mm(flat(a[...]), flat(b[...]), 0, 0)

        def half_block(shape, h):
            return lead((1,) + shape, lambda i, s: jnp.clip(i - 2 * h, 0, 1))

        def others_halves(names, left_arr, left_spec, right_arr, right_spec, shape):
            got = []
            for rep in range(1, reps):
                def body(s, a, b, *outs):
                    made = product(a, b).astype(BF16)
                    for h in (0, 1):
                        @pl.when(pl.program_id(0) // 2 == h)
                        def _(h=h):
                            outs[h][0] = made

                sent = launch(
                    names[1], body, GROUP,
                    [(left_arr, left_spec(rep)), (right_arr, right_spec(rep))],
                    [((2,) + shape, BF16, half_block(shape, h)) for h in (0, 1)],
                )
                got += [to_rep(gate(names[2], a), rep) for a in sent]
            return got

        def others_part(names, left_arr, left_spec, right_arr, right_spec, shape):
            got = []
            for rep in range(1, reps):
                def body(s, a, b, out):
                    out[0] = product(a, b).astype(BF16)

                sent = launch(
                    names[1], body, GROUP,
                    [(left_arr, left_spec(rep)), (right_arr, right_spec(rep))],
                    [((GROUP,) + shape, BF16, lead((1,) + shape))],
                )[0]
                got.append(to_rep(gate(names[2], sent), rep))
            return got

        def own_part(names, left_arr, left_spec, right_arr, right_spec, shape, got, parts=1):
            def body(s, a, b, *refs):
                total = product(a, b)
                for n, ref in enumerate(refs[:-1]):
                    if parts == 1:
                        total = total + ref[0].astype(F32)
                    elif n % 2 == 0:
                        v = jnp.where(pl.program_id(0) < 2, ref[0], refs[n + 1][0])
                        total = total + v.astype(F32)
                refs[-1][0] = total.astype(BF16)

            return launch(
                names[0], body, GROUP,
                [(left_arr, left_spec(0)), (right_arr, right_spec(0))]
                + [(a, lead((1,) + shape) if parts == 1 else half_block(shape, n % 2)) for n, a in enumerate(got)],
                [((GROUP,) + shape, BF16, lead((1,) + shape))],
            )[0]

        def columns(rep):
            return pl.BlockSpec((GROUP, rows, db), lambda i, s: (0, 0, blk(s, rep, i)))

        out_args = (
            (OUT_WEIGHT_GRAD, OUT_WEIGHT_GRAD_OTHER, OUT_WEIGHT_GRAD_REP), branch, lambda rep: whole(branch.shape), grads, columns, (fo, db)
        )
        out_parts = own_part(*out_args, others_part(*out_args))
        out_pieces = among_members(out_parts)
        reg(OUT_PIECES, out_pieces)

        def backward_body(s, g, pre, qkv, probs, cs, lf, rt, *rest):
            w, (wide_out, sum_out, w_all) = rest[:n_w], rest[n_w:]

            @pl.when(pl.program_id(0) == 0)
            def _():
                for rep in range(reps):
                    for k in range(GROUP):
                        w_all[:, at(blk(s, rep, k), db)] = w[rep][k]

            ga = mm(g[0], w_all[:fz], 1, 1)
            u = pre[0]
            t = gelu_parts(u)[1]
            slope = 0.5 * (1.0 + t) + 0.5 * u * (1.0 - t * t) * (
                GELU_A * (1.0 + 3.0 * GELU_B * u * u)
            )
            gp = (ga * slope).astype(BF16)
            wide_out[0, :, :fz] = gp
            sum_out[0, :, :fz] = jnp.sum(gp.astype(F32), axis=0, keepdims=True)
            gc = mm(g[0], w_all[fz:], 1, 1).astype(BF16)
            q, k, v = qkv[0, :, :ez], qkv[0, :, ez : 2 * ez], qkv[0, :, 2 * ez :]
            dq, dk, dv = [], [], []
            for h in range(heads):
                lo, hi = h * HEAD_DIM, (h + 1) * HEAD_DIM
                p, gch = probs[0, h], gc[:, lo:hi]
                dv.append(mm(p.astype(BF16), gch, 0, 0))
                dp = mm(gch, v[:, lo:hi], 1, 1)
                ds = (p * (dp - jnp.sum(p * dp, axis=1, keepdims=True))).astype(BF16)
                dq.append(mm(ds, k[:, lo:hi]) * SCORE_SCALE)
                dk.append(mm(ds, q[:, lo:hi], 0, 0) * SCORE_SCALE)
            c, l, r = cs[0], lf[0], rt[0]
            join_heads = lambda parts: parts[0] if heads == 1 else jnp.concatenate(parts, axis=1)
            dq, dk, dv = join_heads(dq), join_heads(dk), join_heads(dv)
            dq = dq * c - rotated(dq, l, r)
            dk = dk * c - rotated(dk, l, r)
            for j, d in enumerate((dq, dk, dv)):
                low = d.astype(BF16)
                lo = fz + j * ez
                wide_out[0, :, lo : lo + ez] = low
                sum_out[0, :, lo : lo + ez] = jnp.sum(low.astype(F32), axis=0, keepdims=True)

        wide, wide_sums = launch(
            BACKWARD, backward_body, GROUP,
            [
                (grads, row_block(width)), (pre, row_block(fz)), (qkv, row_block(3 * ez)),
                (probs, lead((1, heads, rows, rows))), (cosine, row_block(ez)),
                (left, row_block(ez)), (right, row_block(ez)),
            ]
            + [(a, whole(a.shape)) for a in w_out],
            [((GROUP, rows, fw), BF16, row_block(fw)), ((GROUP, 1, fw), F32, lead((1, 1, fw)))],
            [pltpu.VMEM((fo, width), BF16)],
        )

        in_args = (
            (IN_WEIGHT_GRAD, IN_WEIGHT_GRAD_OTHER, IN_WEIGHT_GRAD_REP), normed, columns, wide, lambda rep: whole(wide.shape), (db, fw)
        )
        in_got = others_halves(*in_args)

        def normed_grad_body(s, gw, x, st, *rest):
            w, outs, (sums, y) = rest[:n_w], rest[n_w:-2], rest[-2:]
            for rep in range(reps):
                for k in range(GROUP):
                    y[:, at(blk(s, rep, k), db)] = mm(gw[0], w[rep][k], 1, 1)
            parted(s, y, outs)
            v = y[...]
            hat = (x[0].astype(F32) - st[0, :, 0:1]) * st[0, :, 1:2]

            @pl.when(pl.program_id(0) == 0)
            def _():
                sums[...] = jnp.zeros(sums.shape, F32)

            sums[0:1] += jnp.sum(v * hat, axis=0, keepdims=True)
            sums[1:2] += jnp.sum(v, axis=0, keepdims=True)

        *gn_parts, gain_sums = launch(
            NORMED_GRAD, normed_grad_body, GROUP,
            [(wide, row_block(fw)), (x_all, row_block(width)), (stats, row_block(128))]
            + [(a, whole(a.shape)) for a in w_in],
            part_outs + [((2, width), F32, whole((2, width)))],
            [pltpu.VMEM((rows, width), F32)],
        )

        own_block = lambda i, s: s[1] ^ i

        two = (2, part, width)

        def add_tensor(name, near_name, got):
            def body(s, *refs):
                ins, outs = refs[:n_t], refs[n_t:]
                total = ins[0][0].astype(F32)
                for ref in ins[1:]:
                    total = total + ref[0].astype(F32)
                for k in range(GROUP):
                    @pl.when(pl.program_id(0) == k)
                    def _(k=k):
                        outs[k % 2][k // 2] = total.astype(outs[k % 2].dtype)

            keep, send = launch(
                name, body, GROUP,
                [(a, lead((1, part, width), own_block)) for a in got],
                [(two, F32, whole(two)), (two, BF16, whole(two))],
            )
            near = to_member(gate(near_name, send), 1)
            reg(near_name, near)
            return keep, near

        def add_near(name, far_name, keep, near):
            def body(s, keep, near, own, send):
                own[...] = keep[0] + near[0].astype(F32)
                send[...] = (keep[1] + near[1].astype(F32)).astype(BF16)

            own, send = launch(
                name, body, 1, [(keep, whole(two)), (near, whole(two))],
                [((part, width), F32, whole((part, width))), ((part, width), BF16, whole((part, width)))],
            )
            far = to_member(gate(far_name, send), 2)
            reg(far_name, far)
            return own, far

        mine_rows = lead((part, width), lambda i, s: s[2])

        def join_rows(name, mine, got):
            def body(s, first, *rest):
                for m, ref in enumerate((first,) + rest[:-1]):
                    rest[-1][at(s[2] ^ m, part), :] = ref[...]

            return launch(
                name, body, 1,
                [(mine, whole(mine.shape))] + [(a, whole(a.shape)) for a in got],
                [((rows, width), BF16, whole((rows, width)))],
            )[0]

        gn_got = among(GN_GOT, gn_parts)
        out_keep, out_near = add_tensor(OUT_ADD, OUT_ADD_NEAR, o_got)
        in_parts = own_part(*in_args, in_got, 2)
        in_pieces = among_members(in_parts)
        o_sums = add_near(OUT_ADD_PAIR, OUT_ADD_PAIR_FAR, out_keep, out_near)
        flat = [row_sums.reshape(GROUP, width), wide_sums.reshape(GROUP, fw)]
        order = ((0, 1), (2, 3))
        low = add_rows(SUMS_LOW, [[(flat[n], a), (flat[n], b)] for n in (0, 1) for a, b in order], (4,))[0]
        small = add_rows(
            SUMS, [[(gain_sums, 0)], [(gain_sums, 1)], [(low, 0), (low, 1)], [(low, 2), (low, 3)]], (4,)
        )[0]
        hop = 1
        while hop < reps:
            got = to_rep(gate(SMALL_REP, small), hop)
            small = add_rows(SUMS_REP, [[(small, r), (got, r)] for r in range(4)], (4,))[0]
            hop *= 2
        gains, bias_total, wide_sum = add_rows(SUMS_SPLIT, [[(small, r)] for r in range(4)], (2, 1, 1))
        bias_total = bias_total[0]
        gn_keep, gn_near = add_tensor(GN_ADD, GN_ADD_NEAR, gn_got)

        both_bias = (out_bias + down_bias).reshape(1, width)

        def hidden_out_body(s, *refs):
            sums, (x, ok, bias, out) = refs[:2], refs[2:]
            total = sums[0][...] + sums[1][...].astype(F32)
            out[...] = (x[...].astype(F32) + ok[...] * (total + bias[...])).astype(BF16)

        hidden_out_mine = launch(
            HIDDEN_OUT, hidden_out_body, 1,
            [(a, whole(a.shape)) for a in o_sums]
            + [(hidden_in, mine_rows), (valid_mine[:, None], whole((part, 1))), (both_bias, whole(both_bias.shape))],
            [((part, width), BF16, whole((part, width)))],
        )[0]
        hidden_out_got = among(HIDDEN_OUT_GOT, [hidden_out_mine] * n_t)[1:]

        for hop in range(1, n_t):
            if hop & (hop - 1) == 0:
                got = to_tensor(gate(SMALL_TENSOR, gains), hop)
                gains = add_rows(GAINS_TENSOR, [[(gains, r), (got, r)] for r in range(2)], (2,))[0]
        gn_sums = add_near(GN_ADD_PAIR, GN_ADD_PAIR_FAR, gn_keep, gn_near)
        sent = add_rows(GAINS_SENT, [[(gains, 0)], [(gains, 1)], [(wide_sum, 0)]], (3,))[0]
        hidden_out = join_rows(HIDDEN_OUT_ROWS, hidden_out_mine, hidden_out_got)
        def finish_out(s, piece, down, wo):
            down[...] = piece[0, :fz].astype(F32)
            wo[...] = piece[0, fz:].astype(F32)

        down_master_grad, out_master_grad = launch(
            FINISH_OUT, finish_out, GROUP,
            [(out_pieces, out_block[2])],
            [(down_master.shape, F32, out_block[0]), (out_master.shape, F32, out_block[1])],
        )
        def input_grad_body(s, *refs):
            sums, (x, g, gn, out) = refs[:2], refs[2:]
            total = sums[0][...] + sums[1][...].astype(F32)
            v = x[...].astype(F32)
            v = v - jnp.mean(v, axis=1, keepdims=True)
            scale = lax.rsqrt(jnp.mean(v * v, axis=1, keepdims=True) + 1e-05)
            hat = v * scale
            gy = total * gn[...]
            d = gy - jnp.mean(gy, axis=1, keepdims=True) - hat * jnp.mean(gy * hat, axis=1, keepdims=True)
            out[...] = (g[...].astype(F32) + d * scale).astype(BF16)

        input_grad_mine = launch(
            INPUT_GRAD, input_grad_body, 1,
            [(a, whole(a.shape)) for a in gn_sums]
            + [(hidden_in, mine_rows), (out_grad, mine_rows), (gain, whole(gain.shape))],
            [((part, width), BF16, whole((part, width)))],
        )[0]
        input_grad_got = among(INPUT_GRAD_GOT, [input_grad_mine] * n_t)[1:]

        got = to_member(gate(SMALL_FAR, sent), 2)
        sent = add_rows(
            GAINS_FAR, [[(sent, 0), (got, 0)], [(sent, 1), (got, 1)], [(sent, 2)], [(got, 2)]], (4,)
        )[0]
        got = to_member(sent, 1)
        def finish_in(s, piece, up, qkv):
            for z in range(GROUP):
                up[:, z * fz : (z + 1) * fz] = piece[z, :, :fz].astype(F32)
                for j in range(3):
                    lo = fz + j * ez
                    qkv[j, :, z * ez : (z + 1) * ez] = piece[z, :, lo : lo + ez].astype(F32)

        up_master_grad, qkv_master_grad = launch(
            FINISH_IN, finish_in, steps_in,
            [(in_pieces, in_block[2])],
            [(up_master.shape, F32, in_block[0]), (qkv_master.shape, F32, in_block[1])],
        )


        def bias_body(s, mine, got, gains, up, qkv, scr):
            gains[...] = mine[0:2, :] + got[0:2, :]
            for k, ref, row in ((0, mine, 2), (2, mine, 3), (1, got, 2), (3, got, 3)):
                scr[pl.ds(s[1] ^ k, 1), :] = ref[row : row + 1, :]
            for z in range(GROUP):
                up[z : z + 1, :] = scr[z : z + 1, :fz]
                for j in range(3):
                    lo = fz + j * ez
                    qkv[j : j + 1, z * ez : (z + 1) * ez] = scr[z : z + 1, lo : lo + ez]

        gains, up_bias_grad, qkv_bias_grad = launch(
            BIAS_GRADS, bias_body, 1, [(sent, whole(sent.shape)), (got, whole(got.shape))],
            [
                ((2, width), F32, whole((2, width))), ((GROUP, fz), F32, whole((GROUP, fz))),
                (qkv_bias.shape, F32, whole(qkv_bias.shape)),
            ],
            [pltpu.VMEM((GROUP, width), F32)],
        )
        up_bias_grad = up_bias_grad.reshape(up_bias.shape)
        input_grad = join_rows(INPUT_GRAD_ROWS, input_grad_mine, input_grad_got)
        return (
            hidden_out, input_grad, gains[0], gains[1], qkv_master_grad, qkv_bias_grad,
            out_master_grad, bias_total, up_master_grad, up_bias_grad, down_master_grad, bias_total,
        )

    return per_device


def solution(mesh):
    placed = (
        P("dp", None), P("dp", None), P(), P(), P(None, "dp", "tensor"), P(None, "tensor"),
        P("tensor", "dp"), P(), P("dp", "tensor"), P("tensor"), P("tensor", "dp"), P(), P("dp", None),
    )
    return jax.shard_map(
        make(mesh.shape["dp"], mesh.shape["tensor"]),
        mesh=mesh,
        in_specs=placed,
        out_specs=(
            P("dp", None), P("dp", None), P(), P(), P(None, "dp", "tensor"), P(None, "tensor"),
            P("tensor", "dp"), P(), P("dp", "tensor"), P("tensor"), P("tensor", "dp"), P(),
        ),
        check_vma=False,
    )
```
